32 devices in a mesh: ctx: 4 (over x, core), dp: 2 (over y), tp: 4 (over z).
Axes of the slice: x: 2, y: 2, z: 4, core: 2. Of those that a mesh axis runs over, the one named last changes fastest.
Arguments:
- token_ids: int32 [4, 4], replicated, may hold values from 0 to 50279
- decode_prompt: int32 [4], replicated, may hold values from 0 to 3, as said below
- embedding: bfloat16 [50280, 4096], P('dp', ('ctx', 'tp')), may hold values from -6 to 6
- norm_gain: float32 [4096], replicated, may hold values from 0.1 to 1.9
- w_zx: bfloat16 [2, 128, 64, 4096], P(None, ('tp', 'ctx')), may hold values from -0.09375 to 0.09375
- w_bcdt: bfloat16 [4096, 384], P(None, ('ctx', 'tp')), may hold values from -0.09375 to 0.09375
- conv_x_weight: float32 [4, 128, 64], P(None, ('tp', 'ctx')), may hold values from -3 to 3
- conv_x_bias: float32 [128, 64], P(('tp', 'ctx')), may hold values from -3 to 3
- conv_bc_weight: float32 [4, 256], replicated, may hold values from -3 to 3
- conv_bc_bias: float32 [256], replicated, may hold values from -3 to 3
- dt_bias: float32 [128], P(('tp', 'ctx')), may hold values from -4 to -1
- a_log: float32 [128], P(('tp', 'ctx')), may hold values from 0 to 2.7
- d_skip: float32 [128], P(('tp', 'ctx')), may hold values from 0.5 to 1.5
- gate_norm_gain: float32 [128, 64], P(('tp', 'ctx')), may hold values from 0.1 to 1.9
- w_out: bfloat16 [128, 64, 4096], P(('tp', 'ctx')), may hold values from -0.0625 to 0.0625
- state_parts: bfloat16 [4, 4, 128, 64, 128], P('ctx', 'dp', 'tp'), may hold values from -6 to 6
- seg_rate: float32 [4, 4, 128], P('ctx', 'dp', 'tp'), may hold values from 0 to 4
- x_tail: bfloat16 [4, 3, 128, 64], P('dp', None, ('tp', 'ctx')), may hold values from -6 to 6
- bc_tail: bfloat16 [4, 3, 256], P('dp'), may hold values from -6 to 6
Outputs:
- mixer_out: bfloat16 [4, 4, 4096], P(None, 'dp', ('ctx', 'tp'))
- final_state: float32 [4, 128, 64, 128], P('dp', ('tp', 'ctx'))
The draws below stay inside these ranges and needn't reach their ends.
Inputs may be any that keep to these rules, and one draw needn't show every extreme that they name: decode_prompt is a permutation of the prompts; slot s is decoded by dp group s // 2, and prompt q is held by dp group q // 2; the 2 prompts held by one dp group are decoded by 2 different dp groups.
All inputs are finite; a program needn't handle non-finite values.
Results may differ from the reference program's by a relative error of at most 0.02.
Values may be sent and summed in bfloat16 or wider, within the bound.
A program may use at most 64 MiB of HBM per device.

```python
import math
import jax
import jax.numpy as jnp
import numpy as np
from jax import lax

D = 4096
HEADS = 128
HEAD_DIM = 64
STATE = 128
VOCAB = 50280
CONV = 4
STEPS = 4
PR_DEV = 2
PROMPTS = 4
PREFILL_SEGMENTS = 4
N_DP = 2


def draw_decode_prompt(key, part):
    base = jax.random.fold_in(key, 11)
    key_label, key_offset, key_link, key_slot = jax.random.split(base, 4)
    label = jax.random.permutation(key_label, N_DP).astype(jnp.int32)
    owner = jnp.argsort(label).astype(jnp.int32)
    offsets = jax.random.permutation(key_offset, N_DP)[:PR_DEV].astype(jnp.int32)
    link_prompt = jax.vmap(lambda single: jax.random.permutation(single, PR_DEV))(jax.random.split(key_link, N_DP)).astype(jnp.int32)
    slot_order = jax.vmap(lambda single: jax.random.permutation(single, PR_DEV))(jax.random.split(key_slot, N_DP)).astype(jnp.int32)
    source = owner[(label[:, None] - offsets[None, :]) % N_DP]
    links = jnp.arange(PR_DEV, dtype=jnp.int32)[None, :]
    prompt = source * PR_DEV + link_prompt[source, links]
    slots = jnp.arange(N_DP, dtype=jnp.int32)[:, None] * PR_DEV + slot_order
    return jnp.zeros((N_DP * PR_DEV,), jnp.int32).at[slots.reshape(-1)].set(prompt.reshape(-1).astype(jnp.int32))


def draw_seg_rate(key, part):
    root_random_key = jax.random.fold_in(key, 23)
    plateau_random_key, quick_random_key, choose_random_key, jitter_random_key, spike_random_key, length_random_key = jax.random.split(root_random_key, 6)
    leading = (PROMPTS, HEADS)
    complete_shape = (PREFILL_SEGMENTS, PROMPTS, HEADS)
    slow_low, slow_high, fast_share, rough_low, rough_high = (0.1, 1.5, 0.25, 0.5, 1.5)
    slow_rate = jnp.exp(jax.random.uniform(plateau_random_key, leading, jnp.float32, math.log(slow_low), math.log(slow_high)))
    fast_rate = jnp.exp(jax.random.uniform(quick_random_key, leading, jnp.float32, math.log(2.0), math.log(5.0)))
    chosen = jax.random.uniform(choose_random_key, leading, jnp.float32) < fast_share
    plateau_rate = jnp.where(chosen, fast_rate, slow_rate) / PREFILL_SEGMENTS
    jitter_amount = jax.random.uniform(jitter_random_key, complete_shape, jnp.float32, rough_low, rough_high)
    spike_events = jax.random.uniform(spike_random_key, complete_shape, jnp.float32) < 1.0 / PREFILL_SEGMENTS
    spike_length = jax.random.uniform(length_random_key, complete_shape, jnp.float32, 0.22, 0.69)
    return (plateau_rate[None] * jitter_amount + jnp.where(spike_events, spike_length, 0.0)).astype(jnp.float32)


def touch_ends(drawn, stream_key, least, largest):
    index_at = [jax.random.randint(jax.random.fold_in(stream_key, axis), (), 0, length) for axis, length in enumerate(drawn.shape)]
    main_axis = drawn.shape.index(max(drawn.shape))
    beside = index_at[:main_axis] + [(index_at[main_axis] + 1) % drawn.shape[main_axis]] + index_at[main_axis + 1:]
    return drawn.at[tuple(index_at)].set(least).at[tuple(beside)].set(largest)


def spiked(result, key, source, target, parts, factor):
    owner, partner = [(jnp.arange(result.shape[axis_at]) // (result.shape[axis_at] // parts)).reshape([-1 if axis == axis_at else 1 for axis in range(result.ndim)]) for axis_at in (source, target)]
    chosen = jax.random.permutation(key, parts)[partner]
    strong = (owner == chosen) | (owner == (partner + parts // 2) % parts)
    return jnp.where(strong, factor * result, result)


def levels(key, extent, cuts, low, largest):
    level = 1.0
    for axis_at, parts in cuts:
        steps = jax.random.uniform(jax.random.fold_in(jax.random.fold_in(key, 6), axis_at), (parts,), jnp.float32, low / len(cuts), largest / len(cuts))
        level = level * jnp.repeat(jnp.exp(steps), extent[axis_at] // parts).reshape((-1,) + (1,) * (len(extent) - 1 - axis_at))
    return level


def rank_bounds(number_of, skew):
    weights = [(1 << 20) // math.isqrt(grade ** skew) + 1 for grade in range(1, number_of + 1)]
    width = 1 + sum(weights) // (1 << 30)
    return np.cumsum(np.array([max(1, weight // width) for weight in weights]))


def ranked_ids(stream_key, shape, amount, skew):
    listing = rank_bounds(amount, skew)
    pick = jax.random.randint(jax.random.fold_in(stream_key, 1), shape, 0, int(listing[amount - 1]))
    rank = jnp.searchsorted(jnp.asarray(listing, jnp.int32), pick, side="right")
    return jax.random.permutation(jax.random.fold_in(stream_key, 2), amount)[rank].astype(jnp.int32)


def gaussian(rng, shape, scale, most, pieces=(), kind=jnp.bfloat16):
    drawn = scale * jax.random.normal(rng, shape, jnp.float32)
    if pieces:
        drawn = drawn * levels(rng, shape, pieces, -0.22, 0.18)
    return jnp.clip(drawn, -most, most).astype(kind)


def gaussian_with(stream_key, dims, width, limit, shards, heavy, kind=jnp.bfloat16):
    entries = width * jax.random.normal(stream_key, dims, jnp.float32)
    if shards:
        entries = entries * levels(stream_key, dims, shards, -0.22, 0.18)
    return jnp.clip(spiked(entries, jax.random.fold_in(stream_key, 3), *heavy), -limit, limit).astype(kind)


def setup_inputs(seed: int = 0) -> dict:
    key_list = jax.random.split(jax.random.key(seed), 20)
    return {
        "token_ids": touch_ends(ranked_ids(key_list[0], (STEPS, PROMPTS), VOCAB, 2), jax.random.fold_in(key_list[0], 3), 0, VOCAB - 1).astype(jnp.int32),
        "decode_prompt": draw_decode_prompt(jax.random.fold_in(key_list[19], 71), 0),
        "embedding": gaussian(key_list[2], (VOCAB, D), 1.0, 6.0, ((0, 2), (1, 16))),
        "norm_gain": jnp.clip(1.0 + 0.18 * jax.random.normal(key_list[3], (D,), jnp.float32), 0.1, 1.9),
        "w_zx": gaussian(key_list[4], (2, HEADS, HEAD_DIM, D), D ** -0.5, 0.09375, ((1, 16),)),
        "w_bcdt": gaussian(key_list[5], (D, 2 * STATE + HEADS), D ** -0.5, 0.09375, ((1, 16),)),
        "conv_x_weight": gaussian(key_list[6], (CONV, HEADS, HEAD_DIM), CONV ** -0.5, 3.0, ((1, 16),), jnp.float32),
        "conv_x_bias": gaussian(key_list[7], (HEADS, HEAD_DIM), 0.5, 3.0, ((0, 16),), jnp.float32),
        "conv_bc_weight": gaussian(key_list[8], (CONV, 2 * STATE), CONV ** -0.5, 3.0, (), jnp.float32),
        "conv_bc_bias": gaussian(key_list[9], (2 * STATE,), 0.5, 3.0, (), jnp.float32),
        "dt_bias": jnp.clip(-4.0 + 3.0 * jax.random.uniform(key_list[10], (HEADS,), jnp.float32) ** levels(key_list[10], (HEADS,), ((0, 16),), -0.2, 0.2), -4.0, -1.0),
        "a_log": jnp.clip(2.7 * jax.random.uniform(key_list[11], (HEADS,), jnp.float32) ** levels(key_list[11], (HEADS,), ((0, 16),), -0.2, 0.2), 0.0, 2.7),
        "d_skip": jnp.clip(0.5 + 1.0 * jax.random.uniform(key_list[12], (HEADS,), jnp.float32) ** levels(key_list[12], (HEADS,), ((0, 16),), -0.2, 0.2), 0.5, 1.5),
        "gate_norm_gain": jnp.clip(1.0 + 0.18 * jax.random.normal(key_list[13], (HEADS, HEAD_DIM), jnp.float32), 0.1, 1.9),
        "w_out": gaussian(key_list[14], (HEADS, HEAD_DIM, D), (HEADS * HEAD_DIM) ** -0.5, 0.0625, ((0, 16),)),
        "state_parts": gaussian_with(key_list[15], (PREFILL_SEGMENTS, PROMPTS, HEADS, HEAD_DIM, STATE), 1.0, 6.0, ((0, 4), (1, 2), (2, 4)), (0, 2, 4, 2.0)),
        "seg_rate": draw_seg_rate(jax.random.fold_in(key_list[19], 71), 0),
        "x_tail": gaussian(key_list[17], (PROMPTS, CONV - 1, HEADS, HEAD_DIM), 1.0, 6.0, ((0, 2), (2, 16))),
        "bc_tail": gaussian(key_list[18], (PROMPTS, CONV - 1, 2 * STATE), 1.0, 6.0, ((0, 2),)),
    }


epsilon = 1e-05

def rms_scale(values, gain):
    return values * lax.rsqrt(lax.optimization_barrier(jnp.mean(values * values, axis=-1, keepdims=True)) + epsilon) * gain

def reference(token_ids, decode_prompt, embedding, norm_gain, w_zx, w_bcdt, conv_x_weight, conv_x_bias, conv_bc_weight, conv_bc_bias, dt_bias, a_log, d_skip, gate_norm_gain, w_out, state_parts, seg_rate, x_tail, bc_tail):
    suffix = jnp.cumsum(seg_rate[::-1], axis=0)[::-1] - seg_rate
    seg_weight = jnp.exp(-suffix)

    def add_segment(running, seg_index):
        segment_part = lax.dynamic_index_in_dim(state_parts, seg_index, 0, keepdims=False).astype(jnp.float32)
        factor = lax.dynamic_index_in_dim(seg_weight, seg_index, 0, keepdims=False)
        scaled = (factor[:, :, None, None] * segment_part).astype(jnp.bfloat16)
        scaled = lax.optimization_barrier(scaled)
        return (running + scaled.astype(jnp.float32), None)
    combined, _ = lax.scan(add_segment, jnp.zeros(state_parts.shape[1:], jnp.float32), jnp.arange(PREFILL_SEGMENTS, dtype=jnp.int32))
    ssm_state = combined[decode_prompt]
    x_window = x_tail[decode_prompt].astype(jnp.float32)
    bc_window = bc_tail[decode_prompt].astype(jnp.float32)
    slot_tokens = token_ids[:, decode_prompt]
    embedded = embedding[slot_tokens]
    normed = rms_scale(embedded.astype(jnp.float32), norm_gain).astype(jnp.bfloat16)
    projected = jnp.einsum('tpd,khed->ktphe', normed.astype(jnp.float32), w_zx.astype(jnp.float32))
    columns = jnp.einsum('tpd,dc->tpc', normed.astype(jnp.float32), w_bcdt.astype(jnp.float32))
    decay_rate = -jnp.exp(a_log)
    gated_steps = []
    for moment in range(STEPS):
        x_window = jnp.concatenate([x_window, projected[1, moment][:, None]], axis=1)
        bc_window = jnp.concatenate([bc_window, columns[moment, :, None, :2 * STATE]], axis=1)
        x_conv = jax.nn.silu(jnp.einsum('pkhe,khe->phe', x_window, conv_x_weight) + conv_x_bias)
        bc_conv = jax.nn.silu(jnp.einsum('pkn,kn->pn', bc_window, conv_bc_weight) + conv_bc_bias)
        step_size = jax.nn.softplus(columns[moment, :, 2 * STATE:] + dt_bias)
        retain = jnp.exp(step_size * decay_rate)
        ssm_state = retain[:, :, None, None] * ssm_state + (step_size[:, :, None] * x_conv)[:, :, :, None] * bc_conv[:, None, None, :STATE]
        output = jnp.einsum('phen,pn->phe', ssm_state, bc_conv[:, STATE:]) + d_skip[None, :, None] * x_conv
        gated_steps.append(output * jax.nn.silu(projected[0, moment]))
        x_window = x_window[:, 1:]
        bc_window = bc_window[:, 1:]
    gated_all = jnp.stack(gated_steps).reshape(STEPS, -1, HEADS * HEAD_DIM)
    normed_out = rms_scale(gated_all, gate_norm_gain.reshape(-1)).astype(jnp.bfloat16)
    mixed = jnp.dot(normed_out.reshape(-1, HEADS * HEAD_DIM), w_out.reshape(HEADS * HEAD_DIM, D), preferred_element_type=jnp.float32)
    return (mixed.reshape(STEPS, -1, D).astype(jnp.bfloat16), ssm_state)
```

```python
import functools

import jax
import jax.numpy as jnp
from jax import lax
from jax.experimental import pallas as pl
from jax.experimental.pallas import tpu as pltpu
from jax.sharding import PartitionSpec as P

HEADS = 128
HEAD_DIM = 64


epsilon = 1e-05


def entering(shard, axis, combine, identity):
    count, here = (lax.axis_size(axis), lax.axis_index(axis))
    everything = lax.all_gather(shard, axis)
    start = jnp.broadcast_to(jnp.asarray(identity, shard.dtype), shard.shape)

    def step(k, before):
        at = count - 1 - k
        reached = at > here
        new = combine(before, everything[at])
        return jnp.where(reached, new, before)

    return lax.fori_loop(0, count, step, start)


def rms_scale(values, gain):
    return values * lax.rsqrt(jnp.mean(values * values, axis=-1, keepdims=True) + epsilon) * gain


def select_rows(picker, values):
    return jnp.tensordot(picker, values, axes=1, precision=lax.Precision.HIGHEST)


def add_rates(earlier, later_one):
    return earlier + later_one


def per_device(
    token_ids,
    decode_prompt,
    embedding,
    norm_gain,
    w_zx,
    w_bcdt,
    conv_x_weight,
    conv_x_bias,
    conv_bc_weight,
    conv_bc_bias,
    dt_bias,
    a_log,
    d_skip,
    gate_norm_gain,
    w_out,
    state_parts,
    seg_rate,
    x_tail,
    bc_tail,
):
    group = lax.axis_index("dp")
    local_count = state_parts.shape[1]
    slot_count = decode_prompt.shape[0]
    head_count = w_zx.shape[1]
    state_width = conv_bc_bias.shape[0] // 2
    after_rates = entering(seg_rate, "ctx", add_rates, jnp.zeros_like(seg_rate))
    seg_weight = jnp.exp(-after_rates[0])
    scaled = seg_weight[:, :, None, None] * state_parts[0].astype(jnp.float32)
    channel_sums = lax.psum_scatter(
        scaled.astype(jnp.bfloat16), "ctx", scatter_dimension=2, tiled=True
    ).astype(jnp.float32)
    combined = lax.all_to_all(
        channel_sums.astype(jnp.bfloat16), "ctx", split_axis=1, concat_axis=2, tiled=True
    ).astype(channel_sums.dtype)
    tails_x = x_tail.astype(jnp.float32)
    tails_bc = bc_tail.astype(jnp.float32)
    own_slots = lax.dynamic_slice_in_dim(decode_prompt, group * local_count, local_count)
    prompt_ids = jnp.arange(slot_count, dtype=jnp.int32)
    every_state, every_x, every_bc = (
        lax.all_gather(combined.astype(jnp.bfloat16), "dp", axis=0, tiled=True).astype(
            combined.dtype
        ),
        lax.all_gather(tails_x.astype(jnp.bfloat16), "dp", axis=0, tiled=True).astype(
            tails_x.dtype
        ),
        lax.all_gather(tails_bc.astype(jnp.bfloat16), "dp", axis=0, tiled=True).astype(
            tails_bc.dtype
        ),
    )
    picker = (own_slots[:, None] == prompt_ids[None, :]).astype(jnp.float32)
    ssm_state = select_rows(picker, every_state)
    x_window = select_rows(picker, every_x)
    bc_window = select_rows(picker, every_bc)
    vocab_rows = embedding.shape[0]
    holder = (decode_prompt[:, None] == prompt_ids[None, :]).astype(jnp.int32)
    slot_tokens = jnp.sum(token_ids[:, None, :] * holder[None], axis=2)
    offset_tokens = slot_tokens - group * vocab_rows
    inside = (offset_tokens >= 0) & (offset_tokens < vocab_rows)
    looked = jnp.take(embedding, jnp.clip(offset_tokens, 0, vocab_rows - 1), axis=0)
    partial_rows = jnp.where(inside[..., None], looked.astype(jnp.float32), 0.0)
    own_rows = lax.psum_scatter(
        partial_rows.astype(jnp.bfloat16), "dp", scatter_dimension=1, tiled=True
    )
    embedded = lax.all_gather(own_rows, ("ctx", "tp"), axis=2, tiled=True)
    steps_count = embedded.shape[0]
    flat_rows = embedded.reshape(-1, embedded.shape[2]).astype(jnp.float32)
    normed = rms_scale(flat_rows, norm_gain).astype(jnp.bfloat16)
    projected = jnp.einsum("rd,khed->krhe", normed, w_zx, preferred_element_type=jnp.float32)
    projected = projected.reshape(
        2, steps_count, local_count, projected.shape[2], projected.shape[3]
    )
    columns = lax.all_gather(
        jnp.dot(normed, w_bcdt, preferred_element_type=jnp.float32),
        ("ctx", "tp"),
        axis=1,
        tiled=True,
    )
    columns = columns.reshape(steps_count, local_count, -1)
    head_block = lax.axis_index("tp") * lax.axis_size("ctx") + lax.axis_index("ctx")
    head_start = 2 * state_width + head_block * head_count
    dt_raw = lax.dynamic_slice_in_dim(columns, head_start, head_count, 2)
    decay_rate = -jnp.exp(a_log)
    gated_steps = []
    for moment in range(steps_count):
        x_window = jnp.concatenate([x_window, projected[1, moment][:, None]], axis=1)
        bc_window = jnp.concatenate(
            [bc_window, columns[moment, :, None, : 2 * state_width]], axis=1
        )
        x_conv = jax.nn.silu(jnp.einsum("pkhe,khe->phe", x_window, conv_x_weight) + conv_x_bias)
        bc_conv = jax.nn.silu(jnp.einsum("pkn,kn->pn", bc_window, conv_bc_weight) + conv_bc_bias)
        step_size = jax.nn.softplus(dt_raw[moment] + dt_bias)
        retain = jnp.exp(step_size * decay_rate)
        ssm_state = (
            retain[:, :, None, None] * ssm_state
            + (step_size[:, :, None] * x_conv)[:, :, :, None] * bc_conv[:, None, None, :state_width]
        )
        output = (
            jnp.einsum("phen,pn->phe", ssm_state, bc_conv[:, state_width:])
            + d_skip[None, :, None] * x_conv
        )
        gated_steps.append(output * jax.nn.silu(projected[0, moment]))
        x_window = x_window[:, 1:]
        bc_window = bc_window[:, 1:]
    gated_all = jnp.stack(gated_steps)
    local_squares = jnp.sum(gated_all * gated_all, axis=(2, 3))
    total_squares = lax.psum(local_squares, ("ctx", "tp"))
    inverse = lax.rsqrt(total_squares / (HEADS * HEAD_DIM) + epsilon)
    normed_out = (gated_all * inverse[:, :, None, None] * gate_norm_gain).astype(jnp.bfloat16)
    partial_out = jnp.einsum("tphe,hed->tpd", normed_out, w_out, preferred_element_type=jnp.float32)
    outer_sum = lax.psum_scatter(
        partial_out.astype(jnp.bfloat16), "ctx", scatter_dimension=2, tiled=True
    ).astype(jnp.float32)
    mixed = lax.psum_scatter(outer_sum, "tp", scatter_dimension=2, tiled=True)
    return (mixed.astype(jnp.bfloat16), ssm_state)


HI = lax.Precision.HIGHEST
F32 = jnp.float32
BF16 = jnp.bfloat16


def f32_dot(a, b):
    return jnp.dot(a, b, precision=HI, preferred_element_type=F32)


def nt_dot(a, b):
    return lax.dot_general(a, b, (((1,), (1,)), ((), ())), preferred_element_type=F32)


def silu(v):
    return v / (1.0 + jnp.exp(-v))


def softplus(v):
    return jnp.maximum(v, 0.0) + jnp.log1p(jnp.exp(-jnp.abs(v)))


ROW_TILE = 16


def drain(ref, sem):
    pltpu.make_async_copy(ref, ref, sem).wait()


def gather_kernel(steps, slots, groups, tok_ref, dec_ref, emb_ref, out_ref, buf, tail, sem, tail_sem):
    vocab = emb_ref.shape[0]
    whole = vocab // ROW_TILE * ROW_TILE
    base = lax.axis_index("dp") * vocab
    per_group = slots // groups
    tail_copy = None
    if whole < vocab:
        tail_copy = pltpu.make_async_copy(emb_ref.at[pl.ds(whole, vocab - whole)], tail, tail_sem)
        tail_copy.start()
    where = []
    for s in range(slots):
        q = dec_ref[s]
        for t in range(steps):
            row = tok_ref[t, q] - base
            clipped = jnp.clip(row, 0, vocab - 1)
            start = jnp.minimum(clipped // ROW_TILE * ROW_TILE, whole - ROW_TILE)
            start = pl.multiple_of(start, ROW_TILE)
            i = s * steps + t
            pltpu.make_async_copy(emb_ref.at[pl.ds(start, ROW_TILE)], buf.at[i], sem).start()
            where.append((row, start))
    if tail_copy is not None:
        tail_copy.wait()
    drain(buf, sem)
    rows = lax.broadcasted_iota(jnp.int32, (ROW_TILE, 1), 0)
    for g in range(groups):
        picked = []
        for t in range(steps):
            for j in range(per_group):
                i = (g * per_group + j) * steps + t
                row, start = where[i]
                value = jnp.sum(
                    jnp.where(rows == row - start, buf[i].astype(F32), 0.0), axis=0, keepdims=True
                )
                if tail_copy is not None:
                    trows = lax.broadcasted_iota(jnp.int32, (vocab - whole, 1), 0)
                    value += jnp.sum(
                        jnp.where(trows == row - whole, tail[...].astype(F32), 0.0),
                        axis=0,
                        keepdims=True,
                    )
                picked.append(value)
        out_ref[g] = jnp.concatenate(picked, axis=0).astype(BF16)


def mixer_kernel(
    sizes,
    dec_hbm,
    part_ref,
    seg_hbm,
    xt_hbm,
    bt_hbm,
    gain_hbm,
    cxw_hbm,
    cxb_hbm,
    cbw_hbm,
    cbb_hbm,
    dtb_hbm,
    alog_hbm,
    skip_hbm,
    gg_hbm,
    wzx_hbm,
    wbc_hbm,
    wout_hbm,
    state_hbm,
    mixed_ref,
    final_ref,
    dec_ref,
    gain_ref,
    cxw_ref,
    cxb_ref,
    cbw_ref,
    cbb_ref,
    dtb_ref,
    alog_ref,
    skip_ref,
    gg_ref,
    pair_recv,
    pair_send,
    wzx,
    wbc,
    wout,
    state_in,
    state_send,
    state_recv,
    plane_recv,
    line_send,
    line_recv,
    seg_recv,
    seg_mate,
    seg_own,
    xt_recv,
    bt_recv,
    col_send,
    col_recv,
    sq_send,
    sq_recv,
    out_send,
    out_recv,
    start_state,
    xfull,
    bcfull,
    gated_ref,
    load_sems,
    small_sems,
    own_sems,
    pair_sems,
    mate_sems,
    state_sems,
    plane_sems,
    line_sems,
    seg_sems,
    xt_sems,
    bt_sems,
    col_sems,
    sq_sems,
    out_sems,
):
    n_ctx, n_dp, n_tp, total_heads = sizes
    c, d, p = lax.axis_index("ctx"), lax.axis_index("dp"), lax.axis_index("tp")
    mine = c * n_tp + p
    here_plane = d * n_ctx + c
    ring, plane = n_ctx * n_tp, n_dp * n_ctx
    steps, per, feats = mixed_ref.shape
    rows = steps * per
    heads, dim = cxb_ref.shape
    chans = heads * dim
    width = cbb_ref.shape[1]
    state_n = width // 2
    taps = cxw_ref.shape[0]
    model = gain_ref.shape[1]
    tp_heads = seg_recv.shape[-1]
    n_cols = wbc_hbm.shape[0]
    all_cols = n_cols * n_ctx * n_tp
    half = wzx_hbm.shape[0] // 2
    mirror = n_tp == 4

    def peer(offset):
        dc, dd, dt = offset
        away = lax.rem(p + dt, n_tp)
        if mirror and dt != n_tp // 2:
            away = n_tp - 1 - (p if dt == 1 else lax.rem(p + n_tp // 2, n_tp))
        return lax.rem(c + dc, n_ctx), lax.rem(d + dd, n_dp), away if dt else p

    def device(offset):
        a, b, e = peer(offset)
        return {"ctx": a, "dp": b, "tp": e}

    far = [1, 2, 3] if mirror else list(range(n_tp - 1, 0, -1))
    routed = [(a, b, 0) for a in reversed(range(n_ctx)) for b in reversed(range(n_dp)) if a + b]
    line = [(0, 0, e) for e in far]
    group = [(a, 0, e) for e in far + [0] for a in reversed(range(n_ctx)) if a + e]
    across = [(0, b, 0) for b in range(1, n_dp)]

    barrier = pltpu.get_barrier_semaphore()
    for o in line + routed:
        pl.semaphore_signal(
            barrier, inc=1, device_id=device(o), device_id_type=pl.DeviceIdType.MESH
        )

    owns = []
    for source, target in (
        (dec_hbm, dec_ref),
        (seg_hbm.at[0], seg_own),
        (xt_hbm, xt_recv.at[d]),
        (bt_hbm, bt_recv.at[d]),
    ):
        load = pltpu.make_async_copy(source, target, own_sems.at[len(owns)])
        load.start()
        owns.append(load)
    loads = []
    smalls = []
    pairs = (
        (state_hbm, state_in),
        (wbc_hbm, wbc),
        (wzx_hbm.at[pl.ds(half, half)], wzx.at[pl.ds(half, half)]),
        (wzx_hbm.at[pl.ds(0, half)], wzx.at[pl.ds(0, half)]),
        (wout_hbm, wout),
    )
    small_pairs = (
        (gain_hbm, gain_ref),
        (cxw_hbm, cxw_ref),
        (cxb_hbm, cxb_ref),
        (cbw_hbm, cbw_ref),
        (cbb_hbm, cbb_ref),
        (dtb_hbm, dtb_ref),
        (alog_hbm, alog_ref),
        (skip_hbm, skip_ref),
        (gg_hbm, gg_ref),
    )

    def fetch(source, target, sem, into):
        load = pltpu.make_async_copy(source, target, sem)
        load.start()
        into.append(load)

    fetch(*pairs[0], load_sems.at[0], loads)
    for i, pair in enumerate(small_pairs):
        fetch(*pair, small_sems.at[i], smalls)
    for i, pair in enumerate(pairs[1:]):
        fetch(*pair, load_sems.at[i + 1], loads)

    def send(source, target, send_sem, recv_sem, place):
        pltpu.make_async_remote_copy(
            src_ref=source,
            dst_ref=target,
            send_sem=send_sem,
            recv_sem=recv_sem,
            device_id=place,
            device_id_type=pl.DeviceIdType.MESH,
        ).start()

    col_send[...] = jnp.zeros_like(col_send)

    pl.semaphore_wait(barrier, len(line) + len(routed))

    for o in routed:
        send(part_ref.at[peer(o)[1]], plane_recv.at[here_plane], plane_sems.at[0], plane_sems.at[1], device(o))
    plane_recv[here_plane] = part_ref[d]

    owns[0].wait()
    owns[1].wait()
    parity = lax.rem(c, 2)
    mate = {"ctx": c + 1 - 2 * parity, "dp": d, "tp": p}
    half_ctx = n_ctx // 2
    blocks = [(a, b) for a in reversed(range(half_ctx)) for b in reversed(range(n_dp))]
    seg_recv[here_plane] = seg_own[...]
    send(seg_own, seg_mate, mate_sems.at[0], mate_sems.at[1], mate)
    for o in routed:
        send(seg_own, seg_recv.at[here_plane], seg_sems.at[0], seg_sems.at[1], device(o))
    picks = []
    for b in range(n_dp):
        target_group = lax.rem(d + b, n_dp)
        pick = jnp.int32(0)
        for j in range(per):
            local = dec_ref[target_group * per + j] - d * per
            pick += jnp.where((local >= 0) & (local < per), local, 0)
        picks.append(pick)
    loads[0].wait()
    for slot, (a, b) in enumerate(blocks):
        first = pl.multiple_of(lax.rem(mate["ctx"] + 2 * a, n_ctx) * chans, chans)
        state_send[slot] = state_in[picks[b], pl.ds(first, chans), :]
        send(state_send.at[slot], pair_recv.at[slot], pair_sems.at[len(blocks)], pair_sems.at[slot], mate)
    owns[2].wait()
    owns[3].wait()
    for o in across:
        send(xt_recv.at[d], xt_recv.at[d], xt_sems.at[0], xt_sems.at[1], device(o))
        send(bt_recv.at[d], bt_recv.at[d], bt_sems.at[0], bt_sems.at[1], device(o))

    fold = (
        lax.broadcasted_iota(jnp.int32, (dim, chans), 0)
        == lax.rem(lax.broadcasted_iota(jnp.int32, (dim, chans), 1), dim)
    ).astype(F32)
    head_rows = lax.broadcasted_iota(jnp.int32, (heads, chans), 0) == lax.div(
        lax.broadcasted_iota(jnp.int32, (heads, chans), 1), dim
    )

    def flat(value):
        return jnp.sum(jnp.where(head_rows, f32_dot(value, fold), 0.0), axis=0, keepdims=True)

    def spread(value, first):
        count = value.shape[1]
        chosen = (
            lax.broadcasted_iota(jnp.int32, (count, chans), 0)
            == first + lax.div(lax.broadcasted_iota(jnp.int32, (count, chans), 1), dim)
        ).astype(F32)
        return f32_dot(value, chosen)

    drain(plane_recv.at[pl.ds(0, plane - 1)], plane_sems.at[1])
    for i in range(n_ctx):
        piece = plane_recv[i].astype(F32)
        for g in range(1, n_dp):
            piece += plane_recv[g * n_ctx + i].astype(F32)
        line_send[i] = piece.astype(BF16)
    for o in line:
        send(line_send, line_recv.at[p], line_sems.at[0], line_sems.at[1], device(o))
    line_recv[p] = line_send[...]

    drain(seg_mate, mate_sems.at[1])
    shrink = []
    for b in range(n_dp):
        row = pl.ds(picks[b], 1)
        shrink.append(jnp.exp(-jnp.where(parity == 0, seg_mate[row, :], seg_own[row, :])))
    ones = [jnp.ones((1, tp_heads), F32)] * n_dp
    shrink = jnp.concatenate(shrink + ones, axis=0)
    shrink_cols = [
        jnp.transpose(spread(shrink, lax.rem(c + 2 * a, n_ctx) * heads)) for a in range(half_ctx)
    ]
    for slot, (a, b) in enumerate(blocks):
        drain(pair_recv.at[slot], pair_sems.at[slot])
        first = pl.multiple_of(lax.rem(c + 2 * a, n_ctx) * chans, chans)
        here = state_in[picks[b], pl.ds(first, chans), :].astype(F32)
        there = pair_recv[slot].astype(F32)
        factor = shrink_cols[a][:, b : b + 1]
        even = jnp.where(parity == 0, here, there)
        odd = jnp.where(parity == 0, there, here)
        added = (factor * even + odd).astype(BF16)
        target = state_recv.at[d * half_ctx + lax.div(c, 2)]
        if a + b:
            pair_send[slot] = added
            send(pair_send.at[slot], target, state_sems.at[0], state_sems.at[1], device((2 * a, b, 0)))
        else:
            state_recv[d * half_ctx + lax.div(c, 2)] = added

    for load in smalls:
        load.wait()
    tap_rows = [flat(cxw_ref[k]) for k in range(taps)]
    bias_row = flat(cxb_ref[...])
    gate_row = flat(gg_ref[...])
    dtb_row = spread(dtb_ref[...], 0)
    rate_row = -jnp.exp(spread(alog_ref[...], 0))
    skip_row = spread(skip_ref[...], 0)

    holders = [lax.div(dec_ref[d * per + j], per) for j in range(per)]
    places = [lax.rem(dec_ref[d * per + j], per) for j in range(per)]
    for sems, ref in ((xt_sems, xt_recv), (bt_sems, bt_recv)):
        if across:
            drain(ref.at[pl.ds(0, n_dp - 1)], sems.at[1])
    plane_rows = lax.broadcasted_iota(jnp.int32, (per, 1), 0)
    for k in range(taps - 1):
        for j in range(per):
            r = k * per + j
            xfull[r : r + 1, :] = flat(xt_recv[holders[j], places[j], k].astype(F32))
            tail = bt_recv[holders[j], k].astype(F32)
            bcfull[r : r + 1, :] = jnp.sum(
                jnp.where(plane_rows == places[j], tail, 0.0), axis=0, keepdims=True
            )

    drain(seg_recv.at[pl.ds(0, plane - 1)], seg_sems.at[1])
    weights = []
    for j in range(per):
        after = jnp.zeros((1, tp_heads), F32)
        ordered = []
        row = pl.ds(places[j], 1)
        for m in reversed(range(half_ctx)):
            ordered.append(jnp.exp(-after))
            for k in (2 * m + 1, 2 * m):
                after = after + seg_recv[holders[j] * n_ctx + k, row, :]
        weights.extend(reversed(ordered))
    weight_cols = jnp.transpose(spread(jnp.concatenate(weights, axis=0), c * heads))

    drain(line_recv.at[pl.ds(0, n_tp - 1)], line_sems.at[1])
    pieces = [line_recv[e, i].astype(F32) for i in range(n_ctx) for e in range(n_tp)]
    embedded = jnp.concatenate(pieces, axis=1)
    scale = lax.rsqrt(jnp.sum(embedded * embedded, axis=1, keepdims=True) / model + epsilon)
    normed = (embedded * scale * gain_ref[...]).astype(BF16)
    loads[1].wait()
    col_send[:, 0:n_cols] = nt_dot(normed, wbc[...])
    for o in group:
        send(col_send, col_recv.at[mine], col_sems.at[0], col_sems.at[1], device(o))
    col_recv[mine] = col_send[...]
    loads[2].wait()
    x_rows = nt_dot(normed, wzx[half : 2 * half, :])
    loads[3].wait()
    z_gate = silu(nt_dot(normed, wzx[0:half, :]))

    lead = (taps - 1) * per
    xfull[lead : lead + rows, :] = x_rows
    conv = bias_row
    for k in range(taps):
        conv = conv + tap_rows[k] * xfull[k * per : k * per + rows, :]
    xc = silu(conv)

    drain(state_recv.at[pl.ds(0, n_dp * half_ctx - 1)], state_sems.at[1])
    for j in range(per):
        begin = None
        for m in range(half_ctx):
            r = j * half_ctx + m
            term = weight_cols[:, r : r + 1] * state_recv[holders[j] * half_ctx + m].astype(F32)
            begin = term if begin is None else begin + term
        start_state[j] = begin

    drain(col_recv.at[pl.ds(0, ring - 1)], col_sems.at[1])
    wide_pad = jnp.zeros((rows, all_cols - col_send.shape[1]), F32)
    columns = jnp.zeros((rows, all_cols), F32)
    for i in range(ring):
        wide = jnp.concatenate([col_recv[i], wide_pad], axis=1)
        columns = columns + (pltpu.roll(wide, n_cols * i, 1) if i else wide)
    bcfull[lead : lead + rows, :] = columns[:, :width]
    conv = cbb_ref[...]
    for k in range(taps):
        conv = conv + cbw_ref[k : k + 1, :] * bcfull[k * per : k * per + rows, :]
    bcc = silu(conv)
    b_all, c_all = bcc[:, :state_n], bcc[:, state_n:]
    head_first = (p * n_ctx + c) * heads
    step_size = softplus(spread(columns[:, width:], head_first) + dtb_row)
    log_keep = step_size * rate_row
    driven = step_size * xc

    row_slot = lax.rem(lax.broadcasted_iota(jnp.int32, (rows, 1), 0), per)
    from_start = jnp.zeros((rows, chans), F32)
    c_low = c_all.astype(BF16)
    for j in range(per):
        from_start += jnp.where(row_slot == j, nt_dot(c_low, start_state[j].astype(BF16)), 0.0)

    def at(value, t):
        return value[t * per : (t + 1) * per]

    total = jnp.zeros((per, chans), F32)
    sums = []
    for t in range(steps):
        total = total + at(log_keep, t)
        sums.append(total)
    for t in range(steps):
        y = jnp.exp(sums[t]) * at(from_start, t) + skip_row * at(xc, t)
        for s in range(t + 1):
            overlap = jnp.sum(at(b_all, s) * at(c_all, t), axis=1, keepdims=True)
            term = at(driven, s) * overlap
            y = y + (term if s == t else jnp.exp(sums[t] - sums[s]) * term)
        gated_ref[t * per : (t + 1) * per, :] = y
    gated = gated_ref[...] * z_gate
    squares = jnp.sum(gated * gated, axis=1, keepdims=True)
    diagonal = lax.broadcasted_iota(jnp.int32, (rows, 128), 0) == lax.broadcasted_iota(
        jnp.int32, (rows, 128), 1
    )
    sq_send[...] = jnp.sum(jnp.where(diagonal, squares, 0.0), axis=0, keepdims=True)
    for o in group:
        send(sq_send, sq_recv.at[mine], sq_sems.at[0], sq_sems.at[1], device(o))
    sq_recv[mine] = sq_send[...]

    loads[4].wait()
    partial = jnp.dot((gated * gate_row).astype(BF16), wout[...], preferred_element_type=F32)
    for i in range(ring):
        out_send[i] = partial[:, i * feats : (i + 1) * feats].astype(BF16)
    for o in group:
        pc, _, pp = peer(o)
        send(out_send.at[pc * n_tp + pp], out_recv.at[mine], out_sems.at[0], out_sems.at[1], device(o))
    out_recv[mine] = out_send[mine]

    late = [jnp.exp(sums[-1] - sums[t]) * at(driven, t) for t in range(steps)]
    flat_rows = jnp.concatenate(late + [jnp.exp(sums[-1])] * (rows // per), axis=0)
    tall = jnp.transpose(flat_rows)
    for j in range(per):
        b_own = jnp.where(row_slot == j, b_all, 0.0)
        final_ref[j] = (
            tall[:, rows + j : rows + j + 1] * start_state[j] + f32_dot(tall[:, :rows], b_own)
        )

    drain(plane_recv.at[pl.ds(0, plane - 1)], plane_sems.at[0])
    drain(line_recv.at[pl.ds(0, n_tp - 1)], line_sems.at[0])
    drain(seg_recv.at[pl.ds(0, plane - 1)], seg_sems.at[0])
    drain(seg_mate, mate_sems.at[0])
    drain(state_send, pair_sems.at[len(blocks)])
    drain(pair_send.at[pl.ds(0, len(blocks) - 1)], state_sems.at[0])
    if across:
        drain(xt_recv.at[pl.ds(0, n_dp - 1)], xt_sems.at[0])
        drain(bt_recv.at[pl.ds(0, n_dp - 1)], bt_sems.at[0])
    drain(col_recv.at[pl.ds(0, ring - 1)], col_sems.at[0])
    drain(sq_recv.at[pl.ds(0, ring - 1)], sq_sems.at[0])
    drain(out_recv.at[pl.ds(0, ring - 1)], out_sems.at[0])

    drain(sq_recv.at[pl.ds(0, ring - 1)], sq_sems.at[1])
    total_squares = sq_recv[0]
    for i in range(1, ring):
        total_squares = total_squares + sq_recv[i]
    total_squares = jnp.sum(jnp.where(diagonal, total_squares, 0.0), axis=1, keepdims=True)
    inverse = lax.rsqrt(total_squares / (total_heads * dim) + epsilon)
    drain(out_recv.at[pl.ds(0, ring - 1)], out_sems.at[1])
    mixed = out_recv[0].astype(F32)
    for i in range(1, ring):
        mixed = mixed + out_recv[i].astype(F32)
    mixed = mixed * inverse
    for t in range(steps):
        mixed_ref[t] = at(mixed, t).astype(BF16)


def kernel_device(
    sizes,
    token_ids,
    decode_prompt,
    embedding,
    norm_gain,
    w_zx,
    w_bcdt,
    conv_x_weight,
    conv_x_bias,
    conv_bc_weight,
    conv_bc_bias,
    dt_bias,
    a_log,
    d_skip,
    gate_norm_gain,
    w_out,
    state_parts,
    seg_rate,
    x_tail,
    bc_tail,
):
    n_ctx, n_dp, n_tp, _ = sizes
    steps = token_ids.shape[0]
    slots = decode_prompt.shape[0]
    per = state_parts.shape[1]
    rows = steps * per
    vocab, feats = embedding.shape
    heads, dim, model = w_zx.shape[1:]
    chans = heads * dim
    tp_heads, state_n = state_parts.shape[2], state_parts.shape[4]
    ring, plane, blocks = n_ctx * n_tp, n_dp * n_ctx, n_dp * (n_ctx // 2)
    smem = pl.BlockSpec(memory_space=pltpu.SMEM)
    vmem = pl.BlockSpec(memory_space=pltpu.VMEM)
    anywhere = pl.BlockSpec(memory_space=pl.ANY)
    sem = pltpu.SemaphoreType.DMA
    rest = max(1, vocab % ROW_TILE)
    part = pl.pallas_call(
        functools.partial(gather_kernel, steps, slots, n_dp),
        out_shape=pltpu.VMEM((n_dp, rows, feats), BF16),
        in_specs=[smem, smem, anywhere],
        out_specs=vmem,
        scratch_shapes=[
            pltpu.VMEM((steps * slots, ROW_TILE, feats), BF16),
            pltpu.VMEM((rest, feats), BF16),
            sem,
            sem,
        ],
        name="gather_rows",
    )(token_ids, decode_prompt, embedding)
    wide = 2 * state_n
    full_rows = -(-(conv_x_weight.shape[0] - 1 + steps) * per // 8) * 8
    smalls = (
        norm_gain[None],
        conv_x_weight,
        conv_x_bias,
        conv_bc_weight,
        conv_bc_bias[None],
        dt_bias[None],
        a_log[None],
        d_skip[None],
        gate_norm_gain,
    )
    bc_planes = jnp.swapaxes(bc_tail, 0, 1)
    mixed, final = pl.pallas_call(
        functools.partial(mixer_kernel, sizes),
        out_shape=(
            pltpu.VMEM((steps, per, feats), BF16),
            pltpu.VMEM((per, chans, state_n), F32),
        ),
        in_specs=[anywhere, vmem] + [anywhere] * 16,
        out_specs=(vmem, vmem),
        scratch_shapes=[
            pltpu.SMEM((slots,), jnp.int32),
            *[pltpu.VMEM(small.shape, small.dtype) for small in smalls],
            pltpu.VMEM((blocks, chans, state_n), BF16),
            pltpu.VMEM((blocks, chans, state_n), BF16),
            pltpu.VMEM((2 * chans, model), BF16),
            pltpu.VMEM(w_bcdt.shape[::-1], BF16),
            pltpu.VMEM((chans, model), BF16),
            pltpu.VMEM((per, tp_heads * dim, state_n), BF16),
            pltpu.VMEM((blocks, chans, state_n), BF16),
            pltpu.VMEM((blocks, chans, state_n), BF16),
            pltpu.VMEM((plane, rows, feats), BF16),
            pltpu.VMEM((n_ctx, rows, feats), BF16),
            pltpu.VMEM((n_tp, n_ctx, rows, feats), BF16),
            pltpu.VMEM((plane, per, tp_heads), F32),
            pltpu.VMEM((per, tp_heads), F32),
            pltpu.VMEM((per, tp_heads), F32),
            pltpu.VMEM((n_dp,) + x_tail.shape, BF16),
            pltpu.VMEM((n_dp,) + bc_planes.shape, BF16),
            pltpu.VMEM((rows, 128), F32),
            pltpu.VMEM((ring, rows, 128), F32),
            pltpu.VMEM((1, 128), F32),
            pltpu.VMEM((ring, 1, 128), F32),
            pltpu.VMEM((ring, rows, feats), BF16),
            pltpu.VMEM((ring, rows, feats), BF16),
            pltpu.VMEM((per, chans, state_n), F32),
            pltpu.VMEM((full_rows, chans), F32),
            pltpu.VMEM((full_rows, wide), F32),
            pltpu.VMEM((rows, chans), F32),
            sem((5,)),
            sem((len(smalls),)),
            sem((4,)),
            sem((blocks + 1,)),
            *[sem((2,))] * 10,
        ],
        compiler_params=pltpu.CompilerParams(
            collective_id=0, has_side_effects=True, vmem_limit_bytes=56 * 1024 * 1024
        ),
        name="mixer",
    )(
        decode_prompt,
        pltpu.with_memory_space_constraint(part, pltpu.VMEM),
        seg_rate,
        x_tail,
        bc_planes,
        *smalls,
        w_zx.reshape(2 * chans, model),
        w_bcdt.T,
        w_out.reshape(chans, model),
        state_parts.reshape(per, tp_heads * dim, state_n),
    )
    return mixed, final.reshape(per, heads, dim, state_n)


def choose_device(sizes, *args):
    embedding, w_zx, w_bcdt = args[2], args[4], args[5]
    heads, dim = w_zx.shape[1:3]
    fits = (
        embedding.shape[1] % 128 == 0
        and sizes[0] % 2 == 0
        and (heads * dim) % 128 == 0
        and w_bcdt.shape[1] <= 128
        and embedding.shape[0] >= ROW_TILE
    )
    if fits:
        return kernel_device(sizes, *args)
    return per_device(*args)


def solution(mesh):
    sizes = (mesh.shape["ctx"], mesh.shape["dp"], mesh.shape["tp"], HEADS)
    return jax.shard_map(
        functools.partial(choose_device, sizes),
        mesh=mesh,
        in_specs=(
            P(),
            P(),
            P("dp", ("ctx", "tp")),
            P(),
            P(None, ("tp", "ctx"), None, None),
            P(None, ("ctx", "tp")),
            P(None, ("tp", "ctx"), None),
            P(("tp", "ctx"), None),
            P(),
            P(),
            P(("tp", "ctx")),
            P(("tp", "ctx")),
            P(("tp", "ctx")),
            P(("tp", "ctx"), None),
            P(("tp", "ctx"), None, None),
            P("ctx", "dp", "tp", None, None),
            P("ctx", "dp", "tp"),
            P("dp", None, ("tp", "ctx"), None),
            P("dp", None, None),
        ),
        out_specs=(P(None, "dp", ("ctx", "tp")), P("dp", ("tp", "ctx"), None, None)),
        check_vma=False,
    )
```

```python
import functools

import jax
import jax.numpy as jnp
from jax import lax
from jax.experimental import pallas as pl
from jax.experimental.pallas import tpu as pltpu
from jax.sharding import PartitionSpec as P

HEADS = 128
HEAD_DIM = 64


epsilon = 1e-05


def entering(shard, axis, combine, identity):
    count, here = (lax.axis_size(axis), lax.axis_index(axis))
    everything = lax.all_gather(shard, axis)
    start = jnp.broadcast_to(jnp.asarray(identity, shard.dtype), shard.shape)

    def step(k, before):
        at = count - 1 - k
        reached = at > here
        new = combine(before, everything[at])
        return jnp.where(reached, new, before)

    return lax.fori_loop(0, count, step, start)


def rms_scale(values, gain):
    return values * lax.rsqrt(jnp.mean(values * values, axis=-1, keepdims=True) + epsilon) * gain


def select_rows(picker, values):
    return jnp.tensordot(picker, values, axes=1, precision=lax.Precision.HIGHEST)


def add_rates(earlier, later_one):
    return earlier + later_one


def per_device(
    token_ids,
    decode_prompt,
    embedding,
    norm_gain,
    w_zx,
    w_bcdt,
    conv_x_weight,
    conv_x_bias,
    conv_bc_weight,
    conv_bc_bias,
    dt_bias,
    a_log,
    d_skip,
    gate_norm_gain,
    w_out,
    state_parts,
    seg_rate,
    x_tail,
    bc_tail,
):
    group = lax.axis_index("dp")
    local_count = state_parts.shape[1]
    slot_count = decode_prompt.shape[0]
    head_count = w_zx.shape[1]
    state_width = conv_bc_bias.shape[0] // 2
    after_rates = entering(seg_rate, "ctx", add_rates, jnp.zeros_like(seg_rate))
    seg_weight = jnp.exp(-after_rates[0])
    scaled = seg_weight[:, :, None, None] * state_parts[0].astype(jnp.float32)
    channel_sums = lax.psum_scatter(
        scaled.astype(jnp.bfloat16), "ctx", scatter_dimension=2, tiled=True
    ).astype(jnp.float32)
    combined = lax.all_to_all(
        channel_sums.astype(jnp.bfloat16), "ctx", split_axis=1, concat_axis=2, tiled=True
    ).astype(channel_sums.dtype)
    tails_x = x_tail.astype(jnp.float32)
    tails_bc = bc_tail.astype(jnp.float32)
    own_slots = lax.dynamic_slice_in_dim(decode_prompt, group * local_count, local_count)
    prompt_ids = jnp.arange(slot_count, dtype=jnp.int32)
    every_state, every_x, every_bc = (
        lax.all_gather(combined.astype(jnp.bfloat16), "dp", axis=0, tiled=True).astype(
            combined.dtype
        ),
        lax.all_gather(tails_x.astype(jnp.bfloat16), "dp", axis=0, tiled=True).astype(
            tails_x.dtype
        ),
        lax.all_gather(tails_bc.astype(jnp.bfloat16), "dp", axis=0, tiled=True).astype(
            tails_bc.dtype
        ),
    )
    picker = (own_slots[:, None] == prompt_ids[None, :]).astype(jnp.float32)
    ssm_state = select_rows(picker, every_state)
    x_window = select_rows(picker, every_x)
    bc_window = select_rows(picker, every_bc)
    vocab_rows = embedding.shape[0]
    holder = (decode_prompt[:, None] == prompt_ids[None, :]).astype(jnp.int32)
    slot_tokens = jnp.sum(token_ids[:, None, :] * holder[None], axis=2)
    offset_tokens = slot_tokens - group * vocab_rows
    inside = (offset_tokens >= 0) & (offset_tokens < vocab_rows)
    looked = jnp.take(embedding, jnp.clip(offset_tokens, 0, vocab_rows - 1), axis=0)
    partial_rows = jnp.where(inside[..., None], looked.astype(jnp.float32), 0.0)
    own_rows = lax.psum_scatter(
        partial_rows.astype(jnp.bfloat16), "dp", scatter_dimension=1, tiled=True
    )
    embedded = lax.all_gather(own_rows, ("ctx", "tp"), axis=2, tiled=True)
    steps_count = embedded.shape[0]
    flat_rows = embedded.reshape(-1, embedded.shape[2]).astype(jnp.float32)
    normed = rms_scale(flat_rows, norm_gain).astype(jnp.bfloat16)
    projected = jnp.einsum("rd,khed->krhe", normed, w_zx, preferred_element_type=jnp.float32)
    projected = projected.reshape(
        2, steps_count, local_count, projected.shape[2], projected.shape[3]
    )
    columns = lax.all_gather(
        jnp.dot(normed, w_bcdt, preferred_element_type=jnp.float32),
        ("ctx", "tp"),
        axis=1,
        tiled=True,
    )
    columns = columns.reshape(steps_count, local_count, -1)
    head_block = lax.axis_index("tp") * lax.axis_size("ctx") + lax.axis_index("ctx")
    head_start = 2 * state_width + head_block * head_count
    dt_raw = lax.dynamic_slice_in_dim(columns, head_start, head_count, 2)
    decay_rate = -jnp.exp(a_log)
    gated_steps = []
    for moment in range(steps_count):
        x_window = jnp.concatenate([x_window, projected[1, moment][:, None]], axis=1)
        bc_window = jnp.concatenate(
            [bc_window, columns[moment, :, None, : 2 * state_width]], axis=1
        )
        x_conv = jax.nn.silu(jnp.einsum("pkhe,khe->phe", x_window, conv_x_weight) + conv_x_bias)
        bc_conv = jax.nn.silu(jnp.einsum("pkn,kn->pn", bc_window, conv_bc_weight) + conv_bc_bias)
        step_size = jax.nn.softplus(dt_raw[moment] + dt_bias)
        retain = jnp.exp(step_size * decay_rate)
        ssm_state = (
            retain[:, :, None, None] * ssm_state
            + (step_size[:, :, None] * x_conv)[:, :, :, None] * bc_conv[:, None, None, :state_width]
        )
        output = (
            jnp.einsum("phen,pn->phe", ssm_state, bc_conv[:, state_width:])
            + d_skip[None, :, None] * x_conv
        )
        gated_steps.append(output * jax.nn.silu(projected[0, moment]))
        x_window = x_window[:, 1:]
        bc_window = bc_window[:, 1:]
    gated_all = jnp.stack(gated_steps)
    local_squares = jnp.sum(gated_all * gated_all, axis=(2, 3))
    total_squares = lax.psum(local_squares, ("ctx", "tp"))
    inverse = lax.rsqrt(total_squares / (HEADS * HEAD_DIM) + epsilon)
    normed_out = (gated_all * inverse[:, :, None, None] * gate_norm_gain).astype(jnp.bfloat16)
    partial_out = jnp.einsum("tphe,hed->tpd", normed_out, w_out, preferred_element_type=jnp.float32)
    outer_sum = lax.psum_scatter(
        partial_out.astype(jnp.bfloat16), "ctx", scatter_dimension=2, tiled=True
    ).astype(jnp.float32)
    mixed = lax.psum_scatter(outer_sum, "tp", scatter_dimension=2, tiled=True)
    return (mixed.astype(jnp.bfloat16), ssm_state)


HI = lax.Precision.HIGHEST
F32 = jnp.float32
BF16 = jnp.bfloat16


def f32_dot(a, b):
    return jnp.dot(a, b, precision=HI, preferred_element_type=F32)


def nt_dot(a, b):
    return lax.dot_general(a, b, (((1,), (1,)), ((), ())), preferred_element_type=F32)


def silu(v):
    return v / (1.0 + jnp.exp(-v))


def softplus(v):
    return jnp.maximum(v, 0.0) + jnp.log1p(jnp.exp(-jnp.abs(v)))


ROW_TILE = 16


def drain(ref, sem):
    pltpu.make_async_copy(ref, ref, sem).wait()


def gather_kernel(steps, slots, groups, tok_ref, dec_ref, emb_ref, out_ref, buf, tail, sem, tail_sem):
    vocab = emb_ref.shape[0]
    whole = vocab // ROW_TILE * ROW_TILE
    base = lax.axis_index("dp") * vocab
    per_group = slots // groups
    tail_copy = None
    if whole < vocab:
        tail_copy = pltpu.make_async_copy(emb_ref.at[pl.ds(whole, vocab - whole)], tail, tail_sem)
        tail_copy.start()
    where = []
    for s in range(slots):
        q = dec_ref[s]
        for t in range(steps):
            row = tok_ref[t, q] - base
            clipped = jnp.clip(row, 0, vocab - 1)
            start = jnp.minimum(clipped // ROW_TILE * ROW_TILE, whole - ROW_TILE)
            start = pl.multiple_of(start, ROW_TILE)
            i = s * steps + t
            pltpu.make_async_copy(emb_ref.at[pl.ds(start, ROW_TILE)], buf.at[i], sem).start()
            where.append((row, start))
    if tail_copy is not None:
        tail_copy.wait()
    drain(buf, sem)
    rows = lax.broadcasted_iota(jnp.int32, (ROW_TILE, 1), 0)
    for g in range(groups):
        picked = []
        for t in range(steps):
            for j in range(per_group):
                i = (g * per_group + j) * steps + t
                row, start = where[i]
                value = jnp.sum(
                    jnp.where(rows == row - start, buf[i].astype(F32), 0.0), axis=0, keepdims=True
                )
                if tail_copy is not None:
                    trows = lax.broadcasted_iota(jnp.int32, (vocab - whole, 1), 0)
                    value += jnp.sum(
                        jnp.where(trows == row - whole, tail[...].astype(F32), 0.0),
                        axis=0,
                        keepdims=True,
                    )
                picked.append(value)
        out_ref[g] = jnp.concatenate(picked, axis=0).astype(BF16)


def mixer_kernel(
    sizes,
    dec_hbm,
    part_ref,
    seg_hbm,
    xt_hbm,
    bt_hbm,
    gain_hbm,
    cxw_hbm,
    cxb_hbm,
    cbw_hbm,
    cbb_hbm,
    dtb_hbm,
    alog_hbm,
    skip_hbm,
    gg_hbm,
    wzx_hbm,
    wbc_hbm,
    wout_hbm,
    state_hbm,
    mixed_ref,
    final_ref,
    dec_ref,
    gain_ref,
    cxw_ref,
    cxb_ref,
    cbw_ref,
    cbb_ref,
    dtb_ref,
    alog_ref,
    skip_ref,
    gg_ref,
    pair_recv,
    pair_send,
    wzx,
    wbc,
    wout,
    state_in,
    state_send,
    state_recv,
    plane_recv,
    line_send,
    line_recv,
    seg_recv,
    seg_mate,
    seg_own,
    xt_recv,
    bt_recv,
    col_send,
    col_recv,
    sq_send,
    sq_recv,
    out_send,
    out_recv,
    start_state,
    xfull,
    bcfull,
    gated_ref,
    load_sems,
    small_sems,
    own_sems,
    pair_sems,
    mate_sems,
    state_sems,
    plane_sems,
    line_sems,
    seg_sems,
    xt_sems,
    bt_sems,
    col_sems,
    sq_sems,
    out_sems,
):
    n_ctx, n_dp, n_tp, total_heads = sizes
    c, d, p = lax.axis_index("ctx"), lax.axis_index("dp"), lax.axis_index("tp")
    mine = c * n_tp + p
    here_plane = d * n_ctx + c
    ring, plane = n_ctx * n_tp, n_dp * n_ctx
    steps, per, feats = mixed_ref.shape
    rows = steps * per
    heads, dim = cxb_ref.shape
    chans = heads * dim
    width = cbb_ref.shape[1]
    state_n = width // 2
    taps = cxw_ref.shape[0]
    model = gain_ref.shape[1]
    tp_heads = seg_recv.shape[-1]
    n_cols = wbc_hbm.shape[0]
    all_cols = n_cols * n_ctx * n_tp
    half = wzx_hbm.shape[0] // 2
    mirror = n_tp == 4

    def peer(offset):
        dc, dd, dt = offset
        away = lax.rem(p + dt, n_tp)
        if mirror and dt != n_tp // 2:
            away = n_tp - 1 - (p if dt == 1 else lax.rem(p + n_tp // 2, n_tp))
        return lax.rem(c + dc, n_ctx), lax.rem(d + dd, n_dp), away if dt else p

    def device(offset):
        a, b, e = peer(offset)
        return {"ctx": a, "dp": b, "tp": e}

    far = [1, 2, 3] if mirror else list(range(n_tp - 1, 0, -1))
    routed = [(a, b, 0) for a in reversed(range(n_ctx)) for b in reversed(range(n_dp)) if a + b]
    line = [(0, 0, e) for e in far]
    group = [(a, 0, e) for e in far + [0] for a in reversed(range(n_ctx)) if a + e]
    across = [(0, b, 0) for b in range(1, n_dp)]

    barrier = pltpu.get_barrier_semaphore()
    for o in line + routed:
        pl.semaphore_signal(
            barrier, inc=1, device_id=device(o), device_id_type=pl.DeviceIdType.MESH
        )

    owns = []
    for source, target in (
        (dec_hbm, dec_ref),
        (seg_hbm.at[0], seg_own),
        (xt_hbm, xt_recv.at[d]),
        (bt_hbm, bt_recv.at[d]),
    ):
        load = pltpu.make_async_copy(source, target, own_sems.at[len(owns)])
        load.start()
        owns.append(load)
    loads = []
    smalls = []
    pairs = (
        (state_hbm, state_in),
        (wbc_hbm, wbc),
        (wzx_hbm.at[pl.ds(half, half)], wzx.at[pl.ds(half, half)]),
        (wzx_hbm.at[pl.ds(0, half)], wzx.at[pl.ds(0, half)]),
        (wout_hbm, wout),
    )
    small_pairs = (
        (gain_hbm, gain_ref),
        (cxw_hbm, cxw_ref),
        (cxb_hbm, cxb_ref),
        (cbw_hbm, cbw_ref),
        (cbb_hbm, cbb_ref),
        (dtb_hbm, dtb_ref),
        (alog_hbm, alog_ref),
        (skip_hbm, skip_ref),
        (gg_hbm, gg_ref),
    )

    def fetch(source, target, sem, into):
        load = pltpu.make_async_copy(source, target, sem)
        load.start()
        into.append(load)

    fetch(*pairs[0], load_sems.at[0], loads)
    for i, pair in enumerate(small_pairs):
        fetch(*pair, small_sems.at[i], smalls)
    def send(source, target, send_sem, recv_sem, place):
        pltpu.make_async_remote_copy(
            src_ref=source,
            dst_ref=target,
            send_sem=send_sem,
            recv_sem=recv_sem,
            device_id=place,
            device_id_type=pl.DeviceIdType.MESH,
        ).start()

    col_send[...] = jnp.zeros_like(col_send)

    pl.semaphore_wait(barrier, len(line) + len(routed))

    for o in routed:
        send(part_ref.at[peer(o)[1]], plane_recv.at[here_plane], plane_sems.at[0], plane_sems.at[1], device(o))
    plane_recv[here_plane] = part_ref[d]

    owns[0].wait()
    owns[1].wait()
    parity = lax.rem(c, 2)
    mate = {"ctx": c + 1 - 2 * parity, "dp": d, "tp": p}
    half_ctx = n_ctx // 2
    blocks = [(a, b) for a in reversed(range(half_ctx)) for b in reversed(range(n_dp))]
    seg_recv[here_plane] = seg_own[...]
    send(seg_own, seg_mate, mate_sems.at[0], mate_sems.at[1], mate)
    for o in routed:
        send(seg_own, seg_recv.at[here_plane], seg_sems.at[0], seg_sems.at[1], device(o))
    owns[2].wait()
    owns[3].wait()
    for o in across:
        send(xt_recv.at[d], xt_recv.at[d], xt_sems.at[0], xt_sems.at[1], device(o))
        send(bt_recv.at[d], bt_recv.at[d], bt_sems.at[0], bt_sems.at[1], device(o))
    picks = []
    for b in range(n_dp):
        target_group = lax.rem(d + b, n_dp)
        pick = jnp.int32(0)
        for j in range(per):
            local = dec_ref[target_group * per + j] - d * per
            pick += jnp.where((local >= 0) & (local < per), local, 0)
        picks.append(pick)
    loads[0].wait()
    for slot, (a, b) in enumerate(blocks):
        first = pl.multiple_of(lax.rem(mate["ctx"] + 2 * a, n_ctx) * chans, chans)
        state_send[slot] = state_in[picks[b], pl.ds(first, chans), :]
        send(state_send.at[slot], pair_recv.at[slot], pair_sems.at[len(blocks)], pair_sems.at[slot], mate)

    for i, pair in enumerate(pairs[1:]):
        fetch(*pair, load_sems.at[i + 1], loads)

    fold = (
        lax.broadcasted_iota(jnp.int32, (dim, chans), 0)
        == lax.rem(lax.broadcasted_iota(jnp.int32, (dim, chans), 1), dim)
    ).astype(F32)
    head_rows = lax.broadcasted_iota(jnp.int32, (heads, chans), 0) == lax.div(
        lax.broadcasted_iota(jnp.int32, (heads, chans), 1), dim
    )

    def flat(value):
        return jnp.sum(jnp.where(head_rows, f32_dot(value, fold), 0.0), axis=0, keepdims=True)

    def spread(value, first):
        count = value.shape[1]
        chosen = (
            lax.broadcasted_iota(jnp.int32, (count, chans), 0)
            == first + lax.div(lax.broadcasted_iota(jnp.int32, (count, chans), 1), dim)
        ).astype(F32)
        return f32_dot(value, chosen)

    drain(seg_mate, mate_sems.at[1])
    shrink = []
    for b in range(n_dp):
        row = pl.ds(picks[b], 1)
        shrink.append(jnp.exp(-jnp.where(parity == 0, seg_mate[row, :], seg_own[row, :])))
    ones = [jnp.ones((1, tp_heads), F32)] * n_dp
    shrink = jnp.concatenate(shrink + ones, axis=0)
    shrink_cols = [
        jnp.transpose(spread(shrink, lax.rem(c + 2 * a, n_ctx) * heads)) for a in range(half_ctx)
    ]
    for slot, (a, b) in enumerate(blocks):
        drain(pair_recv.at[slot], pair_sems.at[slot])
        first = pl.multiple_of(lax.rem(c + 2 * a, n_ctx) * chans, chans)
        here = state_in[picks[b], pl.ds(first, chans), :].astype(F32)
        there = pair_recv[slot].astype(F32)
        factor = shrink_cols[a][:, b : b + 1]
        even = jnp.where(parity == 0, here, there)
        odd = jnp.where(parity == 0, there, here)
        added = (factor * even + odd).astype(BF16)
        target = state_recv.at[d * half_ctx + lax.div(c, 2)]
        if a + b:
            pair_send[slot] = added
            send(pair_send.at[slot], target, state_sems.at[0], state_sems.at[1], device((2 * a, b, 0)))
        else:
            state_recv[d * half_ctx + lax.div(c, 2)] = added

    drain(plane_recv.at[pl.ds(0, plane - 1)], plane_sems.at[1])
    for i in range(n_ctx):
        piece = plane_recv[i].astype(F32)
        for g in range(1, n_dp):
            piece += plane_recv[g * n_ctx + i].astype(F32)
        line_send[i] = piece.astype(BF16)
    for o in line:
        send(line_send, line_recv.at[p], line_sems.at[0], line_sems.at[1], device(o))
    line_recv[p] = line_send[...]


    for load in smalls:
        load.wait()
    tap_rows = [flat(cxw_ref[k]) for k in range(taps)]
    bias_row = flat(cxb_ref[...])
    gate_row = flat(gg_ref[...])
    dtb_row = spread(dtb_ref[...], 0)
    rate_row = -jnp.exp(spread(alog_ref[...], 0))
    skip_row = spread(skip_ref[...], 0)

    holders = [lax.div(dec_ref[d * per + j], per) for j in range(per)]
    places = [lax.rem(dec_ref[d * per + j], per) for j in range(per)]
    for sems, ref in ((xt_sems, xt_recv), (bt_sems, bt_recv)):
        if across:
            drain(ref.at[pl.ds(0, n_dp - 1)], sems.at[1])
    plane_rows = lax.broadcasted_iota(jnp.int32, (per, 1), 0)
    for k in range(taps - 1):
        for j in range(per):
            r = k * per + j
            xfull[r : r + 1, :] = flat(xt_recv[holders[j], places[j], k].astype(F32))
            tail = bt_recv[holders[j], k].astype(F32)
            bcfull[r : r + 1, :] = jnp.sum(
                jnp.where(plane_rows == places[j], tail, 0.0), axis=0, keepdims=True
            )

    drain(seg_recv.at[pl.ds(0, plane - 1)], seg_sems.at[1])
    weights = []
    for j in range(per):
        after = jnp.zeros((1, tp_heads), F32)
        ordered = []
        row = pl.ds(places[j], 1)
        for m in reversed(range(half_ctx)):
            ordered.append(jnp.exp(-after))
            for k in (2 * m + 1, 2 * m):
                after = after + seg_recv[holders[j] * n_ctx + k, row, :]
        weights.extend(reversed(ordered))
    weight_cols = jnp.transpose(spread(jnp.concatenate(weights, axis=0), c * heads))

    drain(line_recv.at[pl.ds(0, n_tp - 1)], line_sems.at[1])
    pieces = [line_recv[e, i].astype(F32) for i in range(n_ctx) for e in range(n_tp)]
    embedded = jnp.concatenate(pieces, axis=1)
    scale = lax.rsqrt(jnp.sum(embedded * embedded, axis=1, keepdims=True) / model + epsilon)
    normed = (embedded * scale * gain_ref[...]).astype(BF16)
    loads[1].wait()
    col_send[:, 0:n_cols] = nt_dot(normed, wbc[...])
    for o in group:
        send(col_send, col_recv.at[mine], col_sems.at[0], col_sems.at[1], device(o))
    col_recv[mine] = col_send[...]
    loads[2].wait()
    x_rows = nt_dot(normed, wzx[half : 2 * half, :])
    loads[3].wait()
    z_gate = silu(nt_dot(normed, wzx[0:half, :]))

    lead = (taps - 1) * per
    xfull[lead : lead + rows, :] = x_rows
    conv = bias_row
    for k in range(taps):
        conv = conv + tap_rows[k] * xfull[k * per : k * per + rows, :]
    xc = silu(conv)

    drain(state_recv.at[pl.ds(0, n_dp * half_ctx - 1)], state_sems.at[1])
    for j in range(per):
        begin = None
        for m in range(half_ctx):
            r = j * half_ctx + m
            term = weight_cols[:, r : r + 1] * state_recv[holders[j] * half_ctx + m].astype(F32)
            begin = term if begin is None else begin + term
        start_state[j] = begin

    drain(col_recv.at[pl.ds(0, ring - 1)], col_sems.at[1])
    wide_pad = jnp.zeros((rows, all_cols - col_send.shape[1]), F32)
    columns = jnp.zeros((rows, all_cols), F32)
    for i in range(ring):
        wide = jnp.concatenate([col_recv[i], wide_pad], axis=1)
        columns = columns + (pltpu.roll(wide, n_cols * i, 1) if i else wide)
    bcfull[lead : lead + rows, :] = columns[:, :width]
    conv = cbb_ref[...]
    for k in range(taps):
        conv = conv + cbw_ref[k : k + 1, :] * bcfull[k * per : k * per + rows, :]
    bcc = silu(conv)
    b_all, c_all = bcc[:, :state_n], bcc[:, state_n:]
    head_first = (p * n_ctx + c) * heads
    step_size = softplus(spread(columns[:, width:], head_first) + dtb_row)
    log_keep = step_size * rate_row
    driven = step_size * xc

    row_slot = lax.rem(lax.broadcasted_iota(jnp.int32, (rows, 1), 0), per)
    from_start = jnp.zeros((rows, chans), F32)
    c_low = c_all.astype(BF16)
    for j in range(per):
        from_start += jnp.where(row_slot == j, nt_dot(c_low, start_state[j].astype(BF16)), 0.0)

    def at(value, t):
        return value[t * per : (t + 1) * per]

    total = jnp.zeros((per, chans), F32)
    sums = []
    for t in range(steps):
        total = total + at(log_keep, t)
        sums.append(total)
    for t in range(steps):
        y = jnp.exp(sums[t]) * at(from_start, t) + skip_row * at(xc, t)
        for s in range(t + 1):
            overlap = jnp.sum(at(b_all, s) * at(c_all, t), axis=1, keepdims=True)
            term = at(driven, s) * overlap
            y = y + (term if s == t else jnp.exp(sums[t] - sums[s]) * term)
        gated_ref[t * per : (t + 1) * per, :] = y
    gated = gated_ref[...] * z_gate
    squares = jnp.sum(gated * gated, axis=1, keepdims=True)
    diagonal = lax.broadcasted_iota(jnp.int32, (rows, 128), 0) == lax.broadcasted_iota(
        jnp.int32, (rows, 128), 1
    )
    sq_send[...] = jnp.sum(jnp.where(diagonal, squares, 0.0), axis=0, keepdims=True)
    for o in group:
        send(sq_send, sq_recv.at[mine], sq_sems.at[0], sq_sems.at[1], device(o))
    sq_recv[mine] = sq_send[...]

    loads[4].wait()
    partial = jnp.dot((gated * gate_row).astype(BF16), wout[...], preferred_element_type=F32)
    for i in range(ring):
        out_send[i] = partial[:, i * feats : (i + 1) * feats].astype(BF16)
    for o in group:
        pc, _, pp = peer(o)
        send(out_send.at[pc * n_tp + pp], out_recv.at[mine], out_sems.at[0], out_sems.at[1], device(o))
    out_recv[mine] = out_send[mine]

    late = [jnp.exp(sums[-1] - sums[t]) * at(driven, t) for t in range(steps)]
    flat_rows = jnp.concatenate(late + [jnp.exp(sums[-1])] * (rows // per), axis=0)
    tall = jnp.transpose(flat_rows)
    for j in range(per):
        b_own = jnp.where(row_slot == j, b_all, 0.0)
        final_ref[j] = (
            tall[:, rows + j : rows + j + 1] * start_state[j] + f32_dot(tall[:, :rows], b_own)
        )

    drain(plane_recv.at[pl.ds(0, plane - 1)], plane_sems.at[0])
    drain(line_recv.at[pl.ds(0, n_tp - 1)], line_sems.at[0])
    drain(seg_recv.at[pl.ds(0, plane - 1)], seg_sems.at[0])
    drain(seg_mate, mate_sems.at[0])
    drain(state_send, pair_sems.at[len(blocks)])
    drain(pair_send.at[pl.ds(0, len(blocks) - 1)], state_sems.at[0])
    if across:
        drain(xt_recv.at[pl.ds(0, n_dp - 1)], xt_sems.at[0])
        drain(bt_recv.at[pl.ds(0, n_dp - 1)], bt_sems.at[0])
    drain(col_recv.at[pl.ds(0, ring - 1)], col_sems.at[0])
    drain(sq_recv.at[pl.ds(0, ring - 1)], sq_sems.at[0])
    drain(out_recv.at[pl.ds(0, ring - 1)], out_sems.at[0])

    drain(sq_recv.at[pl.ds(0, ring - 1)], sq_sems.at[1])
    total_squares = sq_recv[0]
    for i in range(1, ring):
        total_squares = total_squares + sq_recv[i]
    total_squares = jnp.sum(jnp.where(diagonal, total_squares, 0.0), axis=1, keepdims=True)
    inverse = lax.rsqrt(total_squares / (total_heads * dim) + epsilon)
    drain(out_recv.at[pl.ds(0, ring - 1)], out_sems.at[1])
    mixed = out_recv[0].astype(F32)
    for i in range(1, ring):
        mixed = mixed + out_recv[i].astype(F32)
    mixed = mixed * inverse
    for t in range(steps):
        mixed_ref[t] = at(mixed, t).astype(BF16)


def tail_kernel(mixed_in, final_in, mixed_out, final_out, sems):
    copies = [
        pltpu.make_async_copy(final_in, final_out, sems.at[0]),
        pltpu.make_async_copy(mixed_in, mixed_out, sems.at[1]),
    ]
    for copy in copies:
        copy.start()
    for copy in copies:
        copy.wait()


def kernel_device(
    sizes,
    token_ids,
    decode_prompt,
    embedding,
    norm_gain,
    w_zx,
    w_bcdt,
    conv_x_weight,
    conv_x_bias,
    conv_bc_weight,
    conv_bc_bias,
    dt_bias,
    a_log,
    d_skip,
    gate_norm_gain,
    w_out,
    state_parts,
    seg_rate,
    x_tail,
    bc_tail,
):
    n_ctx, n_dp, n_tp, _ = sizes
    steps = token_ids.shape[0]
    slots = decode_prompt.shape[0]
    per = state_parts.shape[1]
    rows = steps * per
    vocab, feats = embedding.shape
    heads, dim, model = w_zx.shape[1:]
    chans = heads * dim
    tp_heads, state_n = state_parts.shape[2], state_parts.shape[4]
    ring, plane, blocks = n_ctx * n_tp, n_dp * n_ctx, n_dp * (n_ctx // 2)
    smem = pl.BlockSpec(memory_space=pltpu.SMEM)
    vmem = pl.BlockSpec(memory_space=pltpu.VMEM)
    anywhere = pl.BlockSpec(memory_space=pl.ANY)
    sem = pltpu.SemaphoreType.DMA
    rest = max(1, vocab % ROW_TILE)
    part = pl.pallas_call(
        functools.partial(gather_kernel, steps, slots, n_dp),
        out_shape=pltpu.VMEM((n_dp, rows, feats), BF16),
        in_specs=[smem, smem, anywhere],
        out_specs=vmem,
        scratch_shapes=[
            pltpu.VMEM((steps * slots, ROW_TILE, feats), BF16),
            pltpu.VMEM((rest, feats), BF16),
            sem,
            sem,
        ],
        name="gather_rows",
    )(token_ids, decode_prompt, embedding)
    wide = 2 * state_n
    full_rows = -(-(conv_x_weight.shape[0] - 1 + steps) * per // 8) * 8
    smalls = (
        norm_gain[None],
        conv_x_weight,
        conv_x_bias,
        conv_bc_weight,
        conv_bc_bias[None],
        dt_bias[None],
        a_log[None],
        d_skip[None],
        gate_norm_gain,
    )
    bc_planes = jnp.swapaxes(bc_tail, 0, 1)
    mixed, final = pl.pallas_call(
        functools.partial(mixer_kernel, sizes),
        out_shape=(
            pltpu.VMEM((steps, per, feats), BF16),
            pltpu.VMEM((per, chans, state_n), F32),
        ),
        in_specs=[anywhere, vmem] + [anywhere] * 16,
        out_specs=(vmem, vmem),
        scratch_shapes=[
            pltpu.SMEM((slots,), jnp.int32),
            *[pltpu.VMEM(small.shape, small.dtype) for small in smalls],
            pltpu.VMEM((blocks, chans, state_n), BF16),
            pltpu.VMEM((blocks, chans, state_n), BF16),
            pltpu.VMEM((2 * chans, model), BF16),
            pltpu.VMEM(w_bcdt.shape[::-1], BF16),
            pltpu.VMEM((chans, model), BF16),
            pltpu.VMEM((per, tp_heads * dim, state_n), BF16),
            pltpu.VMEM((blocks, chans, state_n), BF16),
            pltpu.VMEM((blocks, chans, state_n), BF16),
            pltpu.VMEM((plane, rows, feats), BF16),
            pltpu.VMEM((n_ctx, rows, feats), BF16),
            pltpu.VMEM((n_tp, n_ctx, rows, feats), BF16),
            pltpu.VMEM((plane, per, tp_heads), F32),
            pltpu.VMEM((per, tp_heads), F32),
            pltpu.VMEM((per, tp_heads), F32),
            pltpu.VMEM((n_dp,) + x_tail.shape, BF16),
            pltpu.VMEM((n_dp,) + bc_planes.shape, BF16),
            pltpu.VMEM((rows, 128), F32),
            pltpu.VMEM((ring, rows, 128), F32),
            pltpu.VMEM((1, 128), F32),
            pltpu.VMEM((ring, 1, 128), F32),
            pltpu.VMEM((ring, rows, feats), BF16),
            pltpu.VMEM((ring, rows, feats), BF16),
            pltpu.VMEM((per, chans, state_n), F32),
            pltpu.VMEM((full_rows, chans), F32),
            pltpu.VMEM((full_rows, wide), F32),
            pltpu.VMEM((rows, chans), F32),
            sem((5,)),
            sem((len(smalls),)),
            sem((4,)),
            sem((blocks + 1,)),
            *[sem((2,))] * 10,
        ],
        compiler_params=pltpu.CompilerParams(
            collective_id=0, has_side_effects=True, vmem_limit_bytes=56 * 1024 * 1024
        ),
        name="mixer",
    )(
        decode_prompt,
        pltpu.with_memory_space_constraint(part, pltpu.VMEM),
        seg_rate,
        x_tail,
        bc_planes,
        *smalls,
        w_zx.reshape(2 * chans, model),
        w_bcdt.T,
        w_out.reshape(chans, model),
        state_parts.reshape(per, tp_heads * dim, state_n),
    )
    mixed, final = pl.pallas_call(
        tail_kernel,
        out_shape=(
            jax.ShapeDtypeStruct(mixed.shape, BF16),
            jax.ShapeDtypeStruct(final.shape, F32),
        ),
        in_specs=[anywhere] * 2,
        out_specs=(anywhere, anywhere),
        scratch_shapes=[sem((2,))],
        name="tail",
    )(
        pltpu.with_memory_space_constraint(mixed, pltpu.VMEM),
        pltpu.with_memory_space_constraint(final, pltpu.VMEM),
    )
    return mixed, final.reshape(per, heads, dim, state_n)


def choose_device(sizes, *args):
    embedding, w_zx, w_bcdt = args[2], args[4], args[5]
    heads, dim = w_zx.shape[1:3]
    fits = (
        embedding.shape[1] % 128 == 0
        and sizes[0] % 2 == 0
        and (heads * dim) % 128 == 0
        and w_bcdt.shape[1] <= 128
        and embedding.shape[0] >= ROW_TILE
    )
    if fits:
        return kernel_device(sizes, *args)
    return per_device(*args)


def solution(mesh):
    sizes = (mesh.shape["ctx"], mesh.shape["dp"], mesh.shape["tp"], HEADS)
    return jax.shard_map(
        functools.partial(choose_device, sizes),
        mesh=mesh,
        in_specs=(
            P(),
            P(),
            P("dp", ("ctx", "tp")),
            P(),
            P(None, ("tp", "ctx"), None, None),
            P(None, ("ctx", "tp")),
            P(None, ("tp", "ctx"), None),
            P(("tp", "ctx"), None),
            P(),
            P(),
            P(("tp", "ctx")),
            P(("tp", "ctx")),
            P(("tp", "ctx")),
            P(("tp", "ctx"), None),
            P(("tp", "ctx"), None, None),
            P("ctx", "dp", "tp", None, None),
            P("ctx", "dp", "tp"),
            P("dp", None, ("tp", "ctx"), None),
            P("dp", None, None),
        ),
        out_specs=(P(None, "dp", ("ctx", "tp")), P("dp", ("tp", "ctx"), None, None)),
        check_vma=False,
    )
```

```python
import functools

import jax
import jax.numpy as jnp
from jax import lax
from jax.experimental import pallas as pl
from jax.experimental.pallas import tpu as pltpu
from jax.sharding import PartitionSpec as P

HEADS = 128
HEAD_DIM = 64


epsilon = 1e-05


def entering(shard, axis, combine, identity):
    count, here = (lax.axis_size(axis), lax.axis_index(axis))
    everything = lax.all_gather(shard, axis)
    start = jnp.broadcast_to(jnp.asarray(identity, shard.dtype), shard.shape)

    def step(k, before):
        at = count - 1 - k
        reached = at > here
        new = combine(before, everything[at])
        return jnp.where(reached, new, before)

    return lax.fori_loop(0, count, step, start)


def rms_scale(values, gain):
    return values * lax.rsqrt(jnp.mean(values * values, axis=-1, keepdims=True) + epsilon) * gain


def select_rows(picker, values):
    return jnp.tensordot(picker, values, axes=1, precision=lax.Precision.HIGHEST)


def add_rates(earlier, later_one):
    return earlier + later_one


def per_device(
    token_ids,
    decode_prompt,
    embedding,
    norm_gain,
    w_zx,
    w_bcdt,
    conv_x_weight,
    conv_x_bias,
    conv_bc_weight,
    conv_bc_bias,
    dt_bias,
    a_log,
    d_skip,
    gate_norm_gain,
    w_out,
    state_parts,
    seg_rate,
    x_tail,
    bc_tail,
):
    group = lax.axis_index("dp")
    local_count = state_parts.shape[1]
    slot_count = decode_prompt.shape[0]
    head_count = w_zx.shape[1]
    state_width = conv_bc_bias.shape[0] // 2
    after_rates = entering(seg_rate, "ctx", add_rates, jnp.zeros_like(seg_rate))
    seg_weight = jnp.exp(-after_rates[0])
    scaled = seg_weight[:, :, None, None] * state_parts[0].astype(jnp.float32)
    channel_sums = lax.psum_scatter(
        scaled.astype(jnp.bfloat16), "ctx", scatter_dimension=2, tiled=True
    ).astype(jnp.float32)
    combined = lax.all_to_all(
        channel_sums.astype(jnp.bfloat16), "ctx", split_axis=1, concat_axis=2, tiled=True
    ).astype(channel_sums.dtype)
    tails_x = x_tail.astype(jnp.float32)
    tails_bc = bc_tail.astype(jnp.float32)
    own_slots = lax.dynamic_slice_in_dim(decode_prompt, group * local_count, local_count)
    prompt_ids = jnp.arange(slot_count, dtype=jnp.int32)
    every_state, every_x, every_bc = (
        lax.all_gather(combined.astype(jnp.bfloat16), "dp", axis=0, tiled=True).astype(
            combined.dtype
        ),
        lax.all_gather(tails_x.astype(jnp.bfloat16), "dp", axis=0, tiled=True).astype(
            tails_x.dtype
        ),
        lax.all_gather(tails_bc.astype(jnp.bfloat16), "dp", axis=0, tiled=True).astype(
            tails_bc.dtype
        ),
    )
    picker = (own_slots[:, None] == prompt_ids[None, :]).astype(jnp.float32)
    ssm_state = select_rows(picker, every_state)
    x_window = select_rows(picker, every_x)
    bc_window = select_rows(picker, every_bc)
    vocab_rows = embedding.shape[0]
    holder = (decode_prompt[:, None] == prompt_ids[None, :]).astype(jnp.int32)
    slot_tokens = jnp.sum(token_ids[:, None, :] * holder[None], axis=2)
    offset_tokens = slot_tokens - group * vocab_rows
    inside = (offset_tokens >= 0) & (offset_tokens < vocab_rows)
    looked = jnp.take(embedding, jnp.clip(offset_tokens, 0, vocab_rows - 1), axis=0)
    partial_rows = jnp.where(inside[..., None], looked.astype(jnp.float32), 0.0)
    own_rows = lax.psum_scatter(
        partial_rows.astype(jnp.bfloat16), "dp", scatter_dimension=1, tiled=True
    )
    embedded = lax.all_gather(own_rows, ("ctx", "tp"), axis=2, tiled=True)
    steps_count = embedded.shape[0]
    flat_rows = embedded.reshape(-1, embedded.shape[2]).astype(jnp.float32)
    normed = rms_scale(flat_rows, norm_gain).astype(jnp.bfloat16)
    projected = jnp.einsum("rd,khed->krhe", normed, w_zx, preferred_element_type=jnp.float32)
    projected = projected.reshape(
        2, steps_count, local_count, projected.shape[2], projected.shape[3]
    )
    columns = lax.all_gather(
        jnp.dot(normed, w_bcdt, preferred_element_type=jnp.float32),
        ("ctx", "tp"),
        axis=1,
        tiled=True,
    )
    columns = columns.reshape(steps_count, local_count, -1)
    head_block = lax.axis_index("tp") * lax.axis_size("ctx") + lax.axis_index("ctx")
    head_start = 2 * state_width + head_block * head_count
    dt_raw = lax.dynamic_slice_in_dim(columns, head_start, head_count, 2)
    decay_rate = -jnp.exp(a_log)
    gated_steps = []
    for moment in range(steps_count):
        x_window = jnp.concatenate([x_window, projected[1, moment][:, None]], axis=1)
        bc_window = jnp.concatenate(
            [bc_window, columns[moment, :, None, : 2 * state_width]], axis=1
        )
        x_conv = jax.nn.silu(jnp.einsum("pkhe,khe->phe", x_window, conv_x_weight) + conv_x_bias)
        bc_conv = jax.nn.silu(jnp.einsum("pkn,kn->pn", bc_window, conv_bc_weight) + conv_bc_bias)
        step_size = jax.nn.softplus(dt_raw[moment] + dt_bias)
        retain = jnp.exp(step_size * decay_rate)
        ssm_state = (
            retain[:, :, None, None] * ssm_state
            + (step_size[:, :, None] * x_conv)[:, :, :, None] * bc_conv[:, None, None, :state_width]
        )
        output = (
            jnp.einsum("phen,pn->phe", ssm_state, bc_conv[:, state_width:])
            + d_skip[None, :, None] * x_conv
        )
        gated_steps.append(output * jax.nn.silu(projected[0, moment]))
        x_window = x_window[:, 1:]
        bc_window = bc_window[:, 1:]
    gated_all = jnp.stack(gated_steps)
    local_squares = jnp.sum(gated_all * gated_all, axis=(2, 3))
    total_squares = lax.psum(local_squares, ("ctx", "tp"))
    inverse = lax.rsqrt(total_squares / (HEADS * HEAD_DIM) + epsilon)
    normed_out = (gated_all * inverse[:, :, None, None] * gate_norm_gain).astype(jnp.bfloat16)
    partial_out = jnp.einsum("tphe,hed->tpd", normed_out, w_out, preferred_element_type=jnp.float32)
    outer_sum = lax.psum_scatter(
        partial_out.astype(jnp.bfloat16), "ctx", scatter_dimension=2, tiled=True
    ).astype(jnp.float32)
    mixed = lax.psum_scatter(outer_sum, "tp", scatter_dimension=2, tiled=True)
    return (mixed.astype(jnp.bfloat16), ssm_state)


HI = lax.Precision.HIGHEST
F32 = jnp.float32
BF16 = jnp.bfloat16


def f32_dot(a, b):
    return jnp.dot(a, b, precision=HI, preferred_element_type=F32)


def nt_dot(a, b):
    return lax.dot_general(a, b, (((1,), (1,)), ((), ())), preferred_element_type=F32)


def silu(v):
    return v / (1.0 + jnp.exp(-v))


def softplus(v):
    return jnp.maximum(v, 0.0) + jnp.log1p(jnp.exp(-jnp.abs(v)))


ROW_TILE = 8


def drain(ref, sem):
    pltpu.make_async_copy(ref, ref, sem).wait()


def gather_kernel(steps, slots, groups, tok_ref, dec_ref, emb_ref, out_ref, buf, tail, sem, tail_sem):
    vocab = emb_ref.shape[0]
    whole = vocab // ROW_TILE * ROW_TILE
    base = lax.axis_index("dp") * vocab
    per_group = slots // groups
    tail_copy = None
    if whole < vocab:
        tail_copy = pltpu.make_async_copy(emb_ref.at[pl.ds(whole, vocab - whole)], tail, tail_sem)
        tail_copy.start()
    where = []
    for s in range(slots):
        q = dec_ref[s]
        for t in range(steps):
            row = tok_ref[t, q] - base
            clipped = jnp.clip(row, 0, vocab - 1)
            start = jnp.minimum(clipped // ROW_TILE * ROW_TILE, whole - ROW_TILE)
            start = pl.multiple_of(start, ROW_TILE)
            i = s * steps + t
            pltpu.make_async_copy(emb_ref.at[pl.ds(start, ROW_TILE)], buf.at[i], sem).start()
            where.append((row, start))
    if tail_copy is not None:
        tail_copy.wait()
    drain(buf, sem)
    rows = lax.broadcasted_iota(jnp.int32, (ROW_TILE, 1), 0)
    for g in range(groups):
        picked = []
        for t in range(steps):
            for j in range(per_group):
                i = (g * per_group + j) * steps + t
                row, start = where[i]
                value = jnp.sum(
                    jnp.where(rows == row - start, buf[i].astype(F32), 0.0), axis=0, keepdims=True
                )
                if tail_copy is not None:
                    trows = lax.broadcasted_iota(jnp.int32, (vocab - whole, 1), 0)
                    value += jnp.sum(
                        jnp.where(trows == row - whole, tail[...].astype(F32), 0.0),
                        axis=0,
                        keepdims=True,
                    )
                picked.append(value)
        out_ref[g] = jnp.concatenate(picked, axis=0).astype(BF16)


def mixer_kernel(
    sizes,
    dec_hbm,
    part_ref,
    seg_hbm,
    xt_hbm,
    bt_hbm,
    gain_hbm,
    cxw_hbm,
    cxb_hbm,
    cbw_hbm,
    cbb_hbm,
    dtb_hbm,
    alog_hbm,
    skip_hbm,
    gg_hbm,
    wzx_hbm,
    wbc_hbm,
    wout_hbm,
    state_hbm,
    mixed_ref,
    final_ref,
    dec_ref,
    gain_ref,
    cxw_ref,
    cxb_ref,
    cbw_ref,
    cbb_ref,
    dtb_ref,
    alog_ref,
    skip_ref,
    gg_ref,
    pair_recv,
    pair_send,
    wzx,
    wbc,
    wout,
    state_in,
    state_send,
    state_recv,
    plane_recv,
    line_send,
    line_recv,
    seg_recv,
    seg_mate,
    seg_own,
    xt_recv,
    bt_recv,
    col_send,
    col_recv,
    sq_send,
    sq_recv,
    out_send,
    out_recv,
    start_state,
    start_low,
    xfull,
    bcfull,
    load_sems,
    small_sems,
    own_sems,
    pair_sems,
    mate_sem,
    state_sem,
    plane_sem,
    line_sem,
    seg_sem,
    xt_sem,
    bt_sem,
    col_sem,
    sq_sem,
    out_sem,
    done,
    ready,
):
    n_ctx, n_dp, n_tp, total_heads = sizes
    c, d, p = lax.axis_index("ctx"), lax.axis_index("dp"), lax.axis_index("tp")
    mine = c * n_tp + p
    here_plane = d * n_ctx + c
    ring, plane = n_ctx * n_tp, n_dp * n_ctx
    steps, per, feats = mixed_ref.shape
    rows = steps * per
    heads, dim = cxb_ref.shape
    chans = heads * dim
    width = cbb_ref.shape[1]
    state_n = width // 2
    taps = cxw_ref.shape[0]
    model = gain_ref.shape[1]
    tp_heads = seg_recv.shape[-1]
    n_cols = wbc_hbm.shape[0]
    all_cols = n_cols * n_ctx * n_tp
    half = wzx_hbm.shape[0] // 2
    mirror = n_tp == 4

    def peer(offset):
        dc, dd, dt = offset
        away = lax.rem(p + dt, n_tp)
        if mirror and dt != n_tp // 2:
            away = n_tp - 1 - (p if dt == 1 else lax.rem(p + n_tp // 2, n_tp))
        return lax.rem(c + dc, n_ctx), lax.rem(d + dd, n_dp), away if dt else p

    def device(offset):
        a, b, e = peer(offset)
        return {"ctx": a, "dp": b, "tp": e}

    def along(k):
        return {"ctx": c, "dp": d, "tp": lax.rem(p + k + n_tp, n_tp)}

    far = [1, 2, 3] if mirror else list(range(n_tp - 1, 0, -1))
    routed = [(a, b, 0) for a in reversed(range(n_ctx)) for b in reversed(range(n_dp)) if a + b]
    group = [(a, 0, e) for e in far + [0] for a in reversed(range(n_ctx)) if a + e]
    across = [(0, b, 0) for b in range(1, n_dp)]

    barrier = pltpu.get_barrier_semaphore()
    for o in routed:
        pl.semaphore_signal(
            barrier, inc=1, device_id=device(o), device_id_type=pl.DeviceIdType.MESH
        )
    for k in range(1, n_tp):

        @pl.when(p + k < n_tp)
        def _():
            pl.semaphore_signal(
                barrier, inc=1, device_id=along(k), device_id_type=pl.DeviceIdType.MESH
            )


    owns = []
    for source, target in (
        (dec_hbm, dec_ref),
        (seg_hbm.at[0], seg_own),
        (xt_hbm, xt_recv.at[d]),
        (bt_hbm, bt_recv.at[d]),
    ):
        load = pltpu.make_async_copy(source, target, own_sems.at[len(owns)])
        load.start()
        owns.append(load)
    loads = []
    smalls = []
    pairs = (
        (state_hbm, state_in),
        (wbc_hbm, wbc),
        (wzx_hbm.at[pl.ds(half, half)], wzx.at[pl.ds(half, half)]),
        (wzx_hbm.at[pl.ds(0, half)], wzx.at[pl.ds(0, half)]),
        (wout_hbm, wout),
    )
    small_pairs = (
        (gain_hbm, gain_ref),
        (cxw_hbm, cxw_ref),
        (cxb_hbm, cxb_ref),
        (cbw_hbm, cbw_ref),
        (cbb_hbm, cbb_ref),
        (dtb_hbm, dtb_ref),
        (alog_hbm, alog_ref),
        (skip_hbm, skip_ref),
        (gg_hbm, gg_ref),
    )

    def fetch(source, target, sem, into):
        load = pltpu.make_async_copy(source, target, sem)
        load.start()
        into.append(load)

    fetch(*pairs[0], load_sems.at[0], loads)
    for i, pair in enumerate(small_pairs):
        fetch(*pair, small_sems.at[i], smalls)
    def send(source, target, send_sem, recv_sem, place):
        pltpu.make_async_remote_copy(
            src_ref=source,
            dst_ref=target,
            send_sem=send_sem,
            recv_sem=recv_sem,
            device_id=place,
            device_id_type=pl.DeviceIdType.MESH,
        ).start()

    pl.semaphore_wait(barrier, len(routed) + p)
    for k in range(1, n_tp):

        @pl.when(p >= k)
        def _():
            pl.semaphore_signal(
                ready, inc=1, device_id=along(-k), device_id_type=pl.DeviceIdType.MESH
            )


    for o in routed:
        send(part_ref.at[peer(o)[1]], plane_recv.at[here_plane], done, plane_sem, device(o))
    plane_recv[here_plane] = part_ref[d]

    owns[0].wait()
    owns[1].wait()
    parity = lax.rem(c, 2)
    mate = {"ctx": c + 1 - 2 * parity, "dp": d, "tp": p}
    half_ctx = n_ctx // 2
    blocks = [(a, b) for a in reversed(range(half_ctx)) for b in reversed(range(n_dp))]
    seg_recv[here_plane] = seg_own[...]
    send(seg_own, seg_mate, done, mate_sem, mate)
    for o in routed:
        send(seg_own, seg_recv.at[here_plane], done, seg_sem, device(o))
    owns[2].wait()
    owns[3].wait()
    for o in across:
        send(xt_recv.at[d], xt_recv.at[d], done, xt_sem, device(o))
        send(bt_recv.at[d], bt_recv.at[d], done, bt_sem, device(o))
    picks = []
    for b in range(n_dp):
        target_group = lax.rem(d + b, n_dp)
        pick = jnp.int32(0)
        for j in range(per):
            local = dec_ref[target_group * per + j] - d * per
            pick += jnp.where((local >= 0) & (local < per), local, 0)
        picks.append(pick)
    loads[0].wait()
    for slot, (a, b) in enumerate(blocks):
        first = pl.multiple_of(lax.rem(mate["ctx"] + 2 * a, n_ctx) * chans, chans)
        state_send[slot] = state_in[picks[b], pl.ds(first, chans), :]
        send(state_send.at[slot], pair_recv.at[slot], done, pair_sems.at[slot], mate)

    for i, pair in enumerate(pairs[1:]):
        fetch(*pair, load_sems.at[i + 1], loads)

    fold = (
        lax.broadcasted_iota(jnp.int32, (dim, chans), 0)
        == lax.rem(lax.broadcasted_iota(jnp.int32, (dim, chans), 1), dim)
    ).astype(F32)
    head_rows = lax.broadcasted_iota(jnp.int32, (heads, chans), 0) == lax.div(
        lax.broadcasted_iota(jnp.int32, (heads, chans), 1), dim
    )

    def flat(value):
        return jnp.sum(jnp.where(head_rows, f32_dot(value, fold), 0.0), axis=0, keepdims=True)

    def spread(value, first):
        count = value.shape[1]
        chosen = (
            lax.broadcasted_iota(jnp.int32, (count, chans), 0)
            == first + lax.div(lax.broadcasted_iota(jnp.int32, (count, chans), 1), dim)
        ).astype(F32)
        return f32_dot(value, chosen)

    drain(seg_mate, mate_sem)
    shrink = []
    for b in range(n_dp):
        row = pl.ds(picks[b], 1)
        shrink.append(jnp.exp(-jnp.where(parity == 0, seg_mate[row, :], seg_own[row, :])))
    ones = [jnp.ones((1, tp_heads), F32)] * n_dp
    shrink = jnp.concatenate(shrink + ones, axis=0)
    shrink_cols = [
        jnp.transpose(spread(shrink, lax.rem(c + 2 * a, n_ctx) * heads)) for a in range(half_ctx)
    ]
    for slot, (a, b) in enumerate(blocks):
        drain(pair_recv.at[slot], pair_sems.at[slot])
        first = pl.multiple_of(lax.rem(c + 2 * a, n_ctx) * chans, chans)
        here = state_in[picks[b], pl.ds(first, chans), :].astype(F32)
        there = pair_recv[slot].astype(F32)
        factor = shrink_cols[a][:, b : b + 1]
        even = jnp.where(parity == 0, here, there)
        odd = jnp.where(parity == 0, there, here)
        added = (factor * even + odd).astype(BF16)
        target = state_recv.at[d * half_ctx + lax.div(c, 2)]
        if a + b:
            pair_send[slot] = added
            send(pair_send.at[slot], target, done, state_sem, device((2 * a, b, 0)))
        else:
            state_recv[d * half_ctx + lax.div(c, 2)] = added

    drain(plane_recv.at[pl.ds(0, plane - 1)], plane_sem)
    for i in range(n_ctx):
        piece = plane_recv[i].astype(F32)
        for g in range(1, n_dp):
            piece += plane_recv[g * n_ctx + i].astype(F32)
        line_send[i] = piece.astype(BF16)
    for k in range(n_tp - 1, 0, -1):

        @pl.when(p >= k)
        def _():
            send(line_send, line_recv.at[p], done, line_sem, along(-k))

    @pl.when(p < n_tp - 1)
    def _():
        pl.semaphore_wait(ready, n_tp - 1 - p)

    for k in range(n_tp - 1, 0, -1):

        @pl.when(p + k < n_tp)
        def _():
            send(line_send, line_recv.at[p], done, line_sem, along(k))

    line_recv[p] = line_send[...]


    for load in smalls:
        load.wait()
    tap_rows = [flat(cxw_ref[k]) for k in range(taps)]
    bias_row = flat(cxb_ref[...])
    gate_row = flat(gg_ref[...])
    idle = jnp.zeros((1, total_heads - heads), F32)
    dtb_row = jnp.concatenate([dtb_ref[...], idle], axis=1)
    rate_row = jnp.concatenate([-jnp.exp(alog_ref[...]), idle], axis=1)
    skip_row = jnp.concatenate([skip_ref[...], idle], axis=1)

    holders = [lax.div(dec_ref[d * per + j], per) for j in range(per)]
    places = [lax.rem(dec_ref[d * per + j], per) for j in range(per)]
    for one, ref in ((xt_sem, xt_recv), (bt_sem, bt_recv)):
        if across:
            drain(ref.at[pl.ds(0, n_dp - 1)], one)
    plane_rows = lax.broadcasted_iota(jnp.int32, (per, 1), 0)
    for k in range(taps - 1):
        for j in range(per):
            r = k * per + j
            xfull[r : r + 1, :] = flat(xt_recv[holders[j], places[j], k].astype(F32))
            tail = bt_recv[holders[j], k].astype(F32)
            bcfull[r : r + 1, :] = jnp.sum(
                jnp.where(plane_rows == places[j], tail, 0.0), axis=0, keepdims=True
            )

    drain(seg_recv.at[pl.ds(0, plane - 1)], seg_sem)
    weights = []
    for j in range(per):
        after = jnp.zeros((1, tp_heads), F32)
        ordered = []
        row = pl.ds(places[j], 1)
        for m in reversed(range(half_ctx)):
            ordered.append(jnp.exp(-after))
            for k in (2 * m + 1, 2 * m):
                after = after + seg_recv[holders[j] * n_ctx + k, row, :]
        weights.extend(reversed(ordered))
    weight_cols = jnp.transpose(spread(jnp.concatenate(weights, axis=0), c * heads))

    drain(line_recv.at[pl.ds(0, n_tp - 1)], line_sem)
    pieces = [line_recv[e, i].astype(F32) for i in range(n_ctx) for e in range(n_tp)]
    embedded = jnp.concatenate(pieces, axis=1)
    scale = lax.rsqrt(jnp.sum(embedded * embedded, axis=1, keepdims=True) / model + epsilon)
    normed = (embedded * gain_ref[...]).astype(BF16)
    loads[1].wait()
    narrow = nt_dot(normed, wbc[...]) * scale
    padded = jnp.concatenate([narrow, jnp.zeros((rows, 128 - n_cols), F32)], axis=1)
    col_send[...] = pltpu.roll(padded, lax.rem(n_cols * mine, 128), 1)
    for o in group:
        send(col_send, col_recv.at[mine], done, col_sem, device(o))
    col_recv[mine] = col_send[...]
    loads[2].wait()
    x_rows = nt_dot(normed, wzx[half : 2 * half, :]) * scale
    loads[3].wait()
    z_gate = silu(nt_dot(normed, wzx[0:half, :]) * scale)

    lead = (taps - 1) * per
    xfull[lead : lead + rows, :] = x_rows
    conv = bias_row
    for k in range(taps):
        conv = conv + tap_rows[k] * xfull[k * per : k * per + rows, :]
    xc = silu(conv)

    drain(state_recv.at[pl.ds(0, n_dp * half_ctx - 1)], state_sem)
    for j in range(per):
        begin = None
        for m in range(half_ctx):
            r = j * half_ctx + m
            term = weight_cols[:, r : r + 1] * state_recv[holders[j] * half_ctx + m].astype(F32)
            begin = term if begin is None else begin + term
        start_state[j] = begin
        start_low[j] = begin.astype(BF16)

    drain(col_recv.at[pl.ds(0, ring - 1)], col_sem)
    lanes = lax.broadcasted_iota(jnp.int32, (rows, 128), 1)
    blocks_of = []
    for v in range(-(-all_cols // 128)):
        block = jnp.zeros((rows, 128), F32)
        for i in range(ring):
            low = n_cols * i - 128 * v
            if low < 128 and low + n_cols > 0:
                block = jnp.where((lanes >= low) & (lanes < low + n_cols), col_recv[i], block)
        blocks_of.append(block)
    columns = jnp.concatenate(blocks_of, axis=1)
    bcfull[lead : lead + rows, :] = columns[:, :width]
    head_first = (p * n_ctx + c) * heads
    dt_raw = pltpu.roll(columns[:, width:all_cols], total_heads - head_first, 1)
    step_size = softplus(dt_raw + dtb_row)
    row_of = lax.broadcasted_iota(jnp.int32, (rows, 1), 0)

    def later(value, k):
        return pltpu.roll(value, k * per, 0) if k else value

    total = step_size * rate_row
    k = 1
    while k < steps:
        total = total + jnp.where(row_of >= k * per, later(total, k), 0.0)
        k *= 2
    conv = cbb_ref[...]
    for k in range(taps):
        conv = conv + cbw_ref[k : k + 1, :] * bcfull[k * per : k * per + rows, :]
    bcc = silu(conv)
    b_all, c_all = bcc[:, :state_n], bcc[:, state_n:]

    row_slot = lax.rem(row_of, per)
    from_start = jnp.zeros((rows, chans), F32)
    c_low = c_all.astype(BF16)
    for j in range(per):
        from_start += jnp.where(row_slot == j, nt_dot(c_low, start_low[j]), 0.0)

    def by_head(value):
        if 128 % dim or chans % 128:
            return spread(value, 0)
        packed = 128 // dim
        out = []
        for m in range(chans // 128):
            part = jnp.broadcast_to(value[:, m * packed : m * packed + 1], (rows, 128))
            for q in range(1, packed):
                one = value[:, m * packed + q : m * packed + q + 1]
                part = jnp.where(lanes >= q * dim, one, part)
            out.append(part)
        return jnp.concatenate(out, axis=1)

    def at(value, t):
        return value[t * per : (t + 1) * per]

    y = by_head(jnp.exp(total)) * from_start
    for k in range(steps):
        overlap = jnp.sum(later(b_all, k) * c_all, axis=1, keepdims=True)
        if k:
            valid = row_of >= k * per
            decay = jnp.exp(jnp.where(valid, total - later(total, k), 0.0))
            share = jnp.where(valid, decay * overlap * later(step_size, k), 0.0)
        else:
            share = step_size * overlap + skip_row
        y = y + by_head(share) * later(xc, k)
    gated = y * z_gate
    diagonal = lax.broadcasted_iota(jnp.int32, (rows, 128), 0) == lax.broadcasted_iota(
        jnp.int32, (rows, 128), 1
    )
    loads[4].wait()
    scaled = (gated * gate_row).astype(BF16)
    for e in far + [0]:
        there = peer((0, 0, e))[2]
        cuts = [
            wout[:, pl.ds(pl.multiple_of((a * n_tp + there) * feats, feats), feats)]
            for a in range(n_ctx)
        ]
        partial = jnp.dot(scaled, jnp.concatenate(cuts, axis=1), preferred_element_type=F32)
        for a in range(n_ctx):
            out_send[e * n_ctx + a] = partial[:, a * feats : (a + 1) * feats].astype(BF16)
        for a in reversed(range(n_ctx)):
            if a + e:
                o = (a, 0, e)
                spot = e * n_ctx + peer(o)[0]
                send(out_send.at[spot], out_recv.at[mine], done, out_sem, device(o))
        if e == far[0]:
            squares = jnp.sum(gated * gated, axis=1, keepdims=True)
            sq_send[...] = jnp.sum(jnp.where(diagonal, squares, 0.0), axis=0, keepdims=True)
            for o in group:
                send(sq_send, sq_recv.at[mine], done, sq_sem, device(o))
            sq_recv[mine] = sq_send[...]
    out_recv[mine] = out_send[c]

    last = jnp.concatenate([at(total, steps - 1)] * steps, axis=0)
    late = by_head(jnp.exp(last - total) * step_size) * xc
    flat_rows = jnp.concatenate([late, by_head(jnp.exp(last))], axis=0)
    tall = jnp.transpose(flat_rows)
    for j in range(per):
        b_own = jnp.where(row_slot == j, b_all, 0.0)
        final_ref[j] = (
            tall[:, rows + j : rows + j + 1] * start_state[j] + f32_dot(tall[:, :rows], b_own)
        )

    drain(plane_recv.at[pl.ds(0, plane - 1)], done)
    drain(line_recv.at[pl.ds(0, n_tp - 1)], done)
    drain(seg_recv.at[pl.ds(0, plane - 1)], done)
    drain(seg_mate, done)
    drain(state_send, done)
    drain(pair_send.at[pl.ds(0, len(blocks) - 1)], done)
    if across:
        drain(xt_recv.at[pl.ds(0, n_dp - 1)], done)
        drain(bt_recv.at[pl.ds(0, n_dp - 1)], done)
    drain(col_recv.at[pl.ds(0, ring - 1)], done)
    drain(sq_recv.at[pl.ds(0, ring - 1)], done)
    drain(out_recv.at[pl.ds(0, ring - 1)], done)

    drain(sq_recv.at[pl.ds(0, ring - 1)], sq_sem)
    total_squares = sq_recv[0]
    for i in range(1, ring):
        total_squares = total_squares + sq_recv[i]
    total_squares = jnp.sum(jnp.where(diagonal, total_squares, 0.0), axis=1, keepdims=True)
    inverse = lax.rsqrt(total_squares / (total_heads * dim) + epsilon)
    drain(out_recv.at[pl.ds(0, ring - 1)], out_sem)
    mixed = out_recv[0].astype(F32)
    for i in range(1, ring):
        mixed = mixed + out_recv[i].astype(F32)
    mixed = mixed * inverse
    for t in range(steps):
        mixed_ref[t] = at(mixed, t).astype(BF16)


def tail_kernel(mixed_in, final_in, mixed_out, final_out, sems):
    copies = [
        pltpu.make_async_copy(final_in.at[j], final_out.at[j], sems.at[j])
        for j in range(final_in.shape[0])
    ]
    copies.append(pltpu.make_async_copy(mixed_in, mixed_out, sems.at[len(copies)]))
    for copy in copies:
        copy.start()
    for copy in copies:
        copy.wait()


def kernel_device(
    sizes,
    token_ids,
    decode_prompt,
    embedding,
    norm_gain,
    w_zx,
    w_bcdt,
    conv_x_weight,
    conv_x_bias,
    conv_bc_weight,
    conv_bc_bias,
    dt_bias,
    a_log,
    d_skip,
    gate_norm_gain,
    w_out,
    state_parts,
    seg_rate,
    x_tail,
    bc_tail,
):
    n_ctx, n_dp, n_tp, _ = sizes
    steps = token_ids.shape[0]
    slots = decode_prompt.shape[0]
    per = state_parts.shape[1]
    rows = steps * per
    vocab, feats = embedding.shape
    heads, dim, model = w_zx.shape[1:]
    chans = heads * dim
    tp_heads, state_n = state_parts.shape[2], state_parts.shape[4]
    ring, plane, blocks = n_ctx * n_tp, n_dp * n_ctx, n_dp * (n_ctx // 2)
    smem = pl.BlockSpec(memory_space=pltpu.SMEM)
    vmem = pl.BlockSpec(memory_space=pltpu.VMEM)
    anywhere = pl.BlockSpec(memory_space=pl.ANY)
    sem = pltpu.SemaphoreType.DMA
    rest = max(1, vocab % ROW_TILE)
    part = pl.pallas_call(
        functools.partial(gather_kernel, steps, slots, n_dp),
        out_shape=pltpu.VMEM((n_dp, rows, feats), BF16),
        in_specs=[smem, smem, anywhere],
        out_specs=vmem,
        scratch_shapes=[
            pltpu.VMEM((steps * slots, ROW_TILE, feats), BF16),
            pltpu.VMEM((rest, feats), BF16),
            sem,
            sem,
        ],
        name="gather_rows",
    )(token_ids, decode_prompt, embedding)
    wide = 2 * state_n
    full_rows = -(-(conv_x_weight.shape[0] - 1 + steps) * per // 8) * 8
    smalls = (
        norm_gain[None],
        conv_x_weight,
        conv_x_bias,
        conv_bc_weight,
        conv_bc_bias[None],
        dt_bias[None],
        a_log[None],
        d_skip[None],
        gate_norm_gain,
    )
    bc_planes = jnp.swapaxes(bc_tail, 0, 1)
    mixed, final = pl.pallas_call(
        functools.partial(mixer_kernel, sizes),
        out_shape=(
            pltpu.VMEM((steps, per, feats), BF16),
            pltpu.VMEM((per, chans, state_n), F32),
        ),
        in_specs=[anywhere, vmem] + [anywhere] * 16,
        out_specs=(vmem, vmem),
        scratch_shapes=[
            pltpu.SMEM((slots,), jnp.int32),
            *[pltpu.VMEM(small.shape, small.dtype) for small in smalls],
            pltpu.VMEM((blocks, chans, state_n), BF16),
            pltpu.VMEM((blocks, chans, state_n), BF16),
            pltpu.VMEM((2 * chans, model), BF16),
            pltpu.VMEM(w_bcdt.shape[::-1], BF16),
            pltpu.VMEM((chans, model), BF16),
            pltpu.VMEM((per, tp_heads * dim, state_n), BF16),
            pltpu.VMEM((blocks, chans, state_n), BF16),
            pltpu.VMEM((blocks, chans, state_n), BF16),
            pltpu.VMEM((plane, rows, feats), BF16),
            pltpu.VMEM((n_ctx, rows, feats), BF16),
            pltpu.VMEM((n_tp, n_ctx, rows, feats), BF16),
            pltpu.VMEM((plane, per, tp_heads), F32),
            pltpu.VMEM((per, tp_heads), F32),
            pltpu.VMEM((per, tp_heads), F32),
            pltpu.VMEM((n_dp,) + x_tail.shape, BF16),
            pltpu.VMEM((n_dp,) + bc_planes.shape, BF16),
            pltpu.VMEM((rows, 128), F32),
            pltpu.VMEM((ring, rows, 128), F32),
            pltpu.VMEM((1, 128), F32),
            pltpu.VMEM((ring, 1, 128), F32),
            pltpu.VMEM((ring, rows, feats), BF16),
            pltpu.VMEM((ring, rows, feats), BF16),
            pltpu.VMEM((per, chans, state_n), F32),
            pltpu.VMEM((per, chans, state_n), BF16),
            pltpu.VMEM((full_rows, chans), F32),
            pltpu.VMEM((full_rows, wide), F32),
            sem((5,)),
            sem((len(smalls),)),
            sem((4,)),
            sem((blocks,)),
            *[sem] * 11,
            pltpu.SemaphoreType.REGULAR,
        ],
        compiler_params=pltpu.CompilerParams(
            collective_id=0, has_side_effects=True, vmem_limit_bytes=56 * 1024 * 1024
        ),
        name="mixer",
    )(
        decode_prompt,
        pltpu.with_memory_space_constraint(part, pltpu.VMEM),
        seg_rate,
        x_tail,
        bc_planes,
        *smalls,
        w_zx.reshape(2 * chans, model),
        w_bcdt.T,
        w_out.reshape(chans, model),
        state_parts.reshape(per, tp_heads * dim, state_n),
    )
    mixed, final = pl.pallas_call(
        tail_kernel,
        out_shape=(
            jax.ShapeDtypeStruct(mixed.shape, BF16),
            jax.ShapeDtypeStruct(final.shape, F32),
        ),
        in_specs=[anywhere] * 2,
        out_specs=(anywhere, anywhere),
        scratch_shapes=[sem((per + 1,))],
        name="tail",
    )(
        pltpu.with_memory_space_constraint(mixed, pltpu.VMEM),
        pltpu.with_memory_space_constraint(final, pltpu.VMEM),
    )
    return mixed, final.reshape(per, heads, dim, state_n)


def choose_device(sizes, *args):
    embedding, w_zx, w_bcdt = args[2], args[4], args[5]
    heads, dim = w_zx.shape[1:3]
    fits = (
        embedding.shape[1] % 128 == 0
        and sizes[0] % 2 == 0
        and (heads * dim) % 128 == 0
        and w_bcdt.shape[1] <= 128
        and embedding.shape[0] >= ROW_TILE
    )
    if fits:
        return kernel_device(sizes, *args)
    return per_device(*args)


def solution(mesh):
    sizes = (mesh.shape["ctx"], mesh.shape["dp"], mesh.shape["tp"], HEADS)
    return jax.shard_map(
        functools.partial(choose_device, sizes),
        mesh=mesh,
        in_specs=(
            P(),
            P(),
            P("dp", ("ctx", "tp")),
            P(),
            P(None, ("tp", "ctx"), None, None),
            P(None, ("ctx", "tp")),
            P(None, ("tp", "ctx"), None),
            P(("tp", "ctx"), None),
            P(),
            P(),
            P(("tp", "ctx")),
            P(("tp", "ctx")),
            P(("tp", "ctx")),
            P(("tp", "ctx"), None),
            P(("tp", "ctx"), None, None),
            P("ctx", "dp", "tp", None, None),
            P("ctx", "dp", "tp"),
            P("dp", None, ("tp", "ctx"), None),
            P("dp", None, None),
        ),
        out_specs=(P(None, "dp", ("ctx", "tp")), P("dp", ("tp", "ctx"), None, None)),
        check_vma=False,
    )
```

```python
import functools

import jax
import jax.numpy as jnp
from jax import lax
from jax.experimental import pallas as pl
from jax.experimental.pallas import tpu as pltpu
from jax.sharding import PartitionSpec as P

HEADS = 128
HEAD_DIM = 64


epsilon = 1e-05


def entering(shard, axis, combine, identity):
    count, here = (lax.axis_size(axis), lax.axis_index(axis))
    everything = lax.all_gather(shard, axis)
    start = jnp.broadcast_to(jnp.asarray(identity, shard.dtype), shard.shape)

    def step(k, before):
        at = count - 1 - k
        reached = at > here
        new = combine(before, everything[at])
        return jnp.where(reached, new, before)

    return lax.fori_loop(0, count, step, start)


def rms_scale(values, gain):
    return values * lax.rsqrt(jnp.mean(values * values, axis=-1, keepdims=True) + epsilon) * gain


def select_rows(picker, values):
    return jnp.tensordot(picker, values, axes=1, precision=lax.Precision.HIGHEST)


def add_rates(earlier, later_one):
    return earlier + later_one


def per_device(
    token_ids,
    decode_prompt,
    embedding,
    norm_gain,
    w_zx,
    w_bcdt,
    conv_x_weight,
    conv_x_bias,
    conv_bc_weight,
    conv_bc_bias,
    dt_bias,
    a_log,
    d_skip,
    gate_norm_gain,
    w_out,
    state_parts,
    seg_rate,
    x_tail,
    bc_tail,
):
    group = lax.axis_index("dp")
    local_count = state_parts.shape[1]
    slot_count = decode_prompt.shape[0]
    head_count = w_zx.shape[1]
    state_width = conv_bc_bias.shape[0] // 2
    after_rates = entering(seg_rate, "ctx", add_rates, jnp.zeros_like(seg_rate))
    seg_weight = jnp.exp(-after_rates[0])
    scaled = seg_weight[:, :, None, None] * state_parts[0].astype(jnp.float32)
    channel_sums = lax.psum_scatter(
        scaled.astype(jnp.bfloat16), "ctx", scatter_dimension=2, tiled=True
    ).astype(jnp.float32)
    combined = lax.all_to_all(
        channel_sums.astype(jnp.bfloat16), "ctx", split_axis=1, concat_axis=2, tiled=True
    ).astype(channel_sums.dtype)
    tails_x = x_tail.astype(jnp.float32)
    tails_bc = bc_tail.astype(jnp.float32)
    own_slots = lax.dynamic_slice_in_dim(decode_prompt, group * local_count, local_count)
    prompt_ids = jnp.arange(slot_count, dtype=jnp.int32)
    every_state, every_x, every_bc = (
        lax.all_gather(combined.astype(jnp.bfloat16), "dp", axis=0, tiled=True).astype(
            combined.dtype
        ),
        lax.all_gather(tails_x.astype(jnp.bfloat16), "dp", axis=0, tiled=True).astype(
            tails_x.dtype
        ),
        lax.all_gather(tails_bc.astype(jnp.bfloat16), "dp", axis=0, tiled=True).astype(
            tails_bc.dtype
        ),
    )
    picker = (own_slots[:, None] == prompt_ids[None, :]).astype(jnp.float32)
    ssm_state = select_rows(picker, every_state)
    x_window = select_rows(picker, every_x)
    bc_window = select_rows(picker, every_bc)
    vocab_rows = embedding.shape[0]
    holder = (decode_prompt[:, None] == prompt_ids[None, :]).astype(jnp.int32)
    slot_tokens = jnp.sum(token_ids[:, None, :] * holder[None], axis=2)
    offset_tokens = slot_tokens - group * vocab_rows
    inside = (offset_tokens >= 0) & (offset_tokens < vocab_rows)
    looked = jnp.take(embedding, jnp.clip(offset_tokens, 0, vocab_rows - 1), axis=0)
    partial_rows = jnp.where(inside[..., None], looked.astype(jnp.float32), 0.0)
    own_rows = lax.psum_scatter(
        partial_rows.astype(jnp.bfloat16), "dp", scatter_dimension=1, tiled=True
    )
    embedded = lax.all_gather(own_rows, ("ctx", "tp"), axis=2, tiled=True)
    steps_count = embedded.shape[0]
    flat_rows = embedded.reshape(-1, embedded.shape[2]).astype(jnp.float32)
    normed = rms_scale(flat_rows, norm_gain).astype(jnp.bfloat16)
    projected = jnp.einsum("rd,khed->krhe", normed, w_zx, preferred_element_type=jnp.float32)
    projected = projected.reshape(
        2, steps_count, local_count, projected.shape[2], projected.shape[3]
    )
    columns = lax.all_gather(
        jnp.dot(normed, w_bcdt, preferred_element_type=jnp.float32),
        ("ctx", "tp"),
        axis=1,
        tiled=True,
    )
    columns = columns.reshape(steps_count, local_count, -1)
    head_block = lax.axis_index("tp") * lax.axis_size("ctx") + lax.axis_index("ctx")
    head_start = 2 * state_width + head_block * head_count
    dt_raw = lax.dynamic_slice_in_dim(columns, head_start, head_count, 2)
    decay_rate = -jnp.exp(a_log)
    gated_steps = []
    for moment in range(steps_count):
        x_window = jnp.concatenate([x_window, projected[1, moment][:, None]], axis=1)
        bc_window = jnp.concatenate(
            [bc_window, columns[moment, :, None, : 2 * state_width]], axis=1
        )
        x_conv = jax.nn.silu(jnp.einsum("pkhe,khe->phe", x_window, conv_x_weight) + conv_x_bias)
        bc_conv = jax.nn.silu(jnp.einsum("pkn,kn->pn", bc_window, conv_bc_weight) + conv_bc_bias)
        step_size = jax.nn.softplus(dt_raw[moment] + dt_bias)
        retain = jnp.exp(step_size * decay_rate)
        ssm_state = (
            retain[:, :, None, None] * ssm_state
            + (step_size[:, :, None] * x_conv)[:, :, :, None] * bc_conv[:, None, None, :state_width]
        )
        output = (
            jnp.einsum("phen,pn->phe", ssm_state, bc_conv[:, state_width:])
            + d_skip[None, :, None] * x_conv
        )
        gated_steps.append(output * jax.nn.silu(projected[0, moment]))
        x_window = x_window[:, 1:]
        bc_window = bc_window[:, 1:]
    gated_all = jnp.stack(gated_steps)
    local_squares = jnp.sum(gated_all * gated_all, axis=(2, 3))
    total_squares = lax.psum(local_squares, ("ctx", "tp"))
    inverse = lax.rsqrt(total_squares / (HEADS * HEAD_DIM) + epsilon)
    normed_out = (gated_all * inverse[:, :, None, None] * gate_norm_gain).astype(jnp.bfloat16)
    partial_out = jnp.einsum("tphe,hed->tpd", normed_out, w_out, preferred_element_type=jnp.float32)
    outer_sum = lax.psum_scatter(
        partial_out.astype(jnp.bfloat16), "ctx", scatter_dimension=2, tiled=True
    ).astype(jnp.float32)
    mixed = lax.psum_scatter(outer_sum, "tp", scatter_dimension=2, tiled=True)
    return (mixed.astype(jnp.bfloat16), ssm_state)


HI = lax.Precision.HIGHEST
F32 = jnp.float32
BF16 = jnp.bfloat16


def f32_dot(a, b):
    return jnp.dot(a, b, precision=HI, preferred_element_type=F32)


def nt_dot(a, b):
    return lax.dot_general(a, b, (((1,), (1,)), ((), ())), preferred_element_type=F32)


def silu(v):
    return v / (1.0 + jnp.exp(-v))


def softplus(v):
    return jnp.maximum(v, 0.0) + jnp.log1p(jnp.exp(-jnp.abs(v)))


ROW_TILE = 8


def drain(ref, sem):
    pltpu.make_async_copy(ref, ref, sem).wait()


def gather_kernel(steps, slots, groups, tok_ref, dec_ref, emb_ref, out_ref, buf, tail, sem, tail_sem):
    vocab = emb_ref.shape[0]
    whole = vocab // ROW_TILE * ROW_TILE
    base = lax.axis_index("dp") * vocab
    per_group = slots // groups
    where = []

    def block(i, start):
        return pltpu.make_async_copy(emb_ref.at[pl.ds(start, ROW_TILE)], buf.at[i], sem)

    def rest():
        return pltpu.make_async_copy(emb_ref.at[pl.ds(whole, vocab - whole)], tail, tail_sem)

    in_tail = False
    for s in range(slots):
        q = dec_ref[s]
        for t in range(steps):
            row = tok_ref[t, q] - base
            held = (row >= 0) & (row < whole)
            start = pl.multiple_of(jnp.where(held, row, 0) // ROW_TILE * ROW_TILE, ROW_TILE)
            i = s * steps + t

            @pl.when(held)
            def _():
                block(i, start).start()

            where.append((row, start, held))
            in_tail |= (row >= whole) & (row < vocab)
    if whole < vocab:

        @pl.when(in_tail)
        def _():
            rest().start()

    for i, (row, start, held) in enumerate(where):

        @pl.when(held)
        def _():
            block(i, start).wait()

    if whole < vocab:

        @pl.when(in_tail)
        def _():
            rest().wait()

    rows = lax.broadcasted_iota(jnp.int32, (ROW_TILE, 1), 0)
    for g in range(groups):
        picked = []
        for t in range(steps):
            for j in range(per_group):
                i = (g * per_group + j) * steps + t
                row, start, held = where[i]
                value = jnp.sum(
                    jnp.where(held & (rows == row - start), buf[i].astype(F32), 0.0), axis=0, keepdims=True
                )
                if whole < vocab:
                    trows = lax.broadcasted_iota(jnp.int32, (vocab - whole, 1), 0)
                    value += jnp.sum(
                        jnp.where(trows == row - whole, tail[...].astype(F32), 0.0),
                        axis=0,
                        keepdims=True,
                    )
                picked.append(value)
        out_ref[g] = jnp.concatenate(picked, axis=0).astype(BF16)


def mixer_kernel(
    sizes,
    dec_hbm,
    part_ref,
    seg_hbm,
    xt_hbm,
    bt_hbm,
    gain_hbm,
    cxw_hbm,
    cxb_hbm,
    cbw_hbm,
    cbb_hbm,
    dtb_hbm,
    alog_hbm,
    skip_hbm,
    gg_hbm,
    wzx_hbm,
    wbc_hbm,
    wout_hbm,
    state_hbm,
    mixed_ref,
    final_ref,
    dec_ref,
    gain_ref,
    cxw_ref,
    cxb_ref,
    cbw_ref,
    cbb_ref,
    dtb_ref,
    alog_ref,
    skip_ref,
    gg_ref,
    pair_recv,
    pair_send,
    wzx,
    wbc,
    wout,
    state_in,
    state_send,
    state_recv,
    plane_recv,
    line_send,
    line_recv,
    seg_recv,
    seg_mate,
    seg_own,
    xt_recv,
    bt_recv,
    col_send,
    col_recv,
    sq_send,
    sq_recv,
    out_send,
    out_recv,
    start_state,
    start_low,
    normed_ref,
    xfull,
    bcfull,
    load_sems,
    small_sem,
    own_sems,
    pair_sems,
    mate_sem,
    state_sem,
    plane_sem,
    line_sems,
    seg_sem,
    xt_sem,
    bt_sem,
    col_sem,
    sq_sem,
    out_sem,
    done,
    ready,
):
    n_ctx, n_dp, n_tp, total_heads = sizes
    c, d, p = lax.axis_index("ctx"), lax.axis_index("dp"), lax.axis_index("tp")
    mine = c * n_tp + p
    here_plane = d * n_ctx + c
    ring, plane = n_ctx * n_tp, n_dp * n_ctx
    steps, per, feats = mixed_ref.shape
    rows = steps * per
    heads, dim = cxb_ref.shape
    chans = heads * dim
    width = cbb_ref.shape[1]
    state_n = width // 2
    taps = cxw_ref.shape[0]
    model = gain_ref.shape[1]
    tp_heads = seg_recv.shape[-1]
    n_cols = wbc_hbm.shape[0]
    all_cols = n_cols * n_ctx * n_tp
    half = wzx_hbm.shape[0] // 2
    mirror = n_tp == 4

    def peer(offset):
        dc, dd, dt = offset
        away = lax.rem(p + dt, n_tp)
        if mirror and dt != n_tp // 2:
            away = n_tp - 1 - (p if dt == 1 else lax.rem(p + n_tp // 2, n_tp))
        return lax.rem(c + dc, n_ctx), lax.rem(d + dd, n_dp), away if dt else p

    def device(offset):
        a, b, e = peer(offset)
        return {"ctx": a, "dp": b, "tp": e}

    def along(k):
        return {"ctx": c, "dp": d, "tp": lax.rem(p + k + n_tp, n_tp)}

    far = [1, 2, 3] if mirror else list(range(n_tp - 1, 0, -1))
    routed = [(a, b, 0) for a in reversed(range(n_ctx)) for b in reversed(range(n_dp)) if a + b]
    group = [(a, 0, e) for e in far + [0] for a in reversed(range(n_ctx)) if a + e]
    across = [(0, b, 0) for b in range(1, n_dp)]

    barrier = pltpu.get_barrier_semaphore()
    for o in routed:
        pl.semaphore_signal(
            barrier, inc=1, device_id=device(o), device_id_type=pl.DeviceIdType.MESH
        )
    for k in range(1, n_tp):

        @pl.when(p + k < n_tp)
        def _():
            pl.semaphore_signal(
                barrier, inc=1, device_id=along(k), device_id_type=pl.DeviceIdType.MESH
            )


    owns = []
    for source, target in (
        (dec_hbm, dec_ref),
        (seg_hbm.at[0], seg_own),
        (xt_hbm, xt_recv.at[d]),
        (bt_hbm, bt_recv.at[d]),
    ):
        load = pltpu.make_async_copy(source, target, own_sems.at[len(owns) // 2])
        load.start()
        owns.append(load)
    loads = []
    smalls = []
    pairs = (
        (state_hbm, state_in),
        (wbc_hbm, wbc),
        (wzx_hbm.at[pl.ds(half, half)], wzx.at[pl.ds(half, half)]),
        (wzx_hbm.at[pl.ds(0, half)], wzx.at[pl.ds(0, half)]),
        (wout_hbm, wout),
    )
    small_pairs = (
        (gain_hbm, gain_ref),
        (cxw_hbm, cxw_ref),
        (cxb_hbm, cxb_ref),
        (cbw_hbm, cbw_ref),
        (cbb_hbm, cbb_ref),
        (dtb_hbm, dtb_ref),
        (alog_hbm, alog_ref),
        (skip_hbm, skip_ref),
        (gg_hbm, gg_ref),
    )

    def fetch(source, target, sem, into):
        load = pltpu.make_async_copy(source, target, sem)
        load.start()
        into.append(load)

    fetch(*pairs[0], load_sems.at[0], loads)
    for pair in small_pairs:
        fetch(*pair, small_sem, smalls)
    def send(source, target, send_sem, recv_sem, place):
        pltpu.make_async_remote_copy(
            src_ref=source,
            dst_ref=target,
            send_sem=send_sem,
            recv_sem=recv_sem,
            device_id=place,
            device_id_type=pl.DeviceIdType.MESH,
        ).start()

    pl.semaphore_wait(barrier, len(routed) + p)
    for k in range(1, n_tp):

        @pl.when(p >= k)
        def _():
            pl.semaphore_signal(
                ready, inc=1, device_id=along(-k), device_id_type=pl.DeviceIdType.MESH
            )


    for o in routed:
        send(part_ref.at[peer(o)[1]], plane_recv.at[here_plane], done, plane_sem, device(o))
    plane_recv[here_plane] = part_ref[d]

    owns[0].wait()
    owns[1].wait()
    parity = lax.rem(c, 2)
    mate = {"ctx": c + 1 - 2 * parity, "dp": d, "tp": p}
    half_ctx = n_ctx // 2
    blocks = [(a, b) for a in reversed(range(half_ctx)) for b in reversed(range(n_dp))]
    seg_recv[here_plane] = seg_own[...]
    send(seg_own, seg_mate, done, mate_sem, mate)
    for o in routed:
        send(seg_own, seg_recv.at[here_plane], done, seg_sem, device(o))
    owns[2].wait()
    owns[3].wait()
    for o in across:
        send(xt_recv.at[d], xt_recv.at[d], done, xt_sem, device(o))
        send(bt_recv.at[d], bt_recv.at[d], done, bt_sem, device(o))
    picks = []
    for b in range(n_dp):
        target_group = lax.rem(d + b, n_dp)
        pick = jnp.int32(0)
        for j in range(per):
            local = dec_ref[target_group * per + j] - d * per
            pick += jnp.where((local >= 0) & (local < per), local, 0)
        picks.append(pick)
    loads[0].wait()
    for slot, (a, b) in enumerate(blocks):
        first = pl.multiple_of(lax.rem(mate["ctx"] + 2 * a, n_ctx) * chans, chans)
        state_send[slot] = state_in[picks[b], pl.ds(first, chans), :]
        send(state_send.at[slot], pair_recv.at[slot], done, pair_sems.at[slot], mate)

    for i, pair in enumerate(pairs[1:]):
        fetch(*pair, load_sems.at[i + 1], loads)

    fold = (
        lax.broadcasted_iota(jnp.int32, (dim, chans), 0)
        == lax.rem(lax.broadcasted_iota(jnp.int32, (dim, chans), 1), dim)
    ).astype(F32)
    head_rows = lax.broadcasted_iota(jnp.int32, (heads, chans), 0) == lax.div(
        lax.broadcasted_iota(jnp.int32, (heads, chans), 1), dim
    )

    def flat(value):
        return jnp.sum(jnp.where(head_rows, f32_dot(value, fold), 0.0), axis=0, keepdims=True)

    def spread(value, first):
        count = value.shape[1]
        chosen = (
            lax.broadcasted_iota(jnp.int32, (count, chans), 0)
            == first + lax.div(lax.broadcasted_iota(jnp.int32, (count, chans), 1), dim)
        ).astype(F32)
        return f32_dot(value, chosen)

    drain(seg_mate, mate_sem)
    shrink = []
    for b in range(n_dp):
        row = pl.ds(picks[b], 1)
        shrink.append(jnp.exp(-jnp.where(parity == 0, seg_mate[row, :], seg_own[row, :])))
    ones = [jnp.ones((1, tp_heads), F32)] * n_dp
    shrink = jnp.concatenate(shrink + ones, axis=0)
    shrink_cols = [
        jnp.transpose(spread(shrink, lax.rem(c + 2 * a, n_ctx) * heads)) for a in range(half_ctx)
    ]
    for slot, (a, b) in enumerate(blocks):
        drain(pair_recv.at[slot], pair_sems.at[slot])
        first = pl.multiple_of(lax.rem(c + 2 * a, n_ctx) * chans, chans)
        here = state_in[picks[b], pl.ds(first, chans), :].astype(F32)
        there = pair_recv[slot].astype(F32)
        factor = shrink_cols[a][:, b : b + 1]
        even = jnp.where(parity == 0, here, there)
        odd = jnp.where(parity == 0, there, here)
        added = (factor * even + odd).astype(BF16)
        target = state_recv.at[d * half_ctx + lax.div(c, 2)]
        if a + b:
            pair_send[slot] = added
            send(pair_send.at[slot], target, done, state_sem, device((2 * a, b, 0)))
        else:
            state_recv[d * half_ctx + lax.div(c, 2)] = added

    drain(plane_recv.at[pl.ds(0, plane - 1)], plane_sem)
    for i in range(n_ctx):
        piece = plane_recv[i].astype(F32)
        for g in range(1, n_dp):
            piece += plane_recv[g * n_ctx + i].astype(F32)
        line_send[i] = piece.astype(BF16)
    for k in range(n_tp - 1, 0, -1):

        @pl.when(p >= k)
        def _():
            send(line_send, line_recv.at[p], done, line_sems.at[p], along(-k))

    @pl.when(p < n_tp - 1)
    def _():
        pl.semaphore_wait(ready, n_tp - 1 - p)

    for k in range(n_tp - 1, 0, -1):

        @pl.when(p + k < n_tp)
        def _():
            send(line_send, line_recv.at[p], done, line_sems.at[p], along(k))

    loads[1].wait()
    tallies = []

    def take(values, e):
        spots = [pl.ds(pl.multiple_of((i * n_tp + e) * feats, feats), feats) for i in range(n_ctx)]
        held = jnp.concatenate([values[i].astype(F32) for i in range(n_ctx)], axis=1)
        gains = jnp.concatenate([gain_ref[:, spot] for spot in spots], axis=1)
        low = (held * gains).astype(BF16)
        weights = jnp.concatenate([wbc[:, spot] for spot in spots], axis=1)
        for i, spot in enumerate(spots):
            normed_ref[:, spot] = low[:, i * feats : (i + 1) * feats]
        square = held * held
        while square.shape[1] % 256 == 0:
            width = square.shape[1] // 2
            square = square[:, :width] + square[:, width:]
        tallies.append((square, nt_dot(low, weights)))


    for load in smalls:
        load.wait()
    take([line_send[i] for i in range(n_ctx)], p)
    tap_rows = [flat(cxw_ref[k]) for k in range(taps)]
    bias_row = flat(cxb_ref[...])
    gate_row = flat(gg_ref[...])
    idle = jnp.zeros((1, total_heads - heads), F32)
    dtb_row = jnp.concatenate([dtb_ref[...], idle], axis=1)
    rate_row = jnp.concatenate([-jnp.exp(alog_ref[...]), idle], axis=1)
    skip_row = jnp.concatenate([skip_ref[...], idle], axis=1)

    holders = [lax.div(dec_ref[d * per + j], per) for j in range(per)]
    places = [lax.rem(dec_ref[d * per + j], per) for j in range(per)]
    for one, ref in ((xt_sem, xt_recv), (bt_sem, bt_recv)):
        if across:
            drain(ref.at[pl.ds(0, n_dp - 1)], one)
    plane_rows = lax.broadcasted_iota(jnp.int32, (per, 1), 0)
    for k in range(taps - 1):
        for j in range(per):
            r = k * per + j
            xfull[r : r + 1, :] = flat(xt_recv[holders[j], places[j], k].astype(F32))
            tail = bt_recv[holders[j], k].astype(F32)
            bcfull[r : r + 1, :] = jnp.sum(
                jnp.where(plane_rows == places[j], tail, 0.0), axis=0, keepdims=True
            )

    drain(seg_recv.at[pl.ds(0, plane - 1)], seg_sem)
    weights = []
    for j in range(per):
        after = jnp.zeros((1, tp_heads), F32)
        ordered = []
        row = pl.ds(places[j], 1)
        for m in reversed(range(half_ctx)):
            ordered.append(jnp.exp(-after))
            for k in (2 * m + 1, 2 * m):
                after = after + seg_recv[holders[j] * n_ctx + k, row, :]
        weights.extend(reversed(ordered))
    weight_cols = jnp.transpose(spread(jnp.concatenate(weights, axis=0), c * heads))

    for e in reversed(far):
        there = peer((0, 0, e))[2]
        drain(line_recv.at[there], line_sems.at[there])
        take([line_recv[there, i] for i in range(n_ctx)], there)
    square, narrow = tallies[0]
    for more, columns in tallies[1:]:
        square, narrow = square + more, narrow + columns
    scale = lax.rsqrt(jnp.sum(square, axis=1, keepdims=True) / model + epsilon)
    padded = jnp.concatenate([narrow * scale, jnp.zeros((rows, 128 - n_cols), F32)], axis=1)
    col_send[...] = pltpu.roll(padded, lax.rem(n_cols * mine, 128), 1)
    for o in group:
        send(col_send, col_recv.at[mine], done, col_sem, device(o))
    col_recv[mine] = col_send[...]
    loads[2].wait()
    x_rows = nt_dot(normed_ref[...], wzx[half : 2 * half, :]) * scale
    loads[3].wait()
    z_gate = silu(nt_dot(normed_ref[...], wzx[0:half, :]) * scale)

    lead = (taps - 1) * per
    xfull[lead : lead + rows, :] = x_rows
    conv = bias_row
    for k in range(taps):
        conv = conv + tap_rows[k] * xfull[k * per : k * per + rows, :]
    xc = silu(conv)

    drain(state_recv.at[pl.ds(0, n_dp * half_ctx - 1)], state_sem)
    for j in range(per):
        begin = None
        for m in range(half_ctx):
            r = j * half_ctx + m
            term = weight_cols[:, r : r + 1] * state_recv[holders[j] * half_ctx + m].astype(F32)
            begin = term if begin is None else begin + term
        start_state[j] = begin
        start_low[j] = begin.astype(BF16)

    drain(col_recv.at[pl.ds(0, ring - 1)], col_sem)
    lanes = lax.broadcasted_iota(jnp.int32, (rows, 128), 1)
    blocks_of = []
    for v in range(-(-all_cols // 128)):
        block = jnp.zeros((rows, 128), F32)
        for i in range(ring):
            low = n_cols * i - 128 * v
            if low < 128 and low + n_cols > 0:
                block = jnp.where((lanes >= low) & (lanes < low + n_cols), col_recv[i], block)
        blocks_of.append(block)
    columns = jnp.concatenate(blocks_of, axis=1)
    bcfull[lead : lead + rows, :] = columns[:, :width]
    head_first = (p * n_ctx + c) * heads
    dt_raw = pltpu.roll(columns[:, width:all_cols], total_heads - head_first, 1)
    step_size = softplus(dt_raw + dtb_row)
    row_of = lax.broadcasted_iota(jnp.int32, (rows, 1), 0)

    def later(value, k):
        return pltpu.roll(value, k * per, 0) if k else value

    total = step_size * rate_row
    k = 1
    while k < steps:
        total = total + jnp.where(row_of >= k * per, later(total, k), 0.0)
        k *= 2
    conv = cbb_ref[...]
    for k in range(taps):
        conv = conv + cbw_ref[k : k + 1, :] * bcfull[k * per : k * per + rows, :]
    bcc = silu(conv)
    b_all, c_all = bcc[:, :state_n], bcc[:, state_n:]

    row_slot = lax.rem(row_of, per)
    from_start = jnp.zeros((rows, chans), F32)
    c_low = c_all.astype(BF16)
    for j in range(per):
        from_start += jnp.where(row_slot == j, nt_dot(c_low, start_low[j]), 0.0)

    def by_head(value):
        if 128 % dim or chans % 128:
            return spread(value, 0)
        packed = 128 // dim
        out = []
        for m in range(chans // 128):
            part = jnp.broadcast_to(value[:, m * packed : m * packed + 1], (rows, 128))
            for q in range(1, packed):
                one = value[:, m * packed + q : m * packed + q + 1]
                part = jnp.where(lanes >= q * dim, one, part)
            out.append(part)
        return jnp.concatenate(out, axis=1)

    def at(value, t):
        return value[t * per : (t + 1) * per]

    y = by_head(jnp.exp(total)) * from_start
    for k in range(steps):
        overlap = jnp.sum(later(b_all, k) * c_all, axis=1, keepdims=True)
        if k:
            valid = row_of >= k * per
            decay = jnp.exp(jnp.where(valid, total - later(total, k), 0.0))
            share = jnp.where(valid, decay * overlap * later(step_size, k), 0.0)
        else:
            share = step_size * overlap + skip_row
        y = y + by_head(share) * later(xc, k)
    gated = y * z_gate
    diagonal = lax.broadcasted_iota(jnp.int32, (rows, 128), 0) == lax.broadcasted_iota(
        jnp.int32, (rows, 128), 1
    )
    loads[4].wait()
    scaled = (gated * gate_row).astype(BF16)
    for e in far + [0]:
        there = peer((0, 0, e))[2]
        cuts = [
            wout[:, pl.ds(pl.multiple_of((a * n_tp + there) * feats, feats), feats)]
            for a in range(n_ctx)
        ]
        partial = jnp.dot(scaled, jnp.concatenate(cuts, axis=1), preferred_element_type=F32)
        for a in range(n_ctx):
            out_send[e * n_ctx + a] = partial[:, a * feats : (a + 1) * feats].astype(BF16)
        for a in reversed(range(n_ctx)):
            if a + e:
                o = (a, 0, e)
                spot = e * n_ctx + peer(o)[0]
                send(out_send.at[spot], out_recv.at[mine], done, out_sem, device(o))
        if e == far[0]:
            squares = jnp.sum(gated * gated, axis=1, keepdims=True)
            sq_send[...] = jnp.sum(jnp.where(diagonal, squares, 0.0), axis=0, keepdims=True)
            for o in group:
                send(sq_send, sq_recv.at[mine], done, sq_sem, device(o))
            sq_recv[mine] = sq_send[...]
    out_recv[mine] = out_send[c]

    last = jnp.concatenate([at(total, steps - 1)] * steps, axis=0)
    late = by_head(jnp.exp(last - total) * step_size) * xc
    flat_rows = jnp.concatenate([late, by_head(jnp.exp(last))], axis=0)
    tall = jnp.transpose(flat_rows)
    for j in range(per):
        b_own = jnp.where(row_slot == j, b_all, 0.0)
        final_ref[j] = (
            tall[:, rows + j : rows + j + 1] * start_state[j] + f32_dot(tall[:, :rows], b_own)
        )

    drain(plane_recv.at[pl.ds(0, plane - 1)], done)
    drain(line_recv.at[pl.ds(0, n_tp - 1)], done)
    drain(seg_recv.at[pl.ds(0, plane - 1)], done)
    drain(seg_mate, done)
    drain(state_send, done)
    drain(pair_send.at[pl.ds(0, len(blocks) - 1)], done)
    if across:
        drain(xt_recv.at[pl.ds(0, n_dp - 1)], done)
        drain(bt_recv.at[pl.ds(0, n_dp - 1)], done)
    drain(col_recv.at[pl.ds(0, ring - 1)], done)
    drain(sq_recv.at[pl.ds(0, ring - 1)], done)
    drain(out_recv.at[pl.ds(0, ring - 1)], done)

    drain(sq_recv.at[pl.ds(0, ring - 1)], sq_sem)
    total_squares = sq_recv[0]
    for i in range(1, ring):
        total_squares = total_squares + sq_recv[i]
    total_squares = jnp.sum(jnp.where(diagonal, total_squares, 0.0), axis=1, keepdims=True)
    inverse = lax.rsqrt(total_squares / (total_heads * dim) + epsilon)
    drain(out_recv.at[pl.ds(0, ring - 1)], out_sem)
    mixed = out_recv[0].astype(F32)
    for i in range(1, ring):
        mixed = mixed + out_recv[i].astype(F32)
    mixed = mixed * inverse
    for t in range(steps):
        mixed_ref[t] = at(mixed, t).astype(BF16)


def tail_kernel(mixed_in, final_in, mixed_out, final_out, sems):
    copies = [
        pltpu.make_async_copy(final_in.at[j], final_out.at[j], sems.at[j])
        for j in range(final_in.shape[0])
    ]
    copies.append(pltpu.make_async_copy(mixed_in, mixed_out, sems.at[len(copies)]))
    for copy in copies:
        copy.start()
    for copy in copies:
        copy.wait()


def kernel_device(
    sizes,
    token_ids,
    decode_prompt,
    embedding,
    norm_gain,
    w_zx,
    w_bcdt,
    conv_x_weight,
    conv_x_bias,
    conv_bc_weight,
    conv_bc_bias,
    dt_bias,
    a_log,
    d_skip,
    gate_norm_gain,
    w_out,
    state_parts,
    seg_rate,
    x_tail,
    bc_tail,
):
    n_ctx, n_dp, n_tp, _ = sizes
    steps = token_ids.shape[0]
    slots = decode_prompt.shape[0]
    per = state_parts.shape[1]
    rows = steps * per
    vocab, feats = embedding.shape
    heads, dim, model = w_zx.shape[1:]
    chans = heads * dim
    tp_heads, state_n = state_parts.shape[2], state_parts.shape[4]
    ring, plane, blocks = n_ctx * n_tp, n_dp * n_ctx, n_dp * (n_ctx // 2)
    smem = pl.BlockSpec(memory_space=pltpu.SMEM)
    vmem = pl.BlockSpec(memory_space=pltpu.VMEM)
    anywhere = pl.BlockSpec(memory_space=pl.ANY)
    sem = pltpu.SemaphoreType.DMA
    rest = max(1, vocab % ROW_TILE)
    part = pl.pallas_call(
        functools.partial(gather_kernel, steps, slots, n_dp),
        out_shape=pltpu.VMEM((n_dp, rows, feats), BF16),
        in_specs=[smem, smem, anywhere],
        out_specs=vmem,
        scratch_shapes=[
            pltpu.VMEM((steps * slots, ROW_TILE, feats), BF16),
            pltpu.VMEM((rest, feats), BF16),
            sem,
            sem,
        ],
        name="gather_rows",
    )(token_ids, decode_prompt, embedding)
    wide = 2 * state_n
    full_rows = -(-(conv_x_weight.shape[0] - 1 + steps) * per // 8) * 8
    smalls = (
        norm_gain[None],
        conv_x_weight,
        conv_x_bias,
        conv_bc_weight,
        conv_bc_bias[None],
        dt_bias[None],
        a_log[None],
        d_skip[None],
        gate_norm_gain,
    )
    bc_planes = jnp.swapaxes(bc_tail, 0, 1)
    mixed, final = pl.pallas_call(
        functools.partial(mixer_kernel, sizes),
        out_shape=(
            pltpu.VMEM((steps, per, feats), BF16),
            pltpu.VMEM((per, chans, state_n), F32),
        ),
        in_specs=[anywhere, vmem] + [anywhere] * 16,
        out_specs=(vmem, vmem),
        scratch_shapes=[
            pltpu.SMEM((slots,), jnp.int32),
            *[pltpu.VMEM(small.shape, small.dtype) for small in smalls],
            pltpu.VMEM((blocks, chans, state_n), BF16),
            pltpu.VMEM((blocks, chans, state_n), BF16),
            pltpu.VMEM((2 * chans, model), BF16),
            pltpu.VMEM(w_bcdt.shape[::-1], BF16),
            pltpu.VMEM((chans, model), BF16),
            pltpu.VMEM((per, tp_heads * dim, state_n), BF16),
            pltpu.VMEM((blocks, chans, state_n), BF16),
            pltpu.VMEM((blocks, chans, state_n), BF16),
            pltpu.VMEM((plane, rows, feats), BF16),
            pltpu.VMEM((n_ctx, rows, feats), BF16),
            pltpu.VMEM((n_tp, n_ctx, rows, feats), BF16),
            pltpu.VMEM((plane, per, tp_heads), F32),
            pltpu.VMEM((per, tp_heads), F32),
            pltpu.VMEM((per, tp_heads), F32),
            pltpu.VMEM((n_dp,) + x_tail.shape, BF16),
            pltpu.VMEM((n_dp,) + bc_planes.shape, BF16),
            pltpu.VMEM((rows, 128), F32),
            pltpu.VMEM((ring, rows, 128), F32),
            pltpu.VMEM((1, 128), F32),
            pltpu.VMEM((ring, 1, 128), F32),
            pltpu.VMEM((ring, rows, feats), BF16),
            pltpu.VMEM((ring, rows, feats), BF16),
            pltpu.VMEM((per, chans, state_n), F32),
            pltpu.VMEM((per, chans, state_n), BF16),
            pltpu.VMEM((rows, model), BF16),
            pltpu.VMEM((full_rows, chans), F32),
            pltpu.VMEM((full_rows, wide), F32),
            sem((5,)),
            sem,
            sem((2,)),
            sem((blocks,)),
            *[sem] * 3,
            sem((n_tp,)),
            *[sem] * 7,
            pltpu.SemaphoreType.REGULAR,
        ],
        compiler_params=pltpu.CompilerParams(
            collective_id=0, has_side_effects=True, vmem_limit_bytes=56 * 1024 * 1024
        ),
        name="mixer",
    )(
        decode_prompt,
        pltpu.with_memory_space_constraint(part, pltpu.VMEM),
        seg_rate,
        x_tail,
        bc_planes,
        *smalls,
        w_zx.reshape(2 * chans, model),
        w_bcdt.T,
        w_out.reshape(chans, model),
        state_parts.reshape(per, tp_heads * dim, state_n),
    )
    mixed, final = pl.pallas_call(
        tail_kernel,
        out_shape=(
            jax.ShapeDtypeStruct(mixed.shape, BF16),
            jax.ShapeDtypeStruct(final.shape, F32),
        ),
        in_specs=[anywhere] * 2,
        out_specs=(anywhere, anywhere),
        scratch_shapes=[sem((per + 1,))],
        name="tail",
    )(
        pltpu.with_memory_space_constraint(mixed, pltpu.VMEM),
        pltpu.with_memory_space_constraint(final, pltpu.VMEM),
    )
    return mixed, final.reshape(per, heads, dim, state_n)


def choose_device(sizes, *args):
    embedding, w_zx, w_bcdt = args[2], args[4], args[5]
    heads, dim = w_zx.shape[1:3]
    fits = (
        embedding.shape[1] % 128 == 0
        and sizes[0] % 2 == 0
        and (heads * dim) % 128 == 0
        and w_bcdt.shape[1] <= 128
        and embedding.shape[0] >= ROW_TILE
    )
    if fits:
        return kernel_device(sizes, *args)
    return per_device(*args)


def solution(mesh):
    sizes = (mesh.shape["ctx"], mesh.shape["dp"], mesh.shape["tp"], HEADS)
    return jax.shard_map(
        functools.partial(choose_device, sizes),
        mesh=mesh,
        in_specs=(
            P(),
            P(),
            P("dp", ("ctx", "tp")),
            P(),
            P(None, ("tp", "ctx"), None, None),
            P(None, ("ctx", "tp")),
            P(None, ("tp", "ctx"), None),
            P(("tp", "ctx"), None),
            P(),
            P(),
            P(("tp", "ctx")),
            P(("tp", "ctx")),
            P(("tp", "ctx")),
            P(("tp", "ctx"), None),
            P(("tp", "ctx"), None, None),
            P("ctx", "dp", "tp", None, None),
            P("ctx", "dp", "tp"),
            P("dp", None, ("tp", "ctx"), None),
            P("dp", None, None),
        ),
        out_specs=(P(None, "dp", ("ctx", "tp")), P("dp", ("tp", "ctx"), None, None)),
        check_vma=False,
    )
```

```python
import functools

import jax
import jax.numpy as jnp
from jax import lax
from jax.experimental import pallas as pl
from jax.experimental.pallas import tpu as pltpu
from jax.sharding import PartitionSpec as P

HEADS = 128
HEAD_DIM = 64


epsilon = 1e-05


def entering(shard, axis, combine, identity):
    count, here = (lax.axis_size(axis), lax.axis_index(axis))
    everything = lax.all_gather(shard, axis)
    start = jnp.broadcast_to(jnp.asarray(identity, shard.dtype), shard.shape)

    def step(k, before):
        at = count - 1 - k
        reached = at > here
        new = combine(before, everything[at])
        return jnp.where(reached, new, before)

    return lax.fori_loop(0, count, step, start)


def rms_scale(values, gain):
    return values * lax.rsqrt(jnp.mean(values * values, axis=-1, keepdims=True) + epsilon) * gain


def select_rows(picker, values):
    return jnp.tensordot(picker, values, axes=1, precision=lax.Precision.HIGHEST)


def add_rates(earlier, later_one):
    return earlier + later_one


def per_device(
    token_ids,
    decode_prompt,
    embedding,
    norm_gain,
    w_zx,
    w_bcdt,
    conv_x_weight,
    conv_x_bias,
    conv_bc_weight,
    conv_bc_bias,
    dt_bias,
    a_log,
    d_skip,
    gate_norm_gain,
    w_out,
    state_parts,
    seg_rate,
    x_tail,
    bc_tail,
):
    group = lax.axis_index("dp")
    local_count = state_parts.shape[1]
    slot_count = decode_prompt.shape[0]
    head_count = w_zx.shape[1]
    state_width = conv_bc_bias.shape[0] // 2
    after_rates = entering(seg_rate, "ctx", add_rates, jnp.zeros_like(seg_rate))
    seg_weight = jnp.exp(-after_rates[0])
    scaled = seg_weight[:, :, None, None] * state_parts[0].astype(jnp.float32)
    channel_sums = lax.psum_scatter(
        scaled.astype(jnp.bfloat16), "ctx", scatter_dimension=2, tiled=True
    ).astype(jnp.float32)
    combined = lax.all_to_all(
        channel_sums.astype(jnp.bfloat16), "ctx", split_axis=1, concat_axis=2, tiled=True
    ).astype(channel_sums.dtype)
    tails_x = x_tail.astype(jnp.float32)
    tails_bc = bc_tail.astype(jnp.float32)
    own_slots = lax.dynamic_slice_in_dim(decode_prompt, group * local_count, local_count)
    prompt_ids = jnp.arange(slot_count, dtype=jnp.int32)
    every_state, every_x, every_bc = (
        lax.all_gather(combined.astype(jnp.bfloat16), "dp", axis=0, tiled=True).astype(
            combined.dtype
        ),
        lax.all_gather(tails_x.astype(jnp.bfloat16), "dp", axis=0, tiled=True).astype(
            tails_x.dtype
        ),
        lax.all_gather(tails_bc.astype(jnp.bfloat16), "dp", axis=0, tiled=True).astype(
            tails_bc.dtype
        ),
    )
    picker = (own_slots[:, None] == prompt_ids[None, :]).astype(jnp.float32)
    ssm_state = select_rows(picker, every_state)
    x_window = select_rows(picker, every_x)
    bc_window = select_rows(picker, every_bc)
    vocab_rows = embedding.shape[0]
    holder = (decode_prompt[:, None] == prompt_ids[None, :]).astype(jnp.int32)
    slot_tokens = jnp.sum(token_ids[:, None, :] * holder[None], axis=2)
    offset_tokens = slot_tokens - group * vocab_rows
    inside = (offset_tokens >= 0) & (offset_tokens < vocab_rows)
    looked = jnp.take(embedding, jnp.clip(offset_tokens, 0, vocab_rows - 1), axis=0)
    partial_rows = jnp.where(inside[..., None], looked.astype(jnp.float32), 0.0)
    own_rows = lax.psum_scatter(
        partial_rows.astype(jnp.bfloat16), "dp", scatter_dimension=1, tiled=True
    )
    embedded = lax.all_gather(own_rows, ("ctx", "tp"), axis=2, tiled=True)
    steps_count = embedded.shape[0]
    flat_rows = embedded.reshape(-1, embedded.shape[2]).astype(jnp.float32)
    normed = rms_scale(flat_rows, norm_gain).astype(jnp.bfloat16)
    projected = jnp.einsum("rd,khed->krhe", normed, w_zx, preferred_element_type=jnp.float32)
    projected = projected.reshape(
        2, steps_count, local_count, projected.shape[2], projected.shape[3]
    )
    columns = lax.all_gather(
        jnp.dot(normed, w_bcdt, preferred_element_type=jnp.float32),
        ("ctx", "tp"),
        axis=1,
        tiled=True,
    )
    columns = columns.reshape(steps_count, local_count, -1)
    head_block = lax.axis_index("tp") * lax.axis_size("ctx") + lax.axis_index("ctx")
    head_start = 2 * state_width + head_block * head_count
    dt_raw = lax.dynamic_slice_in_dim(columns, head_start, head_count, 2)
    decay_rate = -jnp.exp(a_log)
    gated_steps = []
    for moment in range(steps_count):
        x_window = jnp.concatenate([x_window, projected[1, moment][:, None]], axis=1)
        bc_window = jnp.concatenate(
            [bc_window, columns[moment, :, None, : 2 * state_width]], axis=1
        )
        x_conv = jax.nn.silu(jnp.einsum("pkhe,khe->phe", x_window, conv_x_weight) + conv_x_bias)
        bc_conv = jax.nn.silu(jnp.einsum("pkn,kn->pn", bc_window, conv_bc_weight) + conv_bc_bias)
        step_size = jax.nn.softplus(dt_raw[moment] + dt_bias)
        retain = jnp.exp(step_size * decay_rate)
        ssm_state = (
            retain[:, :, None, None] * ssm_state
            + (step_size[:, :, None] * x_conv)[:, :, :, None] * bc_conv[:, None, None, :state_width]
        )
        output = (
            jnp.einsum("phen,pn->phe", ssm_state, bc_conv[:, state_width:])
            + d_skip[None, :, None] * x_conv
        )
        gated_steps.append(output * jax.nn.silu(projected[0, moment]))
        x_window = x_window[:, 1:]
        bc_window = bc_window[:, 1:]
    gated_all = jnp.stack(gated_steps)
    local_squares = jnp.sum(gated_all * gated_all, axis=(2, 3))
    total_squares = lax.psum(local_squares, ("ctx", "tp"))
    inverse = lax.rsqrt(total_squares / (HEADS * HEAD_DIM) + epsilon)
    normed_out = (gated_all * inverse[:, :, None, None] * gate_norm_gain).astype(jnp.bfloat16)
    partial_out = jnp.einsum("tphe,hed->tpd", normed_out, w_out, preferred_element_type=jnp.float32)
    outer_sum = lax.psum_scatter(
        partial_out.astype(jnp.bfloat16), "ctx", scatter_dimension=2, tiled=True
    ).astype(jnp.float32)
    mixed = lax.psum_scatter(outer_sum, "tp", scatter_dimension=2, tiled=True)
    return (mixed.astype(jnp.bfloat16), ssm_state)


HI = lax.Precision.HIGHEST
F32 = jnp.float32
BF16 = jnp.bfloat16


def f32_dot(a, b):
    return jnp.dot(a, b, precision=HI, preferred_element_type=F32)


def nt_dot(a, b):
    return lax.dot_general(a, b, (((1,), (1,)), ((), ())), preferred_element_type=F32)


def silu(v):
    return v / (1.0 + jnp.exp(-v))


def softplus(v):
    return jnp.maximum(v, 0.0) + jnp.log1p(jnp.exp(-jnp.abs(v)))


ROW_TILE = 8


def drain(ref, sem):
    pltpu.make_async_copy(ref, ref, sem).wait()


def row_place(steps, tok_ref, dec_ref, vocab, s, t):
    whole = vocab // ROW_TILE * ROW_TILE
    row = tok_ref[t, dec_ref[s]] - lax.axis_index("dp") * vocab
    held = (row >= 0) & (row < whole)
    start = pl.multiple_of(jnp.where(held, row, 0) // ROW_TILE * ROW_TILE, ROW_TILE)
    return row, held, start


def gather_kernel(
    steps, slots, tok_ref, dec_ref, emb_ref, buf, tail, mark, tail_mark, sem, tail_sem
):
    vocab = emb_ref.shape[0]
    whole = vocab // ROW_TILE * ROW_TILE
    where = []

    def block(i, start):
        return pltpu.make_async_copy(emb_ref.at[pl.ds(start, ROW_TILE)], buf.at[i], sem)

    def rest():
        return pltpu.make_async_copy(emb_ref.at[pl.ds(whole, vocab - whole)], tail, tail_sem)

    in_tail = False
    for s in range(slots):
        for t in range(steps):
            row, held, start = row_place(steps, tok_ref, dec_ref, vocab, s, t)
            i = s * steps + t

            @pl.when(held)
            def _():
                block(i, start).start()

            where.append((row, start, held))
            in_tail |= (row >= whole) & (row < vocab)
    if whole < vocab:

        @pl.when(in_tail)
        def _():
            rest().start()

    tile_rows = lax.broadcasted_iota(jnp.int32, mark.shape[1:], 0)
    tail_rows = whole + lax.broadcasted_iota(jnp.int32, tail_mark.shape[1:], 0)
    for i, (row, start, held) in enumerate(where):
        mark[i] = (held & (tile_rows == row - start)).astype(F32)
        tail_mark[i] = (tail_rows == jnp.where(row < vocab, row, -1)).astype(F32)

    for i, (row, start, held) in enumerate(where):

        @pl.when(held)
        def _():
            block(i, start).wait()

    if whole < vocab:

        @pl.when(in_tail)
        def _():
            rest().wait()


def mixer_kernel(
    sizes,
    vocab,
    dec_hbm,
    raw_ref,
    rest_ref,
    mark_ref,
    rest_mark_ref,
    seg_hbm,
    xt_hbm,
    bt_hbm,
    gain_hbm,
    cxw_hbm,
    cxb_hbm,
    cbw_hbm,
    cbb_hbm,
    dtb_hbm,
    alog_hbm,
    skip_hbm,
    gg_hbm,
    wzx_hbm,
    wbc_hbm,
    wout_hbm,
    state_hbm,
    mixed_ref,
    final_ref,
    dec_ref,
    part_ref,
    gain_ref,
    cxw_ref,
    cxb_ref,
    cbw_ref,
    cbb_ref,
    dtb_ref,
    alog_ref,
    skip_ref,
    gg_ref,
    pair_recv,
    pair_send,
    wzx,
    wbc,
    wout,
    state_in,
    state_send,
    state_recv,
    rows_recv,
    line_send,
    seg_recv,
    seg_mate,
    seg_own,
    xt_recv,
    bt_recv,
    col_send,
    col_recv,
    sq_send,
    sq_recv,
    out_send,
    out_recv,
    start_state,
    start_low,
    normed_ref,
    xfull,
    bcfull,
    load_sems,
    small_sem,
    own_sems,
    pair_sems,
    mate_sem,
    state_sem,
    plane_sem,
    line_sems,
    seg_sem,
    xt_sem,
    bt_sem,
    col_sem,
    sq_sem,
    out_sem,
    done,
    ready,
):
    n_ctx, n_dp, n_tp, total_heads = sizes
    c, d, p = lax.axis_index("ctx"), lax.axis_index("dp"), lax.axis_index("tp")
    mine = c * n_tp + p
    here_plane = d * n_ctx + c
    ring, plane = n_ctx * n_tp, n_dp * n_ctx
    steps, per, feats = mixed_ref.shape
    rows = steps * per
    heads, dim = cxb_ref.shape
    chans = heads * dim
    width = cbb_ref.shape[1]
    state_n = width // 2
    taps = cxw_ref.shape[0]
    model = gain_ref.shape[1]
    tp_heads = seg_recv.shape[-1]
    n_cols = wbc_hbm.shape[0]
    all_cols = n_cols * n_ctx * n_tp
    half = wzx_hbm.shape[0] // 2
    mirror = n_tp == 4

    def peer(offset):
        dc, dd, dt = offset
        away = lax.rem(p + dt, n_tp)
        if mirror and dt != n_tp // 2:
            away = n_tp - 1 - (p if dt == 1 else lax.rem(p + n_tp // 2, n_tp))
        return lax.rem(c + dc, n_ctx), lax.rem(d + dd, n_dp), away if dt else p

    def device(offset):
        a, b, e = peer(offset)
        return {"ctx": a, "dp": b, "tp": e}

    def along(k):
        return {"ctx": c, "dp": d, "tp": lax.rem(p + k + n_tp, n_tp)}

    def whole_plane(k):
        return [
            {"ctx": a, "dp": b, "tp": lax.rem(p + k + n_tp, n_tp)}
            for a, b, _ in [peer((a, b, 0)) for a in reversed(range(n_ctx)) for b in reversed(range(n_dp))]
        ]

    far = [1, 2, 3] if mirror else list(range(n_tp - 1, 0, -1))
    routed = [(a, b, 0) for a in reversed(range(n_ctx)) for b in reversed(range(n_dp)) if a + b]
    group = [(a, 0, e) for e in far + [0] for a in reversed(range(n_ctx)) if a + e]
    across = [(0, b, 0) for b in range(1, n_dp)]

    for e in range(n_tp):
        rows_recv[e, n_ctx:] = jnp.zeros((plane - n_ctx, rows, feats), BF16)
    barrier = pltpu.get_barrier_semaphore()
    for k in range(n_tp - 1, 0, -1):

        @pl.when(p + k < n_tp)
        def _():
            for place in whole_plane(k):
                pl.semaphore_signal(
                    barrier, inc=1, device_id=place, device_id_type=pl.DeviceIdType.MESH
                )


    for o in routed:
        pl.semaphore_signal(
            barrier, inc=1, device_id=device(o), device_id_type=pl.DeviceIdType.MESH
        )

    owns = []
    for source, target in (
        (dec_hbm, dec_ref),
        (seg_hbm.at[0], seg_own),
        (xt_hbm, xt_recv.at[d]),
        (bt_hbm, bt_recv.at[d]),
    ):
        load = pltpu.make_async_copy(source, target, own_sems.at[len(owns) // 2])
        load.start()
        owns.append(load)
    loads = []
    smalls = []
    pairs = (
        (state_hbm, state_in),
        (wbc_hbm, wbc),
        (wzx_hbm.at[pl.ds(half, half)], wzx.at[pl.ds(half, half)]),
        (wzx_hbm.at[pl.ds(0, half)], wzx.at[pl.ds(0, half)]),
        (wout_hbm, wout),
    )
    small_pairs = (
        (gain_hbm, gain_ref),
        (cxw_hbm, cxw_ref),
        (cxb_hbm, cxb_ref),
        (cbw_hbm, cbw_ref),
        (cbb_hbm, cbb_ref),
        (dtb_hbm, dtb_ref),
        (alog_hbm, alog_ref),
        (skip_hbm, skip_ref),
        (gg_hbm, gg_ref),
    )

    def fetch(source, target, sem, into):
        load = pltpu.make_async_copy(source, target, sem)
        load.start()
        into.append(load)

    fetch(*pairs[0], load_sems.at[0], loads)
    for pair in small_pairs:
        fetch(*pair, small_sem, smalls)
    def send(source, target, send_sem, recv_sem, place):
        pltpu.make_async_remote_copy(
            src_ref=source,
            dst_ref=target,
            send_sem=send_sem,
            recv_sem=recv_sem,
            device_id=place,
            device_id_type=pl.DeviceIdType.MESH,
        ).start()

    def chosen(mark, values):
        wide = jnp.concatenate([mark] * (feats // 128), axis=1)
        return jnp.sum(jnp.where(wide > 0.5, values.astype(F32), 0.0), axis=0, keepdims=True)

    for g in range(n_dp):
        picked = []
        for t in range(steps):
            for j in range(per):
                i = (g * per + j) * steps + t
                value = chosen(mark_ref[i], raw_ref[i])
                if vocab % ROW_TILE:
                    value += chosen(rest_mark_ref[i], rest_ref[...])
                picked.append(value)
        part_ref[g] = jnp.concatenate(picked, axis=0).astype(BF16)

    pl.semaphore_wait(barrier, len(routed) + plane * p)
    for k in range(1, n_tp):

        @pl.when(p >= k)
        def _():
            pl.semaphore_signal(
                ready, inc=1, device_id=along(-k), device_id_type=pl.DeviceIdType.MESH
            )


    for o in routed:
        send(part_ref.at[peer(o)[1]], rows_recv.at[p, here_plane], done, plane_sem, device(o))
    rows_recv[p, here_plane] = part_ref[d]

    owns[0].wait()
    owns[1].wait()
    parity = lax.rem(c, 2)
    mate = {"ctx": c + 1 - 2 * parity, "dp": d, "tp": p}
    half_ctx = n_ctx // 2
    blocks = [(a, b) for a in reversed(range(half_ctx)) for b in reversed(range(n_dp))]
    seg_recv[here_plane] = seg_own[...]
    send(seg_own, seg_mate, done, mate_sem, mate)
    for o in routed:
        send(seg_own, seg_recv.at[here_plane], done, seg_sem, device(o))
    picks = []
    for b in range(n_dp):
        target_group = lax.rem(d + b, n_dp)
        pick = jnp.int32(0)
        for j in range(per):
            local = dec_ref[target_group * per + j] - d * per
            pick += jnp.where((local >= 0) & (local < per), local, 0)
        picks.append(pick)
    loads[0].wait()
    for slot, (a, b) in enumerate(blocks):
        first = pl.multiple_of(lax.rem(mate["ctx"] + 2 * a, n_ctx) * chans, chans)
        state_send[slot] = state_in[picks[b], pl.ds(first, chans), :]
        send(state_send.at[slot], pair_recv.at[slot], done, pair_sems.at[slot], mate)

    for k in range(n_tp - 1, 0, -1):

        @pl.when(p >= k)
        def _():
            for place in whole_plane(-k):
                send(part_ref.at[place["dp"]], rows_recv.at[p, here_plane], done, line_sems.at[p], place)

    owns[2].wait()
    owns[3].wait()
    for o in across:
        send(xt_recv.at[d], xt_recv.at[d], done, xt_sem, device(o))
        send(bt_recv.at[d], bt_recv.at[d], done, bt_sem, device(o))
    for i, pair in enumerate(pairs[1:]):
        fetch(*pair, load_sems.at[i + 1], loads)

    fold = (
        lax.broadcasted_iota(jnp.int32, (dim, chans), 0)
        == lax.rem(lax.broadcasted_iota(jnp.int32, (dim, chans), 1), dim)
    ).astype(F32)
    head_rows = lax.broadcasted_iota(jnp.int32, (heads, chans), 0) == lax.div(
        lax.broadcasted_iota(jnp.int32, (heads, chans), 1), dim
    )

    def flat(value):
        return jnp.sum(jnp.where(head_rows, f32_dot(value, fold), 0.0), axis=0, keepdims=True)

    def full_lanes(value):
        idle = jnp.zeros((value.shape[0], 128 - value.shape[1]), F32)
        return jnp.concatenate([value, idle], axis=1) if idle.size else value

    def spread(value, first):
        count = value.shape[1]
        chosen = (
            lax.broadcasted_iota(jnp.int32, (count, chans), 0)
            == first + lax.div(lax.broadcasted_iota(jnp.int32, (count, chans), 1), dim)
        ).astype(F32)
        return f32_dot(value, chosen)

    drain(seg_mate, mate_sem)
    shrink = []
    for b in range(n_dp):
        row = pl.ds(picks[b], 1)
        shrink.append(jnp.exp(-jnp.where(parity == 0, seg_mate[row, :], seg_own[row, :])))
    shrink = full_lanes(jnp.concatenate(shrink, axis=0))
    for slot, (a, b) in enumerate(blocks):
        drain(pair_recv.at[slot], pair_sems.at[slot])
        first = pl.multiple_of(lax.rem(c + 2 * a, n_ctx) * chans, chans)
        turned = pltpu.roll(shrink, 128 - lax.rem(c + 2 * a, n_ctx) * heads, 1)
        sums = pair_send.at[slot] if a + b else state_recv.at[d * half_ctx + lax.div(c, 2)]
        for h in range(heads):
            spot = pl.ds(h * dim, dim)
            factor = turned[b : b + 1, h : h + 1]
            here = state_in[picks[b], pl.ds(pl.multiple_of(first + h * dim, dim), dim), :].astype(F32)
            there = pair_recv[slot, spot, :].astype(F32)
            left = jnp.broadcast_to(jnp.where(parity == 0, factor, 1.0), here.shape)
            right = jnp.broadcast_to(jnp.where(parity == 0, 1.0, factor), here.shape)
            sums[spot, :] = (left * here + right * there).astype(BF16)
        target = state_recv.at[d * half_ctx + lax.div(c, 2)]
        if a + b:
            send(pair_send.at[slot], target, done, state_sem, device((2 * a, b, 0)))

    drain(rows_recv.at[p, pl.ds(0, plane - 1)], plane_sem)
    def rows_of(e, i):
        piece = rows_recv[e, i].astype(F32)
        for g in range(1, n_dp):
            piece += rows_recv[e, g * n_ctx + i].astype(F32)
        return piece

    for i in range(n_ctx):
        line_send[i] = rows_of(p, i).astype(BF16)

    @pl.when(p < n_tp - 1)
    def _():
        pl.semaphore_wait(ready, n_tp - 1 - p)

    for k in range(n_tp - 1, 0, -1):

        @pl.when(p + k < n_tp)
        def _():
            send(line_send, rows_recv.at[p, pl.ds(0, n_ctx)], done, line_sems.at[p], along(k))

    loads[1].wait()
    tallies = []

    def take(values, e):
        spots = [pl.ds(pl.multiple_of((i * n_tp + e) * feats, feats), feats) for i in range(n_ctx)]
        held = jnp.concatenate(values, axis=1)
        gains = jnp.concatenate([gain_ref[:, spot] for spot in spots], axis=1)
        low = (held * gains).astype(BF16)
        weights = jnp.concatenate([wbc[:, spot] for spot in spots], axis=1)
        for i, spot in enumerate(spots):
            normed_ref[:, spot] = low[:, i * feats : (i + 1) * feats]
        square = held * held
        while square.shape[1] % 256 == 0:
            width = square.shape[1] // 2
            square = square[:, :width] + square[:, width:]
        tallies.append((square, nt_dot(low, weights)))


    for load in smalls:
        load.wait()
    take([rows_of(p, i) for i in range(n_ctx)], p)
    tap_rows = [flat(cxw_ref[k]) for k in range(taps)]
    bias_row = flat(cxb_ref[...])
    gate_row = flat(gg_ref[...])
    idle = jnp.zeros((1, total_heads - heads), F32)
    dtb_row = jnp.concatenate([dtb_ref[...], idle], axis=1)
    rate_row = jnp.concatenate([-jnp.exp(alog_ref[...]), idle], axis=1)
    skip_row = jnp.concatenate([skip_ref[...], idle], axis=1)

    holders = [lax.div(dec_ref[d * per + j], per) for j in range(per)]
    places = [lax.rem(dec_ref[d * per + j], per) for j in range(per)]
    for one, ref in ((xt_sem, xt_recv), (bt_sem, bt_recv)):
        if across:
            drain(ref.at[pl.ds(0, n_dp - 1)], one)
    plane_rows = lax.broadcasted_iota(jnp.int32, (per, 1), 0)
    for k in range(taps - 1):
        for j in range(per):
            r = k * per + j
            xfull[r : r + 1, :] = flat(xt_recv[holders[j], places[j], k].astype(F32))
            tail = bt_recv[holders[j], k].astype(F32)
            bcfull[r : r + 1, :] = jnp.sum(
                jnp.where(plane_rows == places[j], tail, 0.0), axis=0, keepdims=True
            )

    drain(seg_recv.at[pl.ds(0, plane - 1)], seg_sem)
    weights = []
    for j in range(per):
        after = jnp.zeros((1, tp_heads), F32)
        ordered = []
        row = pl.ds(places[j], 1)
        for m in reversed(range(half_ctx)):
            ordered.append(jnp.exp(-after))
            for k in (2 * m + 1, 2 * m):
                after = after + seg_recv[holders[j] * n_ctx + k, row, :]
        weights.extend(reversed(ordered))
    weights = pltpu.roll(full_lanes(jnp.concatenate(weights, axis=0)), 128 - c * heads, 1)

    for e in reversed(far):
        there = peer((0, 0, e))[2]

        @pl.when(there > p)
        def _():
            drain(rows_recv.at[there], line_sems.at[there])

        @pl.when(there < p)
        def _():
            drain(rows_recv.at[there, pl.ds(0, n_ctx)], line_sems.at[there])

        take([rows_of(there, i) for i in range(n_ctx)], there)
    square, narrow = tallies[0]
    for more, columns in tallies[1:]:
        square, narrow = square + more, narrow + columns
    scale = lax.rsqrt(jnp.sum(square, axis=1, keepdims=True) / model + epsilon)
    padded = jnp.concatenate([narrow * scale, jnp.zeros((rows, 128 - n_cols), F32)], axis=1)
    col_send[...] = pltpu.roll(padded, lax.rem(n_cols * mine, 128), 1)
    for o in group:
        send(col_send, col_recv.at[mine], done, col_sem, device(o))
    col_recv[mine] = col_send[...]
    loads[2].wait()
    x_rows = nt_dot(normed_ref[...], wzx[half : 2 * half, :]) * scale
    loads[3].wait()
    z_gate = silu(nt_dot(normed_ref[...], wzx[0:half, :]) * scale)

    lead = (taps - 1) * per
    xfull[lead : lead + rows, :] = x_rows
    conv = bias_row
    for k in range(taps):
        conv = conv + tap_rows[k] * xfull[k * per : k * per + rows, :]
    xc = silu(conv)

    drain(state_recv.at[pl.ds(0, n_dp * half_ctx - 1)], state_sem)
    for j in range(per):
        for h in range(heads):
            spot = pl.ds(h * dim, dim)
            begin = None
            for m in range(half_ctx):
                r = j * half_ctx + m
                term = state_recv[holders[j] * half_ctx + m, spot, :].astype(F32)
                term = jnp.broadcast_to(weights[r : r + 1, h : h + 1], term.shape) * term
                begin = term if begin is None else begin + term
            start_state[j, spot, :] = begin
            start_low[j, spot, :] = begin.astype(BF16)

    drain(col_recv.at[pl.ds(0, ring - 1)], col_sem)
    lanes = lax.broadcasted_iota(jnp.int32, (rows, 128), 1)
    blocks_of = []
    for v in range(-(-all_cols // 128)):
        block = jnp.zeros((rows, 128), F32)
        for i in range(ring):
            low = n_cols * i - 128 * v
            if low < 128 and low + n_cols > 0:
                block = jnp.where((lanes >= low) & (lanes < low + n_cols), col_recv[i], block)
        blocks_of.append(block)
    columns = jnp.concatenate(blocks_of, axis=1)
    bcfull[lead : lead + rows, :] = columns[:, :width]
    head_first = (p * n_ctx + c) * heads
    dt_raw = pltpu.roll(columns[:, width:all_cols], total_heads - head_first, 1)
    step_size = softplus(dt_raw + dtb_row)
    row_of = lax.broadcasted_iota(jnp.int32, (rows, 1), 0)

    def later(value, k):
        return pltpu.roll(value, k * per, 0) if k else value

    total = step_size * rate_row
    k = 1
    while k < steps:
        total = total + jnp.where(row_of >= k * per, later(total, k), 0.0)
        k *= 2
    conv = cbb_ref[...]
    for k in range(taps):
        conv = conv + cbw_ref[k : k + 1, :] * bcfull[k * per : k * per + rows, :]
    bcc = silu(conv)
    b_all, c_all = bcc[:, :state_n], bcc[:, state_n:]

    row_slot = lax.rem(row_of, per)
    from_start = jnp.zeros((rows, chans), F32)
    c_low = c_all.astype(BF16)
    for j in range(per):
        from_start += jnp.where(row_slot == j, nt_dot(c_low, start_low[j]), 0.0)

    def by_head(value):
        if 128 % dim or chans % 128:
            return spread(value, 0)
        packed = 128 // dim
        out = []
        for m in range(chans // 128):
            part = jnp.broadcast_to(value[:, m * packed : m * packed + 1], (rows, 128))
            for q in range(1, packed):
                one = value[:, m * packed + q : m * packed + q + 1]
                part = jnp.where(lanes >= q * dim, one, part)
            out.append(part)
        return jnp.concatenate(out, axis=1)

    def at(value, t):
        return value[t * per : (t + 1) * per]

    y = by_head(jnp.exp(total)) * from_start
    for k in range(steps):
        overlap = jnp.sum(later(b_all, k) * c_all, axis=1, keepdims=True)
        if k:
            valid = row_of >= k * per
            decay = jnp.exp(jnp.where(valid, total - later(total, k), 0.0))
            share = jnp.where(valid, decay * overlap * later(step_size, k), 0.0)
        else:
            share = step_size * overlap + skip_row
        y = y + by_head(share) * later(xc, k)
    gated = y * z_gate
    diagonal = lax.broadcasted_iota(jnp.int32, (rows, 128), 0) == lax.broadcasted_iota(
        jnp.int32, (rows, 128), 1
    )
    loads[4].wait()
    scaled = (gated * gate_row).astype(BF16)
    base = lax.div(c, 2) * 2
    pieces = []
    for e in far + [0]:
        chips = [[(2 * m, q, e) for q in range(2)] for m in reversed(range(half_ctx))]
        pieces.extend(chips if e == far[0] else [sum(chips, [])])
    for number, piece in enumerate(pieces):
        there = peer((0, 0, piece[0][2]))[2]
        goals = [lax.rem(base + m + q, n_ctx) for m, q, _ in piece]
        cuts = [wout[:, pl.ds(pl.multiple_of((a * n_tp + there) * feats, feats), feats)] for a in goals]
        partial = jnp.dot(scaled, jnp.concatenate(cuts, axis=1), preferred_element_type=F32)
        for i, a in enumerate(goals):
            out_send[there * n_ctx + a] = partial[:, i * feats : (i + 1) * feats].astype(BF16)
        for a, (m, _, e) in zip(goals, piece):
            place = {"ctx": a, "dp": d, "tp": there}
            spot = there * n_ctx + a
            if m + e:
                send(out_send.at[spot], out_recv.at[mine], done, out_sem, place)
        if number == half_ctx - 1:
            squares = jnp.sum(gated * gated, axis=1, keepdims=True)
            sq_send[...] = jnp.sum(jnp.where(diagonal, squares, 0.0), axis=0, keepdims=True)
            for o in group:
                send(sq_send, sq_recv.at[mine], done, sq_sem, device(o))
            sq_recv[mine] = sq_send[...]
    send(out_send.at[p * n_ctx + mate["ctx"]], out_recv.at[mine], done, out_sem, mate)
    out_recv[mine] = out_send[p * n_ctx + c]

    last = jnp.concatenate([at(total, steps - 1)] * steps, axis=0)
    late = by_head(jnp.exp(last - total) * step_size) * xc
    flat_rows = jnp.concatenate([late, by_head(jnp.exp(last))], axis=0)
    tall = jnp.transpose(flat_rows)
    for j in range(per):
        b_own = jnp.where(row_slot == j, b_all, 0.0)
        final_ref[j] = (
            tall[:, rows + j : rows + j + 1] * start_state[j] + f32_dot(tall[:, :rows], b_own)
        )

    drain(rows_recv.at[p, pl.ds(0, plane - 1)], done)
    for k in range(1, n_tp):

        @pl.when(p >= k)
        def _():
            drain(rows_recv.at[p], done)

        @pl.when(p + k < n_tp)
        def _():
            drain(line_send, done)

    drain(seg_recv.at[pl.ds(0, plane - 1)], done)
    drain(seg_mate, done)
    drain(state_send, done)
    drain(pair_send.at[pl.ds(0, len(blocks) - 1)], done)
    if across:
        drain(xt_recv.at[pl.ds(0, n_dp - 1)], done)
        drain(bt_recv.at[pl.ds(0, n_dp - 1)], done)
    drain(col_recv.at[pl.ds(0, ring - 1)], done)
    drain(sq_recv.at[pl.ds(0, ring - 1)], done)
    drain(out_recv.at[pl.ds(0, ring - 1)], done)

    drain(sq_recv.at[pl.ds(0, ring - 1)], sq_sem)
    total_squares = sq_recv[0]
    for i in range(1, ring):
        total_squares = total_squares + sq_recv[i]
    total_squares = jnp.sum(jnp.where(diagonal, total_squares, 0.0), axis=1, keepdims=True)
    inverse = lax.rsqrt(total_squares / (total_heads * dim) + epsilon)
    drain(out_recv.at[pl.ds(0, ring - 1)], out_sem)
    mixed = out_recv[0].astype(F32)
    for i in range(1, ring):
        mixed = mixed + out_recv[i].astype(F32)
    mixed = mixed * inverse
    for t in range(steps):
        mixed_ref[t] = at(mixed, t).astype(BF16)


def tail_kernel(mixed_in, final_in, mixed_out, final_out, sems):
    copies = [
        pltpu.make_async_copy(final_in.at[j], final_out.at[j], sems.at[j])
        for j in range(final_in.shape[0])
    ]
    copies.append(pltpu.make_async_copy(mixed_in, mixed_out, sems.at[len(copies)]))
    for copy in copies:
        copy.start()
    for copy in copies:
        copy.wait()


def kernel_device(
    sizes,
    token_ids,
    decode_prompt,
    embedding,
    norm_gain,
    w_zx,
    w_bcdt,
    conv_x_weight,
    conv_x_bias,
    conv_bc_weight,
    conv_bc_bias,
    dt_bias,
    a_log,
    d_skip,
    gate_norm_gain,
    w_out,
    state_parts,
    seg_rate,
    x_tail,
    bc_tail,
):
    n_ctx, n_dp, n_tp, _ = sizes
    steps = token_ids.shape[0]
    slots = decode_prompt.shape[0]
    per = state_parts.shape[1]
    rows = steps * per
    vocab, feats = embedding.shape
    heads, dim, model = w_zx.shape[1:]
    chans = heads * dim
    tp_heads, state_n = state_parts.shape[2], state_parts.shape[4]
    ring, plane, blocks = n_ctx * n_tp, n_dp * n_ctx, n_dp * (n_ctx // 2)
    smem = pl.BlockSpec(memory_space=pltpu.SMEM)
    vmem = pl.BlockSpec(memory_space=pltpu.VMEM)
    anywhere = pl.BlockSpec(memory_space=pl.ANY)
    sem = pltpu.SemaphoreType.DMA
    rest = max(1, vocab % ROW_TILE)
    picked = pl.pallas_call(
        functools.partial(gather_kernel, steps, slots),
        out_shape=(
            pltpu.VMEM((steps * slots, ROW_TILE, feats), BF16),
            pltpu.VMEM((rest, feats), BF16),
            pltpu.VMEM((steps * slots, ROW_TILE, 128), F32),
            pltpu.VMEM((steps * slots, rest, 128), F32),
        ),
        in_specs=[smem, smem, anywhere],
        out_specs=(vmem,) * 4,
        scratch_shapes=[sem, sem],
        name="gather_rows",
    )(token_ids, decode_prompt, embedding)
    wide = 2 * state_n
    full_rows = -(-(conv_x_weight.shape[0] - 1 + steps) * per // 8) * 8
    smalls = (
        norm_gain[None],
        conv_x_weight,
        conv_x_bias,
        conv_bc_weight,
        conv_bc_bias[None],
        dt_bias[None],
        a_log[None],
        d_skip[None],
        gate_norm_gain,
    )
    bc_planes = jnp.swapaxes(bc_tail, 0, 1)
    mixed, final = pl.pallas_call(
        functools.partial(mixer_kernel, sizes, vocab),
        out_shape=(
            pltpu.VMEM((steps, per, feats), BF16),
            pltpu.VMEM((per, chans, state_n), F32),
        ),
        in_specs=[anywhere] + [vmem] * 4 + [anywhere] * 16,
        out_specs=(vmem, vmem),
        scratch_shapes=[
            pltpu.SMEM((slots,), jnp.int32),
            pltpu.VMEM((n_dp, rows, feats), BF16),
            *[pltpu.VMEM(small.shape, small.dtype) for small in smalls],
            pltpu.VMEM((blocks, chans, state_n), BF16),
            pltpu.VMEM((blocks, chans, state_n), BF16),
            pltpu.VMEM((2 * chans, model), BF16),
            pltpu.VMEM(w_bcdt.shape[::-1], BF16),
            pltpu.VMEM((chans, model), BF16),
            pltpu.VMEM((per, tp_heads * dim, state_n), BF16),
            pltpu.VMEM((blocks, chans, state_n), BF16),
            pltpu.VMEM((blocks, chans, state_n), BF16),
            pltpu.VMEM((n_tp, plane, rows, feats), BF16),
            pltpu.VMEM((n_ctx, rows, feats), BF16),
            pltpu.VMEM((plane, per, tp_heads), F32),
            pltpu.VMEM((per, tp_heads), F32),
            pltpu.VMEM((per, tp_heads), F32),
            pltpu.VMEM((n_dp,) + x_tail.shape, BF16),
            pltpu.VMEM((n_dp,) + bc_planes.shape, BF16),
            pltpu.VMEM((rows, 128), F32),
            pltpu.VMEM((ring, rows, 128), F32),
            pltpu.VMEM((1, 128), F32),
            pltpu.VMEM((ring, 1, 128), F32),
            pltpu.VMEM((ring, rows, feats), BF16),
            pltpu.VMEM((ring, rows, feats), BF16),
            pltpu.VMEM((per, chans, state_n), F32),
            pltpu.VMEM((per, chans, state_n), BF16),
            pltpu.VMEM((rows, model), BF16),
            pltpu.VMEM((full_rows, chans), F32),
            pltpu.VMEM((full_rows, wide), F32),
            sem((5,)),
            sem,
            sem((2,)),
            sem((blocks,)),
            *[sem] * 3,
            sem((n_tp,)),
            *[sem] * 7,
            pltpu.SemaphoreType.REGULAR,
        ],
        compiler_params=pltpu.CompilerParams(
            collective_id=0, has_side_effects=True, vmem_limit_bytes=56 * 1024 * 1024
        ),
        name="mixer",
    )(
        decode_prompt,
        *[pltpu.with_memory_space_constraint(value, pltpu.VMEM) for value in picked],
        seg_rate,
        x_tail,
        bc_planes,
        *smalls,
        w_zx.reshape(2 * chans, model),
        w_bcdt.T,
        w_out.reshape(chans, model),
        state_parts.reshape(per, tp_heads * dim, state_n),
    )
    mixed, final = pl.pallas_call(
        tail_kernel,
        out_shape=(
            jax.ShapeDtypeStruct(mixed.shape, BF16),
            jax.ShapeDtypeStruct(final.shape, F32),
        ),
        in_specs=[anywhere] * 2,
        out_specs=(anywhere, anywhere),
        scratch_shapes=[sem((per + 1,))],
        name="tail",
    )(
        pltpu.with_memory_space_constraint(mixed, pltpu.VMEM),
        pltpu.with_memory_space_constraint(final, pltpu.VMEM),
    )
    return mixed, final.reshape(per, heads, dim, state_n)


def choose_device(sizes, *args):
    embedding, w_zx, w_bcdt = args[2], args[4], args[5]
    heads, dim = w_zx.shape[1:3]
    fits = (
        embedding.shape[1] % 128 == 0
        and sizes[0] % 2 == 0
        and (heads * dim) % 128 == 0
        and w_bcdt.shape[1] <= 128
        and embedding.shape[0] >= ROW_TILE
        and args[15].shape[2] <= 128
    )
    if fits:
        return kernel_device(sizes, *args)
    return per_device(*args)


def solution(mesh):
    sizes = (mesh.shape["ctx"], mesh.shape["dp"], mesh.shape["tp"], HEADS)
    return jax.shard_map(
        functools.partial(choose_device, sizes),
        mesh=mesh,
        in_specs=(
            P(),
            P(),
            P("dp", ("ctx", "tp")),
            P(),
            P(None, ("tp", "ctx"), None, None),
            P(None, ("ctx", "tp")),
            P(None, ("tp", "ctx"), None),
            P(("tp", "ctx"), None),
            P(),
            P(),
            P(("tp", "ctx")),
            P(("tp", "ctx")),
            P(("tp", "ctx")),
            P(("tp", "ctx"), None),
            P(("tp", "ctx"), None, None),
            P("ctx", "dp", "tp", None, None),
            P("ctx", "dp", "tp"),
            P("dp", None, ("tp", "ctx"), None),
            P("dp", None, None),
        ),
        out_specs=(P(None, "dp", ("ctx", "tp")), P("dp", ("tp", "ctx"), None, None)),
        check_vma=False,
    )
```

```python
import functools

import jax
import jax.numpy as jnp
from jax import lax
from jax.experimental import pallas as pl
from jax.experimental.pallas import tpu as pltpu
from jax.sharding import PartitionSpec as P

HEADS = 128
HEAD_DIM = 64


epsilon = 1e-05


def entering(shard, axis, combine, identity):
    count, here = (lax.axis_size(axis), lax.axis_index(axis))
    everything = lax.all_gather(shard, axis)
    start = jnp.broadcast_to(jnp.asarray(identity, shard.dtype), shard.shape)

    def step(k, before):
        at = count - 1 - k
        reached = at > here
        new = combine(before, everything[at])
        return jnp.where(reached, new, before)

    return lax.fori_loop(0, count, step, start)


def rms_scale(values, gain):
    return values * lax.rsqrt(jnp.mean(values * values, axis=-1, keepdims=True) + epsilon) * gain


def select_rows(picker, values):
    return jnp.tensordot(picker, values, axes=1, precision=lax.Precision.HIGHEST)


def add_rates(earlier, later_one):
    return earlier + later_one


def per_device(
    token_ids,
    decode_prompt,
    embedding,
    norm_gain,
    w_zx,
    w_bcdt,
    conv_x_weight,
    conv_x_bias,
    conv_bc_weight,
    conv_bc_bias,
    dt_bias,
    a_log,
    d_skip,
    gate_norm_gain,
    w_out,
    state_parts,
    seg_rate,
    x_tail,
    bc_tail,
):
    group = lax.axis_index("dp")
    local_count = state_parts.shape[1]
    slot_count = decode_prompt.shape[0]
    head_count = w_zx.shape[1]
    state_width = conv_bc_bias.shape[0] // 2
    after_rates = entering(seg_rate, "ctx", add_rates, jnp.zeros_like(seg_rate))
    seg_weight = jnp.exp(-after_rates[0])
    scaled = seg_weight[:, :, None, None] * state_parts[0].astype(jnp.float32)
    channel_sums = lax.psum_scatter(
        scaled.astype(jnp.bfloat16), "ctx", scatter_dimension=2, tiled=True
    ).astype(jnp.float32)
    combined = lax.all_to_all(
        channel_sums.astype(jnp.bfloat16), "ctx", split_axis=1, concat_axis=2, tiled=True
    ).astype(channel_sums.dtype)
    tails_x = x_tail.astype(jnp.float32)
    tails_bc = bc_tail.astype(jnp.float32)
    own_slots = lax.dynamic_slice_in_dim(decode_prompt, group * local_count, local_count)
    prompt_ids = jnp.arange(slot_count, dtype=jnp.int32)
    every_state, every_x, every_bc = (
        lax.all_gather(combined.astype(jnp.bfloat16), "dp", axis=0, tiled=True).astype(
            combined.dtype
        ),
        lax.all_gather(tails_x.astype(jnp.bfloat16), "dp", axis=0, tiled=True).astype(
            tails_x.dtype
        ),
        lax.all_gather(tails_bc.astype(jnp.bfloat16), "dp", axis=0, tiled=True).astype(
            tails_bc.dtype
        ),
    )
    picker = (own_slots[:, None] == prompt_ids[None, :]).astype(jnp.float32)
    ssm_state = select_rows(picker, every_state)
    x_window = select_rows(picker, every_x)
    bc_window = select_rows(picker, every_bc)
    vocab_rows = embedding.shape[0]
    holder = (decode_prompt[:, None] == prompt_ids[None, :]).astype(jnp.int32)
    slot_tokens = jnp.sum(token_ids[:, None, :] * holder[None], axis=2)
    offset_tokens = slot_tokens - group * vocab_rows
    inside = (offset_tokens >= 0) & (offset_tokens < vocab_rows)
    looked = jnp.take(embedding, jnp.clip(offset_tokens, 0, vocab_rows - 1), axis=0)
    partial_rows = jnp.where(inside[..., None], looked.astype(jnp.float32), 0.0)
    own_rows = lax.psum_scatter(
        partial_rows.astype(jnp.bfloat16), "dp", scatter_dimension=1, tiled=True
    )
    embedded = lax.all_gather(own_rows, ("ctx", "tp"), axis=2, tiled=True)
    steps_count = embedded.shape[0]
    flat_rows = embedded.reshape(-1, embedded.shape[2]).astype(jnp.float32)
    normed = rms_scale(flat_rows, norm_gain).astype(jnp.bfloat16)
    projected = jnp.einsum("rd,khed->krhe", normed, w_zx, preferred_element_type=jnp.float32)
    projected = projected.reshape(
        2, steps_count, local_count, projected.shape[2], projected.shape[3]
    )
    columns = lax.all_gather(
        jnp.dot(normed, w_bcdt, preferred_element_type=jnp.float32),
        ("ctx", "tp"),
        axis=1,
        tiled=True,
    )
    columns = columns.reshape(steps_count, local_count, -1)
    head_block = lax.axis_index("tp") * lax.axis_size("ctx") + lax.axis_index("ctx")
    head_start = 2 * state_width + head_block * head_count
    dt_raw = lax.dynamic_slice_in_dim(columns, head_start, head_count, 2)
    decay_rate = -jnp.exp(a_log)
    gated_steps = []
    for moment in range(steps_count):
        x_window = jnp.concatenate([x_window, projected[1, moment][:, None]], axis=1)
        bc_window = jnp.concatenate(
            [bc_window, columns[moment, :, None, : 2 * state_width]], axis=1
        )
        x_conv = jax.nn.silu(jnp.einsum("pkhe,khe->phe", x_window, conv_x_weight) + conv_x_bias)
        bc_conv = jax.nn.silu(jnp.einsum("pkn,kn->pn", bc_window, conv_bc_weight) + conv_bc_bias)
        step_size = jax.nn.softplus(dt_raw[moment] + dt_bias)
        retain = jnp.exp(step_size * decay_rate)
        ssm_state = (
            retain[:, :, None, None] * ssm_state
            + (step_size[:, :, None] * x_conv)[:, :, :, None] * bc_conv[:, None, None, :state_width]
        )
        output = (
            jnp.einsum("phen,pn->phe", ssm_state, bc_conv[:, state_width:])
            + d_skip[None, :, None] * x_conv
        )
        gated_steps.append(output * jax.nn.silu(projected[0, moment]))
        x_window = x_window[:, 1:]
        bc_window = bc_window[:, 1:]
    gated_all = jnp.stack(gated_steps)
    local_squares = jnp.sum(gated_all * gated_all, axis=(2, 3))
    total_squares = lax.psum(local_squares, ("ctx", "tp"))
    inverse = lax.rsqrt(total_squares / (HEADS * HEAD_DIM) + epsilon)
    normed_out = (gated_all * inverse[:, :, None, None] * gate_norm_gain).astype(jnp.bfloat16)
    partial_out = jnp.einsum("tphe,hed->tpd", normed_out, w_out, preferred_element_type=jnp.float32)
    outer_sum = lax.psum_scatter(
        partial_out.astype(jnp.bfloat16), "ctx", scatter_dimension=2, tiled=True
    ).astype(jnp.float32)
    mixed = lax.psum_scatter(outer_sum, "tp", scatter_dimension=2, tiled=True)
    return (mixed.astype(jnp.bfloat16), ssm_state)


HI = lax.Precision.HIGHEST
F32 = jnp.float32
BF16 = jnp.bfloat16


def f32_dot(a, b):
    return jnp.dot(a, b, precision=HI, preferred_element_type=F32)


def nt_dot(a, b):
    return lax.dot_general(a, b, (((1,), (1,)), ((), ())), preferred_element_type=F32)


def silu(v):
    return v / (1.0 + jnp.exp(-v))


def softplus(v):
    return jnp.maximum(v, 0.0) + jnp.log1p(jnp.exp(-jnp.abs(v)))


ROW_TILE = 8


def drain(ref, sem):
    pltpu.make_async_copy(ref, ref, sem).wait()


def row_place(steps, tok_ref, dec_ref, vocab, s, t):
    whole = vocab // ROW_TILE * ROW_TILE
    row = tok_ref[t, dec_ref[s]] - lax.axis_index("dp") * vocab
    held = (row >= 0) & (row < whole)
    start = pl.multiple_of(lax.bitwise_and(jnp.where(held, row, 0), -ROW_TILE), ROW_TILE)
    return row, held, start


def gather_kernel(
    steps, slots, tok_ref, dec_ref, emb_ref, buf, tail, mark, tail_mark, sem, tail_sem
):
    vocab = emb_ref.shape[0]
    whole = vocab // ROW_TILE * ROW_TILE
    where = []

    def block(i, start):
        return pltpu.make_async_copy(emb_ref.at[pl.ds(start, ROW_TILE)], buf.at[i], sem)

    def rest():
        return pltpu.make_async_copy(emb_ref.at[pl.ds(whole, vocab - whole)], tail, tail_sem)

    in_tail = False
    for s in range(slots):
        for t in range(steps):
            row, held, start = row_place(steps, tok_ref, dec_ref, vocab, s, t)
            i = s * steps + t

            @pl.when(held)
            def _():
                block(i, start).start()

            where.append((row, start, held))
            in_tail |= (row >= whole) & (row < vocab)
    if whole < vocab:

        @pl.when(in_tail)
        def _():
            rest().start()

    tile_rows = lax.broadcasted_iota(jnp.int32, mark.shape[1:], 0)
    tail_rows = whole + lax.broadcasted_iota(jnp.int32, tail_mark.shape[1:], 0)
    for i, (row, start, held) in enumerate(where):
        mark[i] = (held & (tile_rows == row - start)).astype(F32)
        tail_mark[i] = (tail_rows == jnp.where(row < vocab, row, -1)).astype(F32)

    for i, (row, start, held) in enumerate(where):

        @pl.when(held)
        def _():
            block(i, start).wait()

    if whole < vocab:

        @pl.when(in_tail)
        def _():
            rest().wait()


def mixer_kernel(
    sizes,
    vocab,
    dec_hbm,
    raw_ref,
    rest_ref,
    mark_ref,
    rest_mark_ref,
    seg_hbm,
    xt_hbm,
    bt_hbm,
    gain_hbm,
    cxw_hbm,
    cxb_hbm,
    cbw_hbm,
    cbb_hbm,
    dtb_hbm,
    alog_hbm,
    skip_hbm,
    gg_hbm,
    wzx_hbm,
    wbc_hbm,
    wout_hbm,
    state_hbm,
    mixed_ref,
    final_ref,
    dec_ref,
    part_ref,
    gain_ref,
    cxw_ref,
    cxb_ref,
    cbw_ref,
    cbb_ref,
    dtb_ref,
    alog_ref,
    skip_ref,
    gg_ref,
    pair_recv,
    pair_send,
    wzx,
    wbc,
    wout,
    state_in,
    state_send,
    state_recv,
    rows_recv,
    line_send,
    seg_recv,
    seg_mate,
    seg_own,
    xt_recv,
    bt_recv,
    col_send,
    col_recv,
    sq_send,
    sq_recv,
    out_send,
    out_recv,
    start_state,
    start_low,
    normed_ref,
    xfull,
    bcfull,
    state_load,
    weight_sem,
    small_sem,
    own_sems,
    pair_sems,
    mate_sem,
    state_sem,
    plane_sem,
    line_sems,
    seg_sem,
    xt_sem,
    bt_sem,
    col_sem,
    sq_sem,
    out_sem,
    done,
    ready,
):
    n_ctx, n_dp, n_tp, total_heads = sizes
    c, d, p = lax.axis_index("ctx"), lax.axis_index("dp"), lax.axis_index("tp")
    mine = c * n_tp + p
    here_plane = d * n_ctx + c
    ring, plane = n_ctx * n_tp, n_dp * n_ctx
    steps, per, feats = mixed_ref.shape
    rows = steps * per
    heads, dim = cxb_ref.shape
    chans = heads * dim
    width = cbb_ref.shape[1]
    state_n = width // 2
    taps = cxw_ref.shape[0]
    model = gain_ref.shape[1]
    tp_heads = seg_recv.shape[-1]
    n_cols = wbc_hbm.shape[0]
    all_cols = n_cols * n_ctx * n_tp
    half = wzx_hbm.shape[0] // 2
    mirror = n_tp == 4

    def peer(offset):
        dc, dd, dt = offset
        away = lax.rem(p + dt, n_tp)
        if mirror and dt != n_tp // 2:
            away = n_tp - 1 - (p if dt == 1 else lax.rem(p + n_tp // 2, n_tp))
        return lax.rem(c + dc, n_ctx), lax.rem(d + dd, n_dp), away if dt else p

    def device(offset):
        a, b, e = peer(offset)
        return {"ctx": a, "dp": b, "tp": e}

    def along(k):
        return {"ctx": c, "dp": d, "tp": lax.rem(p + k + n_tp, n_tp)}

    def whole_plane(k):
        return [
            {"ctx": a, "dp": b, "tp": lax.rem(p + k + n_tp, n_tp)}
            for a, b, _ in [peer((a, b, 0)) for a in reversed(range(n_ctx)) for b in reversed(range(n_dp))]
        ]

    far = [1, 2, 3] if mirror else list(range(n_tp - 1, 0, -1))
    routed = [(a, b, 0) for a in reversed(range(n_ctx)) for b in reversed(range(n_dp)) if a + b]
    group = [(a, 0, e) for e in far + [0] for a in reversed(range(n_ctx)) if a + e]
    across = [(0, b, 0) for b in range(1, n_dp)]

    for e in range(n_tp):
        rows_recv[e, n_ctx:] = jnp.zeros((plane - n_ctx, rows, feats), BF16)
    barrier = pltpu.get_barrier_semaphore()
    for k in range(n_tp - 1, 0, -1):

        @pl.when(p + k < n_tp)
        def _():
            for place in whole_plane(k):
                pl.semaphore_signal(
                    barrier, inc=1, device_id=place, device_id_type=pl.DeviceIdType.MESH
                )


    for o in routed:
        pl.semaphore_signal(
            barrier, inc=1, device_id=device(o), device_id_type=pl.DeviceIdType.MESH
        )

    owns = []
    for source, target in (
        (dec_hbm, dec_ref),
        (seg_hbm.at[0], seg_own),
        (xt_hbm, xt_recv.at[d]),
        (bt_hbm, bt_recv.at[d]),
    ):
        load = pltpu.make_async_copy(source, target, own_sems.at[len(owns) // 2])
        load.start()
        owns.append(load)
    loads = []
    smalls = []
    pairs = (
        (state_hbm, state_in),
        (wbc_hbm, wbc),
        (wzx_hbm.at[pl.ds(half, half)], wzx.at[pl.ds(half, half)]),
        (wzx_hbm.at[pl.ds(0, half)], wzx.at[pl.ds(0, half)]),
        (wout_hbm, wout),
    )
    small_pairs = (
        (gain_hbm, gain_ref),
        (cxw_hbm, cxw_ref),
        (cxb_hbm, cxb_ref),
        (cbw_hbm, cbw_ref),
        (cbb_hbm, cbb_ref),
        (dtb_hbm, dtb_ref),
        (alog_hbm, alog_ref),
        (skip_hbm, skip_ref),
        (gg_hbm, gg_ref),
    )

    def fetch(source, target, sem, into):
        load = pltpu.make_async_copy(source, target, sem)
        load.start()
        into.append(load)

    fetch(*pairs[0], state_load, loads)
    for pair in small_pairs + pairs[1:2]:
        fetch(*pair, small_sem, smalls)
    def send(source, target, send_sem, recv_sem, place):
        pltpu.make_async_remote_copy(
            src_ref=source,
            dst_ref=target,
            send_sem=send_sem,
            recv_sem=recv_sem,
            device_id=place,
            device_id_type=pl.DeviceIdType.MESH,
        ).start()

    def chosen(mark, values):
        wide = jnp.concatenate([mark] * (feats // 128), axis=1)
        return jnp.sum(jnp.where(wide > 0.5, values.astype(F32), 0.0), axis=0, keepdims=True)

    for g in range(n_dp):
        picked = []
        for t in range(steps):
            for j in range(per):
                i = (g * per + j) * steps + t
                value = chosen(mark_ref[i], raw_ref[i])
                if vocab % ROW_TILE:
                    value += chosen(rest_mark_ref[i], rest_ref[...])
                picked.append(value)
        part_ref[g] = jnp.concatenate(picked, axis=0).astype(BF16)

    pl.semaphore_wait(barrier, len(routed) + plane * p)
    for k in range(1, n_tp):

        @pl.when(p >= k)
        def _():
            pl.semaphore_signal(
                ready, inc=1, device_id=along(-k), device_id_type=pl.DeviceIdType.MESH
            )


    for o in routed:
        send(part_ref.at[peer(o)[1]], rows_recv.at[p, here_plane], done, plane_sem, device(o))
    rows_recv[p, here_plane] = part_ref[d]

    owns[0].wait()
    owns[1].wait()
    parity = lax.rem(c, 2)
    mate = {"ctx": c + 1 - 2 * parity, "dp": d, "tp": p}
    half_ctx = n_ctx // 2
    blocks = [(a, b) for a in reversed(range(half_ctx)) for b in reversed(range(n_dp))]
    seg_recv[here_plane] = seg_own[...]
    send(seg_own, seg_mate, done, mate_sem, mate)
    for o in routed:
        send(seg_own, seg_recv.at[here_plane], done, seg_sem, device(o))
    picks = []
    for b in range(n_dp):
        target_group = lax.rem(d + b, n_dp)
        pick = jnp.int32(0)
        for j in range(per):
            local = dec_ref[target_group * per + j] - d * per
            pick += jnp.where((local >= 0) & (local < per), local, 0)
        picks.append(pick)
    loads[0].wait()
    for slot, (a, b) in enumerate(blocks):
        first = pl.multiple_of(lax.rem(mate["ctx"] + 2 * a, n_ctx) * chans, chans)
        state_send[slot] = state_in[picks[b], pl.ds(first, chans), :]
        send(state_send.at[slot], pair_recv.at[slot], done, pair_sems.at[slot], mate)

    for k in range(n_tp - 1, 0, -1):

        @pl.when(p >= k)
        def _():
            for place in whole_plane(-k):
                send(part_ref.at[place["dp"]], rows_recv.at[p, here_plane], done, line_sems.at[p], place)

    owns[2].wait()
    owns[3].wait()
    for o in across:
        send(xt_recv.at[d], xt_recv.at[d], done, xt_sem, device(o))
        send(bt_recv.at[d], bt_recv.at[d], done, bt_sem, device(o))
    for pair in pairs[2:]:
        fetch(*pair, weight_sem, loads)

    fold = (
        lax.broadcasted_iota(jnp.int32, (dim, chans), 0)
        == lax.rem(lax.broadcasted_iota(jnp.int32, (dim, chans), 1), dim)
    ).astype(F32)
    head_rows = lax.broadcasted_iota(jnp.int32, (heads, chans), 0) == lax.div(
        lax.broadcasted_iota(jnp.int32, (heads, chans), 1), dim
    )

    def flat(value):
        return jnp.sum(jnp.where(head_rows, f32_dot(value, fold), 0.0), axis=0, keepdims=True)

    def full_lanes(value):
        idle = jnp.zeros((value.shape[0], 128 - value.shape[1]), F32)
        return jnp.concatenate([value, idle], axis=1) if idle.size else value

    def spread(value, first):
        count = value.shape[1]
        chosen = (
            lax.broadcasted_iota(jnp.int32, (count, chans), 0)
            == first + lax.div(lax.broadcasted_iota(jnp.int32, (count, chans), 1), dim)
        ).astype(F32)
        return f32_dot(value, chosen)

    drain(seg_mate, mate_sem)
    shrink = []
    for b in range(n_dp):
        row = pl.ds(picks[b], 1)
        shrink.append(jnp.exp(-jnp.where(parity == 0, seg_mate[row, :], seg_own[row, :])))
    shrink = full_lanes(jnp.concatenate(shrink, axis=0))
    for slot, (a, b) in enumerate(blocks):
        drain(pair_recv.at[slot], pair_sems.at[slot])
        first = pl.multiple_of(lax.rem(c + 2 * a, n_ctx) * chans, chans)
        turned = pltpu.roll(shrink, 128 - lax.rem(c + 2 * a, n_ctx) * heads, 1)
        sums = pair_send.at[slot] if a + b else state_recv.at[d * half_ctx + lax.div(c, 2)]
        for h in range(heads):
            spot = pl.ds(h * dim, dim)
            factor = turned[b : b + 1, h : h + 1]
            here = state_in[picks[b], pl.ds(pl.multiple_of(first + h * dim, dim), dim), :].astype(F32)
            there = pair_recv[slot, spot, :].astype(F32)
            left = jnp.broadcast_to(jnp.where(parity == 0, factor, 1.0), here.shape)
            right = jnp.broadcast_to(jnp.where(parity == 0, 1.0, factor), here.shape)
            sums[spot, :] = (left * here + right * there).astype(BF16)
        target = state_recv.at[d * half_ctx + lax.div(c, 2)]
        if a + b:
            send(pair_send.at[slot], target, done, state_sem, device((2 * a, b, 0)))

    drain(rows_recv.at[p, pl.ds(0, plane - 1)], plane_sem)
    def rows_of(e, i):
        piece = rows_recv[e, i].astype(F32)
        for g in range(1, n_dp):
            piece += rows_recv[e, g * n_ctx + i].astype(F32)
        return piece

    for i in range(n_ctx):
        line_send[i] = rows_of(p, i).astype(BF16)

    @pl.when(p < n_tp - 1)
    def _():
        pl.semaphore_wait(ready, n_tp - 1 - p)

    for k in range(n_tp - 1, 0, -1):

        @pl.when(p + k < n_tp)
        def _():
            send(line_send, rows_recv.at[p, pl.ds(0, n_ctx)], done, line_sems.at[p], along(k))

    tallies = []

    def take(values, e):
        spots = [pl.ds(pl.multiple_of((i * n_tp + e) * feats, feats), feats) for i in range(n_ctx)]
        held = jnp.concatenate(values, axis=1)
        gains = jnp.concatenate([gain_ref[:, spot] for spot in spots], axis=1)
        low = (held * gains).astype(BF16)
        weights = jnp.concatenate([wbc[:, spot] for spot in spots], axis=1)
        for i, spot in enumerate(spots):
            normed_ref[:, spot] = low[:, i * feats : (i + 1) * feats]
        square = held * held
        while square.shape[1] % 256 == 0:
            width = square.shape[1] // 2
            square = square[:, :width] + square[:, width:]
        tallies.append((square, nt_dot(low, weights)))


    for load in smalls:
        load.wait()
    take([rows_of(p, i) for i in range(n_ctx)], p)
    tap_rows = [flat(cxw_ref[k]) for k in range(taps)]
    bias_row = flat(cxb_ref[...])
    gate_row = flat(gg_ref[...])
    idle = jnp.zeros((1, total_heads - heads), F32)
    dtb_row = jnp.concatenate([dtb_ref[...], idle], axis=1)
    rate_row = jnp.concatenate([-jnp.exp(alog_ref[...]), idle], axis=1)
    skip_row = jnp.concatenate([skip_ref[...], idle], axis=1)

    holders = [lax.div(dec_ref[d * per + j], per) for j in range(per)]
    places = [lax.rem(dec_ref[d * per + j], per) for j in range(per)]
    for one, ref in ((xt_sem, xt_recv), (bt_sem, bt_recv)):
        if across:
            drain(ref.at[pl.ds(0, n_dp - 1)], one)
    plane_rows = lax.broadcasted_iota(jnp.int32, (per, 1), 0)
    for k in range(taps - 1):
        for j in range(per):
            r = k * per + j
            xfull[r : r + 1, :] = flat(xt_recv[holders[j], places[j], k].astype(F32))
            tail = bt_recv[holders[j], k].astype(F32)
            bcfull[r : r + 1, :] = jnp.sum(
                jnp.where(plane_rows == places[j], tail, 0.0), axis=0, keepdims=True
            )

    drain(seg_recv.at[pl.ds(0, plane - 1)], seg_sem)
    weights = []
    for j in range(per):
        after = jnp.zeros((1, tp_heads), F32)
        ordered = []
        row = pl.ds(places[j], 1)
        for m in reversed(range(half_ctx)):
            ordered.append(jnp.exp(-after))
            for k in (2 * m + 1, 2 * m):
                after = after + seg_recv[holders[j] * n_ctx + k, row, :]
        weights.extend(reversed(ordered))
    weights = pltpu.roll(full_lanes(jnp.concatenate(weights, axis=0)), 128 - c * heads, 1)

    for e in reversed(far):
        there = peer((0, 0, e))[2]

        @pl.when(there > p)
        def _():
            drain(rows_recv.at[there], line_sems.at[there])

        @pl.when(there < p)
        def _():
            drain(rows_recv.at[there, pl.ds(0, n_ctx)], line_sems.at[there])

        take([rows_of(there, i) for i in range(n_ctx)], there)
    square, narrow = tallies[0]
    for more, columns in tallies[1:]:
        square, narrow = square + more, narrow + columns
    scale = lax.rsqrt(jnp.sum(square, axis=1, keepdims=True) / model + epsilon)
    padded = jnp.concatenate([narrow, jnp.zeros((rows, 128 - n_cols), F32)], axis=1)
    col_send[...] = pltpu.roll(padded, lax.rem(n_cols * mine, 128), 1) * scale
    for o in group:
        send(col_send, col_recv.at[mine], done, col_sem, device(o))
    col_recv[mine] = col_send[...]
    for load in loads[1:]:
        load.wait()
    x_rows = nt_dot(normed_ref[...], wzx[half : 2 * half, :]) * scale
    z_gate = silu(nt_dot(normed_ref[...], wzx[0:half, :]) * scale)

    lead = (taps - 1) * per
    xfull[lead : lead + rows, :] = x_rows
    conv = bias_row
    for k in range(taps):
        conv = conv + tap_rows[k] * xfull[k * per : k * per + rows, :]
    xc = silu(conv)

    drain(state_recv.at[pl.ds(0, n_dp * half_ctx - 1)], state_sem)
    for j in range(per):
        for h in range(heads):
            spot = pl.ds(h * dim, dim)
            begin = None
            for m in range(half_ctx):
                r = j * half_ctx + m
                term = state_recv[holders[j] * half_ctx + m, spot, :].astype(F32)
                term = jnp.broadcast_to(weights[r : r + 1, h : h + 1], term.shape) * term
                begin = term if begin is None else begin + term
            start_state[j, spot, :] = begin
            start_low[j, spot, :] = begin.astype(BF16)

    drain(col_recv.at[pl.ds(0, ring - 1)], col_sem)
    lanes = lax.broadcasted_iota(jnp.int32, (rows, 128), 1)
    blocks_of = []
    for v in range(-(-all_cols // 128)):
        block = jnp.zeros((rows, 128), F32)
        for i in range(ring):
            low = n_cols * i - 128 * v
            if low < 128 and low + n_cols > 0:
                block = jnp.where((lanes >= low) & (lanes < low + n_cols), col_recv[i], block)
        blocks_of.append(block)
    columns = jnp.concatenate(blocks_of, axis=1)
    bcfull[lead : lead + rows, :] = columns[:, :width]
    head_first = (p * n_ctx + c) * heads
    dt_raw = pltpu.roll(columns[:, width:all_cols], total_heads - head_first, 1)
    step_size = softplus(dt_raw + dtb_row)
    row_of = lax.broadcasted_iota(jnp.int32, (rows, 1), 0)

    def later(value, k):
        return pltpu.roll(value, k * per, 0) if k else value

    total = step_size * rate_row
    k = 1
    while k < steps:
        total = total + jnp.where(row_of >= k * per, later(total, k), 0.0)
        k *= 2
    conv = cbb_ref[...]
    for k in range(taps):
        conv = conv + cbw_ref[k : k + 1, :] * bcfull[k * per : k * per + rows, :]
    bcc = silu(conv)
    b_all, c_all = bcc[:, :state_n], bcc[:, state_n:]

    row_slot = lax.rem(row_of, per)
    from_start = jnp.zeros((rows, chans), F32)
    c_low = c_all.astype(BF16)
    for j in range(per):
        from_start += jnp.where(row_slot == j, nt_dot(c_low, start_low[j]), 0.0)

    def by_head(value):
        if 128 % dim or chans % 128:
            return spread(value, 0)
        packed = 128 // dim
        out = []
        for m in range(chans // 128):
            part = jnp.broadcast_to(value[:, m * packed : m * packed + 1], (rows, 128))
            for q in range(1, packed):
                one = value[:, m * packed + q : m * packed + q + 1]
                part = jnp.where(lanes >= q * dim, one, part)
            out.append(part)
        return jnp.concatenate(out, axis=1)

    def at(value, t):
        return value[t * per : (t + 1) * per]

    y = by_head(jnp.exp(total)) * from_start
    for k in range(steps):
        overlap = jnp.sum(later(b_all, k) * c_all, axis=1, keepdims=True)
        if k:
            valid = row_of >= k * per
            decay = jnp.exp(jnp.where(valid, total - later(total, k), 0.0))
            share = jnp.where(valid, decay * overlap * later(step_size, k), 0.0)
        else:
            share = step_size * overlap + skip_row
        y = y + by_head(share) * later(xc, k)
    gated = y * z_gate
    diagonal = lax.broadcasted_iota(jnp.int32, (rows, 128), 0) == lax.broadcasted_iota(
        jnp.int32, (rows, 128), 1
    )
    scaled = (gated * gate_row).astype(BF16)
    base = lax.div(c, 2) * 2
    pieces = []
    for e in far + [0]:
        chips = [[(2 * m, q, e) for q in range(2)] for m in reversed(range(half_ctx))]
        pieces.extend(chips if e == far[0] else [sum(chips, [])])
    for number, piece in enumerate(pieces):
        there = peer((0, 0, piece[0][2]))[2]
        goals = [lax.rem(base + m + q, n_ctx) for m, q, _ in piece]
        cuts = [wout[:, pl.ds(pl.multiple_of((a * n_tp + there) * feats, feats), feats)] for a in goals]
        partial = jnp.dot(scaled, jnp.concatenate(cuts, axis=1), preferred_element_type=F32)
        for i, a in enumerate(goals):
            out_send[there * n_ctx + a] = partial[:, i * feats : (i + 1) * feats].astype(BF16)
        for a, (m, _, e) in zip(goals, piece):
            place = {"ctx": a, "dp": d, "tp": there}
            spot = there * n_ctx + a
            if m + e:
                send(out_send.at[spot], out_recv.at[mine], done, out_sem, place)
        if number == half_ctx - 1:
            squares = jnp.sum(gated * gated, axis=1, keepdims=True)
            sq_send[...] = jnp.sum(jnp.where(diagonal, squares, 0.0), axis=0, keepdims=True)
            for o in group:
                send(sq_send, sq_recv.at[mine], done, sq_sem, device(o))
            sq_recv[mine] = sq_send[...]
    send(out_send.at[p * n_ctx + mate["ctx"]], out_recv.at[mine], done, out_sem, mate)
    out_recv[mine] = out_send[p * n_ctx + c]

    last = jnp.concatenate([at(total, steps - 1)] * steps, axis=0)
    late = by_head(jnp.exp(last - total) * step_size) * xc
    flat_rows = jnp.concatenate([late, by_head(jnp.exp(last))], axis=0)
    tall = jnp.transpose(flat_rows)
    for j in range(per):
        b_own = jnp.where(row_slot == j, b_all, 0.0)
        final_ref[j] = (
            tall[:, rows + j : rows + j + 1] * start_state[j] + f32_dot(tall[:, :rows], b_own)
        )

    drain(rows_recv.at[p, pl.ds(0, plane - 1)], done)
    for k in range(1, n_tp):

        @pl.when(p >= k)
        def _():
            drain(rows_recv.at[p], done)

        @pl.when(p + k < n_tp)
        def _():
            drain(line_send, done)

    drain(seg_recv.at[pl.ds(0, plane - 1)], done)
    drain(seg_mate, done)
    drain(state_send, done)
    drain(pair_send.at[pl.ds(0, len(blocks) - 1)], done)
    if across:
        drain(xt_recv.at[pl.ds(0, n_dp - 1)], done)
        drain(bt_recv.at[pl.ds(0, n_dp - 1)], done)
    drain(col_recv.at[pl.ds(0, ring - 1)], done)
    drain(sq_recv.at[pl.ds(0, ring - 1)], done)
    drain(out_recv.at[pl.ds(0, ring - 1)], done)

    drain(sq_recv.at[pl.ds(0, ring - 1)], sq_sem)
    total_squares = sq_recv[0]
    for i in range(1, ring):
        total_squares = total_squares + sq_recv[i]
    total_squares = jnp.sum(jnp.where(diagonal, total_squares, 0.0), axis=1, keepdims=True)
    inverse = lax.rsqrt(total_squares / (total_heads * dim) + epsilon)
    drain(out_recv.at[pl.ds(0, ring - 1)], out_sem)
    mixed = out_recv[0].astype(F32)
    for i in range(1, ring):
        mixed = mixed + out_recv[i].astype(F32)
    mixed = mixed * inverse
    for t in range(steps):
        mixed_ref[t] = at(mixed, t).astype(BF16)


def tail_kernel(mixed_in, final_in, mixed_out, final_out, sems):
    copies = [
        pltpu.make_async_copy(final_in.at[j], final_out.at[j], sems.at[j])
        for j in range(final_in.shape[0])
    ]
    copies.append(pltpu.make_async_copy(mixed_in, mixed_out, sems.at[len(copies)]))
    for copy in copies:
        copy.start()
    for copy in copies:
        copy.wait()


def kernel_device(
    sizes,
    token_ids,
    decode_prompt,
    embedding,
    norm_gain,
    w_zx,
    w_bcdt,
    conv_x_weight,
    conv_x_bias,
    conv_bc_weight,
    conv_bc_bias,
    dt_bias,
    a_log,
    d_skip,
    gate_norm_gain,
    w_out,
    state_parts,
    seg_rate,
    x_tail,
    bc_tail,
):
    n_ctx, n_dp, n_tp, _ = sizes
    steps = token_ids.shape[0]
    slots = decode_prompt.shape[0]
    per = state_parts.shape[1]
    rows = steps * per
    vocab, feats = embedding.shape
    heads, dim, model = w_zx.shape[1:]
    chans = heads * dim
    tp_heads, state_n = state_parts.shape[2], state_parts.shape[4]
    ring, plane, blocks = n_ctx * n_tp, n_dp * n_ctx, n_dp * (n_ctx // 2)
    smem = pl.BlockSpec(memory_space=pltpu.SMEM)
    vmem = pl.BlockSpec(memory_space=pltpu.VMEM)
    anywhere = pl.BlockSpec(memory_space=pl.ANY)
    sem = pltpu.SemaphoreType.DMA
    rest = max(1, vocab % ROW_TILE)
    picked = pl.pallas_call(
        functools.partial(gather_kernel, steps, slots),
        out_shape=(
            pltpu.VMEM((steps * slots, ROW_TILE, feats), BF16),
            pltpu.VMEM((rest, feats), BF16),
            pltpu.VMEM((steps * slots, ROW_TILE, 128), F32),
            pltpu.VMEM((steps * slots, rest, 128), F32),
        ),
        in_specs=[smem, smem, anywhere],
        out_specs=(vmem,) * 4,
        scratch_shapes=[sem, sem],
        name="gather_rows",
    )(token_ids, decode_prompt, embedding)
    wide = 2 * state_n
    full_rows = -(-(conv_x_weight.shape[0] - 1 + steps) * per // 8) * 8
    smalls = (
        norm_gain[None],
        conv_x_weight,
        conv_x_bias,
        conv_bc_weight,
        conv_bc_bias[None],
        dt_bias[None],
        a_log[None],
        d_skip[None],
        gate_norm_gain,
    )
    bc_planes = jnp.swapaxes(bc_tail, 0, 1)
    mixed, final = pl.pallas_call(
        functools.partial(mixer_kernel, sizes, vocab),
        out_shape=(
            pltpu.VMEM((steps, per, feats), BF16),
            pltpu.VMEM((per, chans, state_n), F32),
        ),
        in_specs=[anywhere] + [vmem] * 4 + [anywhere] * 16,
        out_specs=(vmem, vmem),
        scratch_shapes=[
            pltpu.SMEM((slots,), jnp.int32),
            pltpu.VMEM((n_dp, rows, feats), BF16),
            *[pltpu.VMEM(small.shape, small.dtype) for small in smalls],
            pltpu.VMEM((blocks, chans, state_n), BF16),
            pltpu.VMEM((blocks, chans, state_n), BF16),
            pltpu.VMEM((2 * chans, model), BF16),
            pltpu.VMEM(w_bcdt.shape[::-1], BF16),
            pltpu.VMEM((chans, model), BF16),
            pltpu.VMEM((per, tp_heads * dim, state_n), BF16),
            pltpu.VMEM((blocks, chans, state_n), BF16),
            pltpu.VMEM((blocks, chans, state_n), BF16),
            pltpu.VMEM((n_tp, plane, rows, feats), BF16),
            pltpu.VMEM((n_ctx, rows, feats), BF16),
            pltpu.VMEM((plane, per, tp_heads), F32),
            pltpu.VMEM((per, tp_heads), F32),
            pltpu.VMEM((per, tp_heads), F32),
            pltpu.VMEM((n_dp,) + x_tail.shape, BF16),
            pltpu.VMEM((n_dp,) + bc_planes.shape, BF16),
            pltpu.VMEM((rows, 128), F32),
            pltpu.VMEM((ring, rows, 128), F32),
            pltpu.VMEM((1, 128), F32),
            pltpu.VMEM((ring, 1, 128), F32),
            pltpu.VMEM((ring, rows, feats), BF16),
            pltpu.VMEM((ring, rows, feats), BF16),
            pltpu.VMEM((per, chans, state_n), F32),
            pltpu.VMEM((per, chans, state_n), BF16),
            pltpu.VMEM((rows, model), BF16),
            pltpu.VMEM((full_rows, chans), F32),
            pltpu.VMEM((full_rows, wide), F32),
            sem,
            sem,
            sem,
            sem((2,)),
            sem((blocks,)),
            *[sem] * 3,
            sem((n_tp,)),
            *[sem] * 7,
            pltpu.SemaphoreType.REGULAR,
        ],
        compiler_params=pltpu.CompilerParams(
            collective_id=0, has_side_effects=True, vmem_limit_bytes=56 * 1024 * 1024
        ),
        name="mixer",
    )(
        decode_prompt,
        *[pltpu.with_memory_space_constraint(value, pltpu.VMEM) for value in picked],
        seg_rate,
        x_tail,
        bc_planes,
        *smalls,
        w_zx.reshape(2 * chans, model),
        w_bcdt.T,
        w_out.reshape(chans, model),
        state_parts.reshape(per, tp_heads * dim, state_n),
    )
    mixed, final = pl.pallas_call(
        tail_kernel,
        out_shape=(
            jax.ShapeDtypeStruct(mixed.shape, BF16),
            jax.ShapeDtypeStruct(final.shape, F32),
        ),
        in_specs=[anywhere] * 2,
        out_specs=(anywhere, anywhere),
        scratch_shapes=[sem((per + 1,))],
        name="tail",
    )(
        pltpu.with_memory_space_constraint(mixed, pltpu.VMEM),
        pltpu.with_memory_space_constraint(final, pltpu.VMEM),
    )
    return mixed, final.reshape(per, heads, dim, state_n)


def choose_device(sizes, *args):
    embedding, w_zx, w_bcdt = args[2], args[4], args[5]
    heads, dim = w_zx.shape[1:3]
    fits = (
        embedding.shape[1] % 128 == 0
        and sizes[0] % 2 == 0
        and (heads * dim) % 128 == 0
        and w_bcdt.shape[1] <= 128
        and embedding.shape[0] >= ROW_TILE
        and args[15].shape[2] <= 128
    )
    if fits:
        return kernel_device(sizes, *args)
    return per_device(*args)


def solution(mesh):
    sizes = (mesh.shape["ctx"], mesh.shape["dp"], mesh.shape["tp"], HEADS)
    return jax.shard_map(
        functools.partial(choose_device, sizes),
        mesh=mesh,
        in_specs=(
            P(),
            P(),
            P("dp", ("ctx", "tp")),
            P(),
            P(None, ("tp", "ctx"), None, None),
            P(None, ("ctx", "tp")),
            P(None, ("tp", "ctx"), None),
            P(("tp", "ctx"), None),
            P(),
            P(),
            P(("tp", "ctx")),
            P(("tp", "ctx")),
            P(("tp", "ctx")),
            P(("tp", "ctx"), None),
            P(("tp", "ctx"), None, None),
            P("ctx", "dp", "tp", None, None),
            P("ctx", "dp", "tp"),
            P("dp", None, ("tp", "ctx"), None),
            P("dp", None, None),
        ),
        out_specs=(P(None, "dp", ("ctx", "tp")), P("dp", ("tp", "ctx"), None, None)),
        check_vma=False,
    )
```

```python
import functools

import jax
import jax.numpy as jnp
from jax import lax
from jax.experimental import pallas as pl
from jax.experimental.pallas import tpu as pltpu
from jax.sharding import PartitionSpec as P

HEADS = 128
HEAD_DIM = 64


epsilon = 1e-05


def entering(shard, axis, combine, identity):
    count, here = (lax.axis_size(axis), lax.axis_index(axis))
    everything = lax.all_gather(shard, axis)
    start = jnp.broadcast_to(jnp.asarray(identity, shard.dtype), shard.shape)

    def step(k, before):
        at = count - 1 - k
        reached = at > here
        new = combine(before, everything[at])
        return jnp.where(reached, new, before)

    return lax.fori_loop(0, count, step, start)


def rms_scale(values, gain):
    return values * lax.rsqrt(jnp.mean(values * values, axis=-1, keepdims=True) + epsilon) * gain


def select_rows(picker, values):
    return jnp.tensordot(picker, values, axes=1, precision=lax.Precision.HIGHEST)


def add_rates(earlier, later_one):
    return earlier + later_one


def per_device(
    token_ids,
    decode_prompt,
    embedding,
    norm_gain,
    w_zx,
    w_bcdt,
    conv_x_weight,
    conv_x_bias,
    conv_bc_weight,
    conv_bc_bias,
    dt_bias,
    a_log,
    d_skip,
    gate_norm_gain,
    w_out,
    state_parts,
    seg_rate,
    x_tail,
    bc_tail,
):
    group = lax.axis_index("dp")
    local_count = state_parts.shape[1]
    slot_count = decode_prompt.shape[0]
    head_count = w_zx.shape[1]
    state_width = conv_bc_bias.shape[0] // 2
    after_rates = entering(seg_rate, "ctx", add_rates, jnp.zeros_like(seg_rate))
    seg_weight = jnp.exp(-after_rates[0])
    scaled = seg_weight[:, :, None, None] * state_parts[0].astype(jnp.float32)
    channel_sums = lax.psum_scatter(
        scaled.astype(jnp.bfloat16), "ctx", scatter_dimension=2, tiled=True
    ).astype(jnp.float32)
    combined = lax.all_to_all(
        channel_sums.astype(jnp.bfloat16), "ctx", split_axis=1, concat_axis=2, tiled=True
    ).astype(channel_sums.dtype)
    tails_x = x_tail.astype(jnp.float32)
    tails_bc = bc_tail.astype(jnp.float32)
    own_slots = lax.dynamic_slice_in_dim(decode_prompt, group * local_count, local_count)
    prompt_ids = jnp.arange(slot_count, dtype=jnp.int32)
    every_state, every_x, every_bc = (
        lax.all_gather(combined.astype(jnp.bfloat16), "dp", axis=0, tiled=True).astype(
            combined.dtype
        ),
        lax.all_gather(tails_x.astype(jnp.bfloat16), "dp", axis=0, tiled=True).astype(
            tails_x.dtype
        ),
        lax.all_gather(tails_bc.astype(jnp.bfloat16), "dp", axis=0, tiled=True).astype(
            tails_bc.dtype
        ),
    )
    picker = (own_slots[:, None] == prompt_ids[None, :]).astype(jnp.float32)
    ssm_state = select_rows(picker, every_state)
    x_window = select_rows(picker, every_x)
    bc_window = select_rows(picker, every_bc)
    vocab_rows = embedding.shape[0]
    holder = (decode_prompt[:, None] == prompt_ids[None, :]).astype(jnp.int32)
    slot_tokens = jnp.sum(token_ids[:, None, :] * holder[None], axis=2)
    offset_tokens = slot_tokens - group * vocab_rows
    inside = (offset_tokens >= 0) & (offset_tokens < vocab_rows)
    looked = jnp.take(embedding, jnp.clip(offset_tokens, 0, vocab_rows - 1), axis=0)
    partial_rows = jnp.where(inside[..., None], looked.astype(jnp.float32), 0.0)
    own_rows = lax.psum_scatter(
        partial_rows.astype(jnp.bfloat16), "dp", scatter_dimension=1, tiled=True
    )
    embedded = lax.all_gather(own_rows, ("ctx", "tp"), axis=2, tiled=True)
    steps_count = embedded.shape[0]
    flat_rows = embedded.reshape(-1, embedded.shape[2]).astype(jnp.float32)
    normed = rms_scale(flat_rows, norm_gain).astype(jnp.bfloat16)
    projected = jnp.einsum("rd,khed->krhe", normed, w_zx, preferred_element_type=jnp.float32)
    projected = projected.reshape(
        2, steps_count, local_count, projected.shape[2], projected.shape[3]
    )
    columns = lax.all_gather(
        jnp.dot(normed, w_bcdt, preferred_element_type=jnp.float32),
        ("ctx", "tp"),
        axis=1,
        tiled=True,
    )
    columns = columns.reshape(steps_count, local_count, -1)
    head_block = lax.axis_index("tp") * lax.axis_size("ctx") + lax.axis_index("ctx")
    head_start = 2 * state_width + head_block * head_count
    dt_raw = lax.dynamic_slice_in_dim(columns, head_start, head_count, 2)
    decay_rate = -jnp.exp(a_log)
    gated_steps = []
    for moment in range(steps_count):
        x_window = jnp.concatenate([x_window, projected[1, moment][:, None]], axis=1)
        bc_window = jnp.concatenate(
            [bc_window, columns[moment, :, None, : 2 * state_width]], axis=1
        )
        x_conv = jax.nn.silu(jnp.einsum("pkhe,khe->phe", x_window, conv_x_weight) + conv_x_bias)
        bc_conv = jax.nn.silu(jnp.einsum("pkn,kn->pn", bc_window, conv_bc_weight) + conv_bc_bias)
        step_size = jax.nn.softplus(dt_raw[moment] + dt_bias)
        retain = jnp.exp(step_size * decay_rate)
        ssm_state = (
            retain[:, :, None, None] * ssm_state
            + (step_size[:, :, None] * x_conv)[:, :, :, None] * bc_conv[:, None, None, :state_width]
        )
        output = (
            jnp.einsum("phen,pn->phe", ssm_state, bc_conv[:, state_width:])
            + d_skip[None, :, None] * x_conv
        )
        gated_steps.append(output * jax.nn.silu(projected[0, moment]))
        x_window = x_window[:, 1:]
        bc_window = bc_window[:, 1:]
    gated_all = jnp.stack(gated_steps)
    local_squares = jnp.sum(gated_all * gated_all, axis=(2, 3))
    total_squares = lax.psum(local_squares, ("ctx", "tp"))
    inverse = lax.rsqrt(total_squares / (HEADS * HEAD_DIM) + epsilon)
    normed_out = (gated_all * inverse[:, :, None, None] * gate_norm_gain).astype(jnp.bfloat16)
    partial_out = jnp.einsum("tphe,hed->tpd", normed_out, w_out, preferred_element_type=jnp.float32)
    outer_sum = lax.psum_scatter(
        partial_out.astype(jnp.bfloat16), "ctx", scatter_dimension=2, tiled=True
    ).astype(jnp.float32)
    mixed = lax.psum_scatter(outer_sum, "tp", scatter_dimension=2, tiled=True)
    return (mixed.astype(jnp.bfloat16), ssm_state)


HI = lax.Precision.HIGHEST
F32 = jnp.float32
BF16 = jnp.bfloat16


def f32_dot(a, b):
    return jnp.dot(a, b, precision=HI, preferred_element_type=F32)


def nt_dot(a, b):
    return lax.dot_general(a, b, (((1,), (1,)), ((), ())), preferred_element_type=F32)


def silu(v):
    return v / (1.0 + jnp.exp(-v))


def softplus(v):
    return jnp.maximum(v, 0.0) + jnp.log1p(jnp.exp(-jnp.abs(v)))


ROW_TILE = 8


def drain(ref, sem):
    pltpu.make_async_copy(ref, ref, sem).wait()


def row_place(tok_ref, vocab, s, t):
    whole = vocab // ROW_TILE * ROW_TILE
    row = tok_ref[t, s] - lax.axis_index("dp") * vocab
    held = (row >= 0) & (row < whole)
    start = pl.multiple_of(lax.bitwise_and(jnp.where(held, row, 0), -ROW_TILE), ROW_TILE)
    return row, held, start


def gather_kernel(
    steps, slots, tok_ref, emb_ref, buf, tail, mark, tail_mark, sem, tail_sem
):
    vocab = emb_ref.shape[0]
    whole = vocab // ROW_TILE * ROW_TILE
    where = []

    def block(i, start):
        return pltpu.make_async_copy(emb_ref.at[pl.ds(start, ROW_TILE)], buf.at[i], sem)

    def rest():
        return pltpu.make_async_copy(emb_ref.at[pl.ds(whole, vocab - whole)], tail, tail_sem)

    in_tail = False
    for s in range(slots):
        for t in range(steps):
            row, held, start = row_place(tok_ref, vocab, s, t)
            i = s * steps + t

            @pl.when(held)
            def _():
                block(i, start).start()

            where.append((row, start, held))
            in_tail |= (row >= whole) & (row < vocab)
    if whole < vocab:

        @pl.when(in_tail)
        def _():
            rest().start()

    tile_rows = lax.broadcasted_iota(jnp.int32, mark.shape[1:], 0)
    tail_rows = whole + lax.broadcasted_iota(jnp.int32, tail_mark.shape[1:], 0)
    for i, (row, start, held) in enumerate(where):
        mark[i] = (held & (tile_rows == row - start)).astype(F32)
        tail_mark[i] = (tail_rows == jnp.where(row < vocab, row, -1)).astype(F32)

    for i, (row, start, held) in enumerate(where):

        @pl.when(held)
        def _():
            block(i, start).wait()

    if whole < vocab:

        @pl.when(in_tail)
        def _():
            rest().wait()


def mixer_kernel(
    sizes,
    vocab,
    dec_hbm,
    raw_ref,
    rest_ref,
    mark_ref,
    rest_mark_ref,
    seg_hbm,
    xt_hbm,
    bt_hbm,
    gain_hbm,
    cxw_hbm,
    cxb_hbm,
    cbw_hbm,
    cbb_hbm,
    dtb_hbm,
    alog_hbm,
    skip_hbm,
    gg_hbm,
    wzx_hbm,
    wbc_hbm,
    wout_hbm,
    state_hbm,
    mixed_ref,
    final_ref,
    dec_ref,
    part_ref,
    gain_ref,
    cxw_ref,
    cxb_ref,
    cbw_ref,
    cbb_ref,
    dtb_ref,
    alog_ref,
    skip_ref,
    gg_ref,
    pair_recv,
    pair_send,
    wzx,
    wbc,
    wout,
    state_in,
    state_send,
    state_recv,
    rows_recv,
    line_send,
    seg_recv,
    seg_mate,
    seg_own,
    xt_recv,
    bt_recv,
    col_send,
    col_recv,
    sq_send,
    sq_recv,
    out_send,
    out_recv,
    start_state,
    start_low,
    normed_ref,
    xfull,
    bcfull,
    state_load,
    weight_sem,
    small_sem,
    own_sems,
    pair_sems,
    mate_sem,
    state_sem,
    plane_sem,
    line_sems,
    seg_sem,
    xt_sem,
    bt_sem,
    col_sem,
    sq_sem,
    out_sem,
    done,
    ready,
):
    n_ctx, n_dp, n_tp, total_heads = sizes
    c, d, p = lax.axis_index("ctx"), lax.axis_index("dp"), lax.axis_index("tp")
    mine = c * n_tp + p
    here_plane = d * n_ctx + c
    ring, plane = n_ctx * n_tp, n_dp * n_ctx
    steps, per, feats = mixed_ref.shape
    rows = steps * per
    heads, dim = cxb_ref.shape
    chans = heads * dim
    width = cbb_ref.shape[1]
    state_n = width // 2
    taps = cxw_ref.shape[0]
    model = gain_ref.shape[1]
    tp_heads = seg_recv.shape[-1]
    n_cols = wbc_hbm.shape[0]
    all_cols = n_cols * n_ctx * n_tp
    half = wzx_hbm.shape[0] // 2
    mirror = n_tp == 4

    def peer(offset):
        dc, dd, dt = offset
        away = lax.rem(p + dt, n_tp)
        if mirror and dt != n_tp // 2:
            away = n_tp - 1 - (p if dt == 1 else lax.rem(p + n_tp // 2, n_tp))
        return lax.rem(c + dc, n_ctx), lax.rem(d + dd, n_dp), away if dt else p

    def device(offset):
        a, b, e = peer(offset)
        return {"ctx": a, "dp": b, "tp": e}

    def along(k):
        return {"ctx": c, "dp": d, "tp": lax.rem(p + k + n_tp, n_tp)}

    def whole_plane(k):
        return [
            {"ctx": a, "dp": b, "tp": lax.rem(p + k + n_tp, n_tp)}
            for a, b, _ in [peer((a, b, 0)) for a in reversed(range(n_ctx)) for b in reversed(range(n_dp))]
        ]

    far = [1, 2, 3] if mirror else list(range(n_tp - 1, 0, -1))
    routed = [(a, b, 0) for a in reversed(range(n_ctx)) for b in reversed(range(n_dp)) if a + b]
    group = [(a, 0, e) for e in far + [0] for a in reversed(range(n_ctx)) if a + e]
    across = [(0, b, 0) for b in range(1, n_dp)]

    for e in range(n_tp):
        rows_recv[e, n_ctx:] = jnp.zeros((plane - n_ctx, rows, feats), BF16)
    barrier = pltpu.get_barrier_semaphore()
    for k in range(n_tp - 1, 0, -1):

        @pl.when(p + k < n_tp)
        def _():
            for place in whole_plane(k):
                pl.semaphore_signal(
                    barrier, inc=1, device_id=place, device_id_type=pl.DeviceIdType.MESH
                )


    for o in routed:
        pl.semaphore_signal(
            barrier, inc=1, device_id=device(o), device_id_type=pl.DeviceIdType.MESH
        )

    owns = []
    for source, target in (
        (dec_hbm, dec_ref),
        (seg_hbm.at[0], seg_own),
        (xt_hbm, xt_recv.at[d]),
        (bt_hbm, bt_recv.at[d]),
    ):
        load = pltpu.make_async_copy(source, target, own_sems.at[len(owns) // 2])
        load.start()
        owns.append(load)
    loads = []
    smalls = []
    pairs = (
        (state_hbm, state_in),
        (wbc_hbm, wbc),
        (wzx_hbm.at[pl.ds(half, half)], wzx.at[pl.ds(half, half)]),
        (wzx_hbm.at[pl.ds(0, half)], wzx.at[pl.ds(0, half)]),
        (wout_hbm, wout),
    )
    small_pairs = (
        (gain_hbm, gain_ref),
        (cxw_hbm, cxw_ref),
        (cxb_hbm, cxb_ref),
        (cbw_hbm, cbw_ref),
        (cbb_hbm, cbb_ref),
        (dtb_hbm, dtb_ref),
        (alog_hbm, alog_ref),
        (skip_hbm, skip_ref),
        (gg_hbm, gg_ref),
    )

    def fetch(source, target, sem, into):
        load = pltpu.make_async_copy(source, target, sem)
        load.start()
        into.append(load)

    fetch(*pairs[0], state_load, loads)
    for pair in small_pairs + pairs[1:2]:
        fetch(*pair, small_sem, smalls)
    def send(source, target, send_sem, recv_sem, place):
        pltpu.make_async_remote_copy(
            src_ref=source,
            dst_ref=target,
            send_sem=send_sem,
            recv_sem=recv_sem,
            device_id=place,
            device_id_type=pl.DeviceIdType.MESH,
        ).start()

    owns[0].wait()
    owns[1].wait()
    def chosen(mark, values):
        wide = jnp.concatenate([mark] * (feats // 128), axis=1)
        return jnp.sum(jnp.where(wide > 0.5, values.astype(F32), 0.0), axis=0, keepdims=True)

    for g in range(n_dp):
        picked = []
        for t in range(steps):
            for j in range(per):
                i = dec_ref[g * per + j] * steps + t
                value = chosen(mark_ref[i], raw_ref[i])
                if vocab % ROW_TILE:
                    value += chosen(rest_mark_ref[i], rest_ref[...])
                picked.append(value)
        part_ref[g] = jnp.concatenate(picked, axis=0).astype(BF16)

    pl.semaphore_wait(barrier, len(routed) + plane * p)
    for k in range(1, n_tp):

        @pl.when(p >= k)
        def _():
            pl.semaphore_signal(
                ready, inc=1, device_id=along(-k), device_id_type=pl.DeviceIdType.MESH
            )


    for o in routed:
        send(part_ref.at[peer(o)[1]], rows_recv.at[p, here_plane], done, plane_sem, device(o))
    rows_recv[p, here_plane] = part_ref[d]

    parity = lax.rem(c, 2)
    mate = {"ctx": c + 1 - 2 * parity, "dp": d, "tp": p}
    half_ctx = n_ctx // 2
    blocks = [(a, b) for a in reversed(range(half_ctx)) for b in reversed(range(n_dp))]
    seg_recv[here_plane] = seg_own[...]
    send(seg_own, seg_mate, done, mate_sem, mate)
    for o in routed:
        send(seg_own, seg_recv.at[here_plane], done, seg_sem, device(o))
    picks = []
    for b in range(n_dp):
        target_group = lax.rem(d + b, n_dp)
        pick = jnp.int32(0)
        for j in range(per):
            local = dec_ref[target_group * per + j] - d * per
            pick += jnp.where((local >= 0) & (local < per), local, 0)
        picks.append(pick)
    loads[0].wait()
    for slot, (a, b) in enumerate(blocks):
        first = pl.multiple_of(lax.rem(mate["ctx"] + 2 * a, n_ctx) * chans, chans)
        state_send[slot] = state_in[picks[b], pl.ds(first, chans), :]
        send(state_send.at[slot], pair_recv.at[slot], done, pair_sems.at[slot], mate)

    for k in range(n_tp - 1, 0, -1):

        @pl.when(p >= k)
        def _():
            for place in whole_plane(-k):
                send(part_ref.at[place["dp"]], rows_recv.at[p, here_plane], done, line_sems.at[p], place)

    owns[2].wait()
    owns[3].wait()
    for o in across:
        send(xt_recv.at[d], xt_recv.at[d], done, xt_sem, device(o))
        send(bt_recv.at[d], bt_recv.at[d], done, bt_sem, device(o))
    for pair in pairs[2:]:
        fetch(*pair, weight_sem, loads)

    fold = (
        lax.broadcasted_iota(jnp.int32, (dim, chans), 0)
        == lax.rem(lax.broadcasted_iota(jnp.int32, (dim, chans), 1), dim)
    ).astype(F32)
    head_rows = lax.broadcasted_iota(jnp.int32, (heads, chans), 0) == lax.div(
        lax.broadcasted_iota(jnp.int32, (heads, chans), 1), dim
    )

    def flat(value):
        return jnp.sum(jnp.where(head_rows, f32_dot(value, fold), 0.0), axis=0, keepdims=True)

    def full_lanes(value):
        idle = jnp.zeros((value.shape[0], 128 - value.shape[1]), F32)
        return jnp.concatenate([value, idle], axis=1) if idle.size else value

    def spread(value, first):
        count = value.shape[1]
        chosen = (
            lax.broadcasted_iota(jnp.int32, (count, chans), 0)
            == first + lax.div(lax.broadcasted_iota(jnp.int32, (count, chans), 1), dim)
        ).astype(F32)
        return f32_dot(value, chosen)

    drain(seg_mate, mate_sem)
    shrink = []
    for b in range(n_dp):
        row = pl.ds(picks[b], 1)
        shrink.append(jnp.exp(-jnp.where(parity == 0, seg_mate[row, :], seg_own[row, :])))
    shrink = full_lanes(jnp.concatenate(shrink, axis=0))
    for slot, (a, b) in enumerate(blocks):
        drain(pair_recv.at[slot], pair_sems.at[slot])
        first = pl.multiple_of(lax.rem(c + 2 * a, n_ctx) * chans, chans)
        turned = pltpu.roll(shrink, 128 - lax.rem(c + 2 * a, n_ctx) * heads, 1)
        sums = pair_send.at[slot] if a + b else state_recv.at[d * half_ctx + lax.div(c, 2)]
        for h in range(heads):
            spot = pl.ds(h * dim, dim)
            factor = turned[b : b + 1, h : h + 1]
            here = state_in[picks[b], pl.ds(pl.multiple_of(first + h * dim, dim), dim), :].astype(F32)
            there = pair_recv[slot, spot, :].astype(F32)
            left = jnp.broadcast_to(jnp.where(parity == 0, factor, 1.0), here.shape)
            right = jnp.broadcast_to(jnp.where(parity == 0, 1.0, factor), here.shape)
            sums[spot, :] = (left * here + right * there).astype(BF16)
        target = state_recv.at[d * half_ctx + lax.div(c, 2)]
        if a + b:
            send(pair_send.at[slot], target, done, state_sem, device((2 * a, b, 0)))

    drain(rows_recv.at[p, pl.ds(0, plane - 1)], plane_sem)
    def rows_of(e, i):
        piece = rows_recv[e, i].astype(F32)
        for g in range(1, n_dp):
            piece += rows_recv[e, g * n_ctx + i].astype(F32)
        return piece

    for i in range(n_ctx):
        line_send[i] = rows_of(p, i).astype(BF16)

    @pl.when(p < n_tp - 1)
    def _():
        pl.semaphore_wait(ready, n_tp - 1 - p)

    for k in range(n_tp - 1, 0, -1):

        @pl.when(p + k < n_tp)
        def _():
            send(line_send, rows_recv.at[p, pl.ds(0, n_ctx)], done, line_sems.at[p], along(k))

    tallies = []

    def take(values, e):
        spots = [pl.ds(pl.multiple_of((i * n_tp + e) * feats, feats), feats) for i in range(n_ctx)]
        held = jnp.concatenate(values, axis=1)
        gains = jnp.concatenate([gain_ref[:, spot] for spot in spots], axis=1)
        low = (held * gains).astype(BF16)
        weights = jnp.concatenate([wbc[:, spot] for spot in spots], axis=1)
        for i, spot in enumerate(spots):
            normed_ref[:, spot] = low[:, i * feats : (i + 1) * feats]
        square = held * held
        while square.shape[1] % 256 == 0:
            width = square.shape[1] // 2
            square = square[:, :width] + square[:, width:]
        tallies.append((square, nt_dot(low, weights)))


    for load in smalls:
        load.wait()
    take([rows_of(p, i) for i in range(n_ctx)], p)
    tap_rows = [flat(cxw_ref[k]) for k in range(taps)]
    bias_row = flat(cxb_ref[...])
    gate_row = flat(gg_ref[...])
    idle = jnp.zeros((1, total_heads - heads), F32)
    dtb_row = jnp.concatenate([dtb_ref[...], idle], axis=1)
    rate_row = jnp.concatenate([-jnp.exp(alog_ref[...]), idle], axis=1)
    skip_row = jnp.concatenate([skip_ref[...], idle], axis=1)

    holders = [lax.div(dec_ref[d * per + j], per) for j in range(per)]
    places = [lax.rem(dec_ref[d * per + j], per) for j in range(per)]
    for one, ref in ((xt_sem, xt_recv), (bt_sem, bt_recv)):
        if across:
            drain(ref.at[pl.ds(0, n_dp - 1)], one)
    plane_rows = lax.broadcasted_iota(jnp.int32, (per, 1), 0)
    for k in range(taps - 1):
        for j in range(per):
            r = k * per + j
            xfull[r : r + 1, :] = flat(xt_recv[holders[j], places[j], k].astype(F32))
            tail = bt_recv[holders[j], k].astype(F32)
            bcfull[r : r + 1, :] = jnp.sum(
                jnp.where(plane_rows == places[j], tail, 0.0), axis=0, keepdims=True
            )

    drain(seg_recv.at[pl.ds(0, plane - 1)], seg_sem)
    weights = []
    for j in range(per):
        after = jnp.zeros((1, tp_heads), F32)
        ordered = []
        row = pl.ds(places[j], 1)
        for m in reversed(range(half_ctx)):
            ordered.append(jnp.exp(-after))
            for k in (2 * m + 1, 2 * m):
                after = after + seg_recv[holders[j] * n_ctx + k, row, :]
        weights.extend(reversed(ordered))
    weights = pltpu.roll(full_lanes(jnp.concatenate(weights, axis=0)), 128 - c * heads, 1)

    for e in reversed(far):
        there = peer((0, 0, e))[2]

        @pl.when(there > p)
        def _():
            drain(rows_recv.at[there], line_sems.at[there])

        @pl.when(there < p)
        def _():
            drain(rows_recv.at[there, pl.ds(0, n_ctx)], line_sems.at[there])

        take([rows_of(there, i) for i in range(n_ctx)], there)
    square, narrow = tallies[0]
    for more, columns in tallies[1:]:
        square, narrow = square + more, narrow + columns
    scale = lax.rsqrt(jnp.sum(square, axis=1, keepdims=True) / model + epsilon)
    padded = jnp.concatenate([narrow, jnp.zeros((rows, 128 - n_cols), F32)], axis=1)
    col_send[...] = pltpu.roll(padded, lax.rem(n_cols * mine, 128), 1) * scale
    for o in group:
        send(col_send, col_recv.at[mine], done, col_sem, device(o))
    col_recv[mine] = col_send[...]
    for load in loads[1:]:
        load.wait()
    x_rows = nt_dot(normed_ref[...], wzx[half : 2 * half, :]) * scale
    z_gate = silu(nt_dot(normed_ref[...], wzx[0:half, :]) * scale)

    lead = (taps - 1) * per
    xfull[lead : lead + rows, :] = x_rows
    conv = bias_row
    for k in range(taps):
        conv = conv + tap_rows[k] * xfull[k * per : k * per + rows, :]
    xc = silu(conv)

    drain(state_recv.at[pl.ds(0, n_dp * half_ctx - 1)], state_sem)
    for j in range(per):
        for h in range(heads):
            spot = pl.ds(h * dim, dim)
            begin = None
            for m in range(half_ctx):
                r = j * half_ctx + m
                term = state_recv[holders[j] * half_ctx + m, spot, :].astype(F32)
                term = jnp.broadcast_to(weights[r : r + 1, h : h + 1], term.shape) * term
                begin = term if begin is None else begin + term
            start_low[j, spot, :] = begin.astype(BF16)

    drain(col_recv.at[pl.ds(0, ring - 1)], col_sem)
    lanes = lax.broadcasted_iota(jnp.int32, (rows, 128), 1)
    blocks_of = []
    for v in range(-(-all_cols // 128)):
        block = jnp.zeros((rows, 128), F32)
        for i in range(ring):
            low = n_cols * i - 128 * v
            if low < 128 and low + n_cols > 0:
                block = jnp.where((lanes >= low) & (lanes < low + n_cols), col_recv[i], block)
        blocks_of.append(block)
    columns = jnp.concatenate(blocks_of, axis=1)
    bcfull[lead : lead + rows, :] = columns[:, :width]
    head_first = (p * n_ctx + c) * heads
    dt_raw = pltpu.roll(columns[:, width:all_cols], total_heads - head_first, 1)
    step_size = softplus(dt_raw + dtb_row)
    row_of = lax.broadcasted_iota(jnp.int32, (rows, 1), 0)

    def later(value, k):
        return pltpu.roll(value, k * per, 0) if k else value

    total = step_size * rate_row
    k = 1
    while k < steps:
        total = total + jnp.where(row_of >= k * per, later(total, k), 0.0)
        k *= 2
    conv = cbb_ref[...]
    for k in range(taps):
        conv = conv + cbw_ref[k : k + 1, :] * bcfull[k * per : k * per + rows, :]
    bcc = silu(conv)
    b_all, c_all = bcc[:, :state_n], bcc[:, state_n:]

    row_slot = lax.rem(row_of, per)
    from_start = jnp.zeros((rows, chans), F32)
    c_low = c_all.astype(BF16)
    for j in range(per):
        from_start += jnp.where(row_slot == j, nt_dot(c_low, start_low[j]), 0.0)

    def by_head(value):
        if 128 % dim or chans % 128:
            return spread(value, 0)
        packed = 128 // dim
        out = []
        for m in range(chans // 128):
            part = jnp.broadcast_to(value[:, m * packed : m * packed + 1], (rows, 128))
            for q in range(1, packed):
                one = value[:, m * packed + q : m * packed + q + 1]
                part = jnp.where(lanes >= q * dim, one, part)
            out.append(part)
        return jnp.concatenate(out, axis=1)

    def at(value, t):
        return value[t * per : (t + 1) * per]

    y = by_head(jnp.exp(total)) * from_start
    for k in range(steps):
        overlap = jnp.sum(later(b_all, k) * c_all, axis=1, keepdims=True)
        if k:
            valid = row_of >= k * per
            decay = jnp.exp(jnp.where(valid, total - later(total, k), 0.0))
            share = jnp.where(valid, decay * overlap * later(step_size, k), 0.0)
        else:
            share = step_size * overlap + skip_row
        y = y + by_head(share) * later(xc, k)
    gated = y * z_gate
    diagonal = lax.broadcasted_iota(jnp.int32, (rows, 128), 0) == lax.broadcasted_iota(
        jnp.int32, (rows, 128), 1
    )
    scaled = (gated * gate_row).astype(BF16)
    base = lax.div(c, 2) * 2
    pieces = []
    for e in far + [0]:
        chips = [[(2 * m, q, e) for q in range(2)] for m in reversed(range(half_ctx))]
        pieces.extend(chips if e == far[0] else [sum(chips, [])])
    for number, piece in enumerate(pieces):
        there = peer((0, 0, piece[0][2]))[2]
        goals = [lax.rem(base + m + q, n_ctx) for m, q, _ in piece]
        cuts = [wout[:, pl.ds(pl.multiple_of((a * n_tp + there) * feats, feats), feats)] for a in goals]
        partial = jnp.dot(scaled, jnp.concatenate(cuts, axis=1), preferred_element_type=F32)
        for i, a in enumerate(goals):
            out_send[there * n_ctx + a] = partial[:, i * feats : (i + 1) * feats].astype(BF16)
        for a, (m, _, e) in zip(goals, piece):
            place = {"ctx": a, "dp": d, "tp": there}
            spot = there * n_ctx + a
            if m + e:
                send(out_send.at[spot], out_recv.at[mine], done, out_sem, place)
        if number == half_ctx - 1:
            squares = jnp.sum(gated * gated, axis=1, keepdims=True)
            sq_send[...] = jnp.sum(jnp.where(diagonal, squares, 0.0), axis=0, keepdims=True)
            for o in group:
                send(sq_send, sq_recv.at[mine], done, sq_sem, device(o))
            sq_recv[mine] = sq_send[...]
    send(out_send.at[p * n_ctx + mate["ctx"]], out_recv.at[mine], done, out_sem, mate)
    out_recv[mine] = out_send[p * n_ctx + c]

    for j in range(per):
        for h in range(heads):
            spot = pl.ds(h * dim, dim)
            begin = None
            for m in range(half_ctx):
                r = j * half_ctx + m
                term = state_recv[holders[j] * half_ctx + m, spot, :].astype(F32)
                term = jnp.broadcast_to(weights[r : r + 1, h : h + 1], term.shape) * term
                begin = term if begin is None else begin + term
            start_state[j, spot, :] = begin

    last = jnp.concatenate([at(total, steps - 1)] * steps, axis=0)
    late = by_head(jnp.exp(last - total) * step_size) * xc
    flat_rows = jnp.concatenate([late, by_head(jnp.exp(last))], axis=0)
    tall = jnp.transpose(flat_rows)
    for j in range(per):
        b_own = jnp.where(row_slot == j, b_all, 0.0)
        final_ref[j] = (
            tall[:, rows + j : rows + j + 1] * start_state[j] + f32_dot(tall[:, :rows], b_own)
        )

    drain(rows_recv.at[p, pl.ds(0, plane - 1)], done)
    for k in range(1, n_tp):

        @pl.when(p >= k)
        def _():
            drain(rows_recv.at[p], done)

        @pl.when(p + k < n_tp)
        def _():
            drain(line_send, done)

    drain(seg_recv.at[pl.ds(0, plane - 1)], done)
    drain(seg_mate, done)
    drain(state_send, done)
    drain(pair_send.at[pl.ds(0, len(blocks) - 1)], done)
    if across:
        drain(xt_recv.at[pl.ds(0, n_dp - 1)], done)
        drain(bt_recv.at[pl.ds(0, n_dp - 1)], done)
    drain(col_recv.at[pl.ds(0, ring - 1)], done)
    drain(sq_recv.at[pl.ds(0, ring - 1)], done)
    drain(out_recv.at[pl.ds(0, ring - 1)], done)

    drain(sq_recv.at[pl.ds(0, ring - 1)], sq_sem)
    total_squares = sq_recv[0]
    for i in range(1, ring):
        total_squares = total_squares + sq_recv[i]
    total_squares = jnp.sum(jnp.where(diagonal, total_squares, 0.0), axis=1, keepdims=True)
    inverse = lax.rsqrt(total_squares / (total_heads * dim) + epsilon)
    drain(out_recv.at[pl.ds(0, ring - 1)], out_sem)
    mixed = out_recv[0].astype(F32)
    for i in range(1, ring):
        mixed = mixed + out_recv[i].astype(F32)
    mixed = mixed * inverse
    for t in range(steps):
        mixed_ref[t] = at(mixed, t).astype(BF16)


def tail_kernel(mixed_in, final_in, mixed_out, final_out, sems):
    copies = [
        pltpu.make_async_copy(final_in.at[j], final_out.at[j], sems.at[j])
        for j in range(final_in.shape[0])
    ]
    copies.append(pltpu.make_async_copy(mixed_in, mixed_out, sems.at[len(copies)]))
    for copy in copies:
        copy.start()
    for copy in copies:
        copy.wait()


def kernel_device(
    sizes,
    token_ids,
    decode_prompt,
    embedding,
    norm_gain,
    w_zx,
    w_bcdt,
    conv_x_weight,
    conv_x_bias,
    conv_bc_weight,
    conv_bc_bias,
    dt_bias,
    a_log,
    d_skip,
    gate_norm_gain,
    w_out,
    state_parts,
    seg_rate,
    x_tail,
    bc_tail,
):
    n_ctx, n_dp, n_tp, _ = sizes
    steps = token_ids.shape[0]
    slots = decode_prompt.shape[0]
    per = state_parts.shape[1]
    rows = steps * per
    vocab, feats = embedding.shape
    heads, dim, model = w_zx.shape[1:]
    chans = heads * dim
    tp_heads, state_n = state_parts.shape[2], state_parts.shape[4]
    ring, plane, blocks = n_ctx * n_tp, n_dp * n_ctx, n_dp * (n_ctx // 2)
    smem = pl.BlockSpec(memory_space=pltpu.SMEM)
    vmem = pl.BlockSpec(memory_space=pltpu.VMEM)
    anywhere = pl.BlockSpec(memory_space=pl.ANY)
    sem = pltpu.SemaphoreType.DMA
    rest = max(1, vocab % ROW_TILE)
    picked = pl.pallas_call(
        functools.partial(gather_kernel, steps, slots),
        out_shape=(
            pltpu.VMEM((steps * slots, ROW_TILE, feats), BF16),
            pltpu.VMEM((rest, feats), BF16),
            pltpu.VMEM((steps * slots, ROW_TILE, 128), F32),
            pltpu.VMEM((steps * slots, rest, 128), F32),
        ),
        in_specs=[smem, anywhere],
        out_specs=(vmem,) * 4,
        scratch_shapes=[sem, sem],
        name="gather_rows",
    )(token_ids, embedding)
    wide = 2 * state_n
    full_rows = -(-(conv_x_weight.shape[0] - 1 + steps) * per // 8) * 8
    smalls = (
        norm_gain[None],
        conv_x_weight,
        conv_x_bias,
        conv_bc_weight,
        conv_bc_bias[None],
        dt_bias[None],
        a_log[None],
        d_skip[None],
        gate_norm_gain,
    )
    bc_planes = jnp.swapaxes(bc_tail, 0, 1)
    mixed, final = pl.pallas_call(
        functools.partial(mixer_kernel, sizes, vocab),
        out_shape=(
            pltpu.VMEM((steps, per, feats), BF16),
            pltpu.VMEM((per, chans, state_n), F32),
        ),
        in_specs=[anywhere] + [vmem] * 4 + [anywhere] * 16,
        out_specs=(vmem, vmem),
        scratch_shapes=[
            pltpu.SMEM((slots,), jnp.int32),
            pltpu.VMEM((n_dp, rows, feats), BF16),
            *[pltpu.VMEM(small.shape, small.dtype) for small in smalls],
            pltpu.VMEM((blocks, chans, state_n), BF16),
            pltpu.VMEM((blocks, chans, state_n), BF16),
            pltpu.VMEM((2 * chans, model), BF16),
            pltpu.VMEM(w_bcdt.shape[::-1], BF16),
            pltpu.VMEM((chans, model), BF16),
            pltpu.VMEM((per, tp_heads * dim, state_n), BF16),
            pltpu.VMEM((blocks, chans, state_n), BF16),
            pltpu.VMEM((blocks, chans, state_n), BF16),
            pltpu.VMEM((n_tp, plane, rows, feats), BF16),
            pltpu.VMEM((n_ctx, rows, feats), BF16),
            pltpu.VMEM((plane, per, tp_heads), F32),
            pltpu.VMEM((per, tp_heads), F32),
            pltpu.VMEM((per, tp_heads), F32),
            pltpu.VMEM((n_dp,) + x_tail.shape, BF16),
            pltpu.VMEM((n_dp,) + bc_planes.shape, BF16),
            pltpu.VMEM((rows, 128), F32),
            pltpu.VMEM((ring, rows, 128), F32),
            pltpu.VMEM((1, 128), F32),
            pltpu.VMEM((ring, 1, 128), F32),
            pltpu.VMEM((ring, rows, feats), BF16),
            pltpu.VMEM((ring, rows, feats), BF16),
            pltpu.VMEM((per, chans, state_n), F32),
            pltpu.VMEM((per, chans, state_n), BF16),
            pltpu.VMEM((rows, model), BF16),
            pltpu.VMEM((full_rows, chans), F32),
            pltpu.VMEM((full_rows, wide), F32),
            sem,
            sem,
            sem,
            sem((2,)),
            sem((blocks,)),
            *[sem] * 3,
            sem((n_tp,)),
            *[sem] * 7,
            pltpu.SemaphoreType.REGULAR,
        ],
        compiler_params=pltpu.CompilerParams(
            collective_id=0, has_side_effects=True, vmem_limit_bytes=56 * 1024 * 1024
        ),
        name="mixer",
    )(
        decode_prompt,
        *[pltpu.with_memory_space_constraint(value, pltpu.VMEM) for value in picked],
        seg_rate,
        x_tail,
        bc_planes,
        *smalls,
        w_zx.reshape(2 * chans, model),
        w_bcdt.T,
        w_out.reshape(chans, model),
        state_parts.reshape(per, tp_heads * dim, state_n),
    )
    mixed, final = pl.pallas_call(
        tail_kernel,
        out_shape=(
            jax.ShapeDtypeStruct(mixed.shape, BF16),
            jax.ShapeDtypeStruct(final.shape, F32),
        ),
        in_specs=[anywhere] * 2,
        out_specs=(anywhere, anywhere),
        scratch_shapes=[sem((per + 1,))],
        name="tail",
    )(
        pltpu.with_memory_space_constraint(mixed, pltpu.VMEM),
        pltpu.with_memory_space_constraint(final, pltpu.VMEM),
    )
    return mixed, final.reshape(per, heads, dim, state_n)


def choose_device(sizes, *args):
    embedding, w_zx, w_bcdt = args[2], args[4], args[5]
    heads, dim = w_zx.shape[1:3]
    fits = (
        embedding.shape[1] % 128 == 0
        and sizes[0] % 2 == 0
        and (heads * dim) % 128 == 0
        and w_bcdt.shape[1] <= 128
        and embedding.shape[0] >= ROW_TILE
        and args[15].shape[2] <= 128
    )
    if fits:
        return kernel_device(sizes, *args)
    return per_device(*args)


def solution(mesh):
    sizes = (mesh.shape["ctx"], mesh.shape["dp"], mesh.shape["tp"], HEADS)
    return jax.shard_map(
        functools.partial(choose_device, sizes),
        mesh=mesh,
        in_specs=(
            P(),
            P(),
            P("dp", ("ctx", "tp")),
            P(),
            P(None, ("tp", "ctx"), None, None),
            P(None, ("ctx", "tp")),
            P(None, ("tp", "ctx"), None),
            P(("tp", "ctx"), None),
            P(),
            P(),
            P(("tp", "ctx")),
            P(("tp", "ctx")),
            P(("tp", "ctx")),
            P(("tp", "ctx"), None),
            P(("tp", "ctx"), None, None),
            P("ctx", "dp", "tp", None, None),
            P("ctx", "dp", "tp"),
            P("dp", None, ("tp", "ctx"), None),
            P("dp", None, None),
        ),
        out_specs=(P(None, "dp", ("ctx", "tp")), P("dp", ("tp", "ctx"), None, None)),
        check_vma=False,
    )
```

```python
import functools

import jax
import jax.numpy as jnp
from jax import lax
from jax.experimental import pallas as pl
from jax.experimental.pallas import tpu as pltpu
from jax.sharding import PartitionSpec as P

HEADS = 128
HEAD_DIM = 64


epsilon = 1e-05


def entering(shard, axis, combine, identity):
    count, here = (lax.axis_size(axis), lax.axis_index(axis))
    everything = lax.all_gather(shard, axis)
    start = jnp.broadcast_to(jnp.asarray(identity, shard.dtype), shard.shape)

    def step(k, before):
        at = count - 1 - k
        reached = at > here
        new = combine(before, everything[at])
        return jnp.where(reached, new, before)

    return lax.fori_loop(0, count, step, start)


def rms_scale(values, gain):
    return values * lax.rsqrt(jnp.mean(values * values, axis=-1, keepdims=True) + epsilon) * gain


def select_rows(picker, values):
    return jnp.tensordot(picker, values, axes=1, precision=lax.Precision.HIGHEST)


def add_rates(earlier, later_one):
    return earlier + later_one


def per_device(
    token_ids,
    decode_prompt,
    embedding,
    norm_gain,
    w_zx,
    w_bcdt,
    conv_x_weight,
    conv_x_bias,
    conv_bc_weight,
    conv_bc_bias,
    dt_bias,
    a_log,
    d_skip,
    gate_norm_gain,
    w_out,
    state_parts,
    seg_rate,
    x_tail,
    bc_tail,
):
    group = lax.axis_index("dp")
    local_count = state_parts.shape[1]
    slot_count = decode_prompt.shape[0]
    head_count = w_zx.shape[1]
    state_width = conv_bc_bias.shape[0] // 2
    after_rates = entering(seg_rate, "ctx", add_rates, jnp.zeros_like(seg_rate))
    seg_weight = jnp.exp(-after_rates[0])
    scaled = seg_weight[:, :, None, None] * state_parts[0].astype(jnp.float32)
    channel_sums = lax.psum_scatter(
        scaled.astype(jnp.bfloat16), "ctx", scatter_dimension=2, tiled=True
    ).astype(jnp.float32)
    combined = lax.all_to_all(
        channel_sums.astype(jnp.bfloat16), "ctx", split_axis=1, concat_axis=2, tiled=True
    ).astype(channel_sums.dtype)
    tails_x = x_tail.astype(jnp.float32)
    tails_bc = bc_tail.astype(jnp.float32)
    own_slots = lax.dynamic_slice_in_dim(decode_prompt, group * local_count, local_count)
    prompt_ids = jnp.arange(slot_count, dtype=jnp.int32)
    every_state, every_x, every_bc = (
        lax.all_gather(combined.astype(jnp.bfloat16), "dp", axis=0, tiled=True).astype(
            combined.dtype
        ),
        lax.all_gather(tails_x.astype(jnp.bfloat16), "dp", axis=0, tiled=True).astype(
            tails_x.dtype
        ),
        lax.all_gather(tails_bc.astype(jnp.bfloat16), "dp", axis=0, tiled=True).astype(
            tails_bc.dtype
        ),
    )
    picker = (own_slots[:, None] == prompt_ids[None, :]).astype(jnp.float32)
    ssm_state = select_rows(picker, every_state)
    x_window = select_rows(picker, every_x)
    bc_window = select_rows(picker, every_bc)
    vocab_rows = embedding.shape[0]
    holder = (decode_prompt[:, None] == prompt_ids[None, :]).astype(jnp.int32)
    slot_tokens = jnp.sum(token_ids[:, None, :] * holder[None], axis=2)
    offset_tokens = slot_tokens - group * vocab_rows
    inside = (offset_tokens >= 0) & (offset_tokens < vocab_rows)
    looked = jnp.take(embedding, jnp.clip(offset_tokens, 0, vocab_rows - 1), axis=0)
    partial_rows = jnp.where(inside[..., None], looked.astype(jnp.float32), 0.0)
    own_rows = lax.psum_scatter(
        partial_rows.astype(jnp.bfloat16), "dp", scatter_dimension=1, tiled=True
    )
    embedded = lax.all_gather(own_rows, ("ctx", "tp"), axis=2, tiled=True)
    steps_count = embedded.shape[0]
    flat_rows = embedded.reshape(-1, embedded.shape[2]).astype(jnp.float32)
    normed = rms_scale(flat_rows, norm_gain).astype(jnp.bfloat16)
    projected = jnp.einsum("rd,khed->krhe", normed, w_zx, preferred_element_type=jnp.float32)
    projected = projected.reshape(
        2, steps_count, local_count, projected.shape[2], projected.shape[3]
    )
    columns = lax.all_gather(
        jnp.dot(normed, w_bcdt, preferred_element_type=jnp.float32),
        ("ctx", "tp"),
        axis=1,
        tiled=True,
    )
    columns = columns.reshape(steps_count, local_count, -1)
    head_block = lax.axis_index("tp") * lax.axis_size("ctx") + lax.axis_index("ctx")
    head_start = 2 * state_width + head_block * head_count
    dt_raw = lax.dynamic_slice_in_dim(columns, head_start, head_count, 2)
    decay_rate = -jnp.exp(a_log)
    gated_steps = []
    for moment in range(steps_count):
        x_window = jnp.concatenate([x_window, projected[1, moment][:, None]], axis=1)
        bc_window = jnp.concatenate(
            [bc_window, columns[moment, :, None, : 2 * state_width]], axis=1
        )
        x_conv = jax.nn.silu(jnp.einsum("pkhe,khe->phe", x_window, conv_x_weight) + conv_x_bias)
        bc_conv = jax.nn.silu(jnp.einsum("pkn,kn->pn", bc_window, conv_bc_weight) + conv_bc_bias)
        step_size = jax.nn.softplus(dt_raw[moment] + dt_bias)
        retain = jnp.exp(step_size * decay_rate)
        ssm_state = (
            retain[:, :, None, None] * ssm_state
            + (step_size[:, :, None] * x_conv)[:, :, :, None] * bc_conv[:, None, None, :state_width]
        )
        output = (
            jnp.einsum("phen,pn->phe", ssm_state, bc_conv[:, state_width:])
            + d_skip[None, :, None] * x_conv
        )
        gated_steps.append(output * jax.nn.silu(projected[0, moment]))
        x_window = x_window[:, 1:]
        bc_window = bc_window[:, 1:]
    gated_all = jnp.stack(gated_steps)
    local_squares = jnp.sum(gated_all * gated_all, axis=(2, 3))
    total_squares = lax.psum(local_squares, ("ctx", "tp"))
    inverse = lax.rsqrt(total_squares / (HEADS * HEAD_DIM) + epsilon)
    normed_out = (gated_all * inverse[:, :, None, None] * gate_norm_gain).astype(jnp.bfloat16)
    partial_out = jnp.einsum("tphe,hed->tpd", normed_out, w_out, preferred_element_type=jnp.float32)
    outer_sum = lax.psum_scatter(
        partial_out.astype(jnp.bfloat16), "ctx", scatter_dimension=2, tiled=True
    ).astype(jnp.float32)
    mixed = lax.psum_scatter(outer_sum, "tp", scatter_dimension=2, tiled=True)
    return (mixed.astype(jnp.bfloat16), ssm_state)


HI = lax.Precision.HIGHEST
F32 = jnp.float32
BF16 = jnp.bfloat16


def f32_dot(a, b):
    return jnp.dot(a, b, precision=HI, preferred_element_type=F32)


def nt_dot(a, b):
    return lax.dot_general(a, b, (((1,), (1,)), ((), ())), preferred_element_type=F32)


def silu(v):
    return v / (1.0 + jnp.exp(-v))


def softplus(v):
    return jnp.maximum(v, 0.0) + jnp.log1p(jnp.exp(-jnp.abs(v)))


ROW_TILE = 8


def drain(ref, sem):
    pltpu.make_async_copy(ref, ref, sem).wait()


def row_place(tok_ref, vocab, s, t):
    whole = vocab // ROW_TILE * ROW_TILE
    row = tok_ref[t, s] - lax.axis_index("dp") * vocab
    held = (row >= 0) & (row < whole)
    start = pl.multiple_of(lax.bitwise_and(jnp.where(held, row, 0), -ROW_TILE), ROW_TILE)
    return row, held, start


def gather_kernel(
    steps, slots, tok_ref, emb_ref, buf, tail, mark, tail_mark, sem, tail_sem
):
    vocab = emb_ref.shape[0]
    whole = vocab // ROW_TILE * ROW_TILE
    where = []

    def block(i, start):
        return pltpu.make_async_copy(emb_ref.at[pl.ds(start, ROW_TILE)], buf.at[i], sem)

    def rest():
        return pltpu.make_async_copy(emb_ref.at[pl.ds(whole, vocab - whole)], tail, tail_sem)

    in_tail = False
    for s in range(slots):
        for t in range(steps):
            row, held, start = row_place(tok_ref, vocab, s, t)
            i = s * steps + t

            @pl.when(held)
            def _():
                block(i, start).start()

            where.append((row, start, held))
            in_tail |= (row >= whole) & (row < vocab)
    if whole < vocab:

        @pl.when(in_tail)
        def _():
            rest().start()

    tile_rows = lax.broadcasted_iota(jnp.int32, mark.shape[1:], 0)
    tail_rows = whole + lax.broadcasted_iota(jnp.int32, tail_mark.shape[1:], 0)
    for i, (row, start, held) in enumerate(where):
        mark[i] = (held & (tile_rows == row - start)).astype(F32)
        tail_mark[i] = (tail_rows == jnp.where(row < vocab, row, -1)).astype(F32)

    for i, (row, start, held) in enumerate(where):

        @pl.when(held)
        def _():
            block(i, start).wait()

    if whole < vocab:

        @pl.when(in_tail)
        def _():
            rest().wait()


def mixer_kernel(
    sizes,
    vocab,
    dec_hbm,
    raw_ref,
    rest_ref,
    mark_ref,
    rest_mark_ref,
    seg_hbm,
    xt_hbm,
    bt_hbm,
    gain_hbm,
    cxw_hbm,
    cxb_hbm,
    cbw_hbm,
    cbb_hbm,
    dtb_hbm,
    alog_hbm,
    skip_hbm,
    gg_hbm,
    wzx_hbm,
    wbc_hbm,
    wout_hbm,
    state_hbm,
    mixed_ref,
    final_ref,
    dec_ref,
    part_ref,
    gain_ref,
    cxw_ref,
    cxb_ref,
    cbw_ref,
    cbb_ref,
    dtb_ref,
    alog_ref,
    skip_ref,
    gg_ref,
    pair_recv,
    pair_send,
    wzx,
    wbc,
    wout,
    state_in,
    state_send,
    state_recv,
    rows_recv,
    line_send,
    seg_recv,
    seg_mate,
    seg_own,
    xt_recv,
    bt_recv,
    col_send,
    col_recv,
    sq_send,
    sq_recv,
    out_send,
    out_recv,
    start_state,
    start_low,
    normed_ref,
    xfull,
    bcfull,
    state_load,
    weight_sem,
    small_sem,
    own_sems,
    pair_sems,
    mate_sem,
    state_sem,
    plane_sem,
    line_sems,
    seg_sem,
    xt_sem,
    bt_sem,
    col_sem,
    sq_sem,
    out_sem,
    done,
    ready,
):
    n_ctx, n_dp, n_tp, total_heads = sizes
    c, d, p = lax.axis_index("ctx"), lax.axis_index("dp"), lax.axis_index("tp")
    mine = c * n_tp + p
    here_plane = d * n_ctx + c
    ring, plane = n_ctx * n_tp, n_dp * n_ctx
    steps, per, feats = mixed_ref.shape
    rows = steps * per
    heads, dim = cxb_ref.shape
    chans = heads * dim
    width = cbb_ref.shape[1]
    state_n = width // 2
    taps = cxw_ref.shape[0]
    model = gain_ref.shape[1]
    tp_heads = seg_recv.shape[-1]
    n_cols = wbc_hbm.shape[0]
    all_cols = n_cols * n_ctx * n_tp
    half = wzx_hbm.shape[0] // 2
    mirror = n_tp == 4

    def peer(offset):
        dc, dd, dt = offset
        away = lax.rem(p + dt, n_tp)
        if mirror and dt != n_tp // 2:
            away = n_tp - 1 - (p if dt == 1 else lax.rem(p + n_tp // 2, n_tp))
        return lax.rem(c + dc, n_ctx), lax.rem(d + dd, n_dp), away if dt else p

    def device(offset):
        a, b, e = peer(offset)
        return {"ctx": a, "dp": b, "tp": e}

    def along(k):
        return {"ctx": c, "dp": d, "tp": lax.rem(p + k + n_tp, n_tp)}

    def whole_plane(k):
        return [
            {"ctx": a, "dp": b, "tp": lax.rem(p + k + n_tp, n_tp)}
            for a, b, _ in [peer((a, b, 0)) for a in reversed(range(n_ctx)) for b in reversed(range(n_dp))]
        ]

    far = [1, 2, 3] if mirror else list(range(n_tp - 1, 0, -1))
    routed = [(a, b, 0) for a in reversed(range(n_ctx)) for b in reversed(range(n_dp)) if a + b]
    group = [(a, 0, e) for e in far + [0] for a in reversed(range(n_ctx)) if a + e]
    across = [(0, b, 0) for b in range(1, n_dp)]

    barrier = pltpu.get_barrier_semaphore()
    for k in range(n_tp - 1, 0, -1):

        @pl.when(p + k < n_tp)
        def _():
            for place in whole_plane(k):
                pl.semaphore_signal(
                    barrier, inc=1, device_id=place, device_id_type=pl.DeviceIdType.MESH
                )


    for o in routed:
        pl.semaphore_signal(
            barrier, inc=1, device_id=device(o), device_id_type=pl.DeviceIdType.MESH
        )

    owns = []
    for source, target in (
        (dec_hbm, dec_ref),
        (seg_hbm.at[0], seg_own),
        (xt_hbm, xt_recv.at[d]),
        (bt_hbm, bt_recv.at[d]),
    ):
        load = pltpu.make_async_copy(source, target, own_sems.at[len(owns) // 2])
        load.start()
        owns.append(load)
    loads = []
    smalls = []
    pairs = (
        (state_hbm, state_in),
        (wbc_hbm, wbc),
        (wzx_hbm.at[pl.ds(half, half)], wzx.at[pl.ds(half, half)]),
        (wzx_hbm.at[pl.ds(0, half)], wzx.at[pl.ds(0, half)]),
        (wout_hbm, wout),
    )
    small_pairs = (
        (gain_hbm, gain_ref),
        (cxw_hbm, cxw_ref),
        (cxb_hbm, cxb_ref),
        (cbw_hbm, cbw_ref),
        (cbb_hbm, cbb_ref),
        (dtb_hbm, dtb_ref),
        (alog_hbm, alog_ref),
        (skip_hbm, skip_ref),
        (gg_hbm, gg_ref),
    )

    def fetch(source, target, sem, into):
        load = pltpu.make_async_copy(source, target, sem)
        load.start()
        into.append(load)

    fetch(*pairs[0], state_load, loads)
    for pair in small_pairs + pairs[1:2]:
        fetch(*pair, small_sem, smalls)
    def send(source, target, send_sem, recv_sem, place):
        pltpu.make_async_remote_copy(
            src_ref=source,
            dst_ref=target,
            send_sem=send_sem,
            recv_sem=recv_sem,
            device_id=place,
            device_id_type=pl.DeviceIdType.MESH,
        ).start()

    for e in range(n_tp - 1):

        @pl.when(e < p)
        def _():
            rows_recv[e, n_ctx:] = jnp.zeros((plane - n_ctx, rows, feats), BF16)

    owns[0].wait()
    owns[1].wait()
    def chosen(mark, values):
        wide = jnp.concatenate([mark] * (feats // 128), axis=1)
        return jnp.sum(jnp.where(wide > 0.5, values.astype(F32), 0.0), axis=0, keepdims=True)

    for g in range(n_dp):
        picked = []
        for t in range(steps):
            for j in range(per):
                i = dec_ref[g * per + j] * steps + t
                value = chosen(mark_ref[i], raw_ref[i])
                if vocab % ROW_TILE:
                    value += chosen(rest_mark_ref[i], rest_ref[...])
                picked.append(value)
        part_ref[g] = jnp.concatenate(picked, axis=0).astype(BF16)

    pl.semaphore_wait(barrier, len(routed) + plane * p)
    for k in range(1, n_tp):

        @pl.when(p >= k)
        def _():
            pl.semaphore_signal(
                ready, inc=1, device_id=along(-k), device_id_type=pl.DeviceIdType.MESH
            )


    for o in routed:
        send(part_ref.at[peer(o)[1]], rows_recv.at[p, here_plane], done, plane_sem, device(o))
    rows_recv[p, here_plane] = part_ref[d]

    parity = lax.rem(c, 2)
    mate = {"ctx": c + 1 - 2 * parity, "dp": d, "tp": p}
    half_ctx = n_ctx // 2
    blocks = [(a, b) for a in reversed(range(half_ctx)) for b in reversed(range(n_dp))]
    seg_recv[here_plane] = seg_own[...]
    send(seg_own, seg_mate, done, mate_sem, mate)
    for o in routed:
        send(seg_own, seg_recv.at[here_plane], done, seg_sem, device(o))
    picks = []
    for b in range(n_dp):
        target_group = lax.rem(d + b, n_dp)
        pick = jnp.int32(0)
        for j in range(per):
            local = dec_ref[target_group * per + j] - d * per
            pick += jnp.where((local >= 0) & (local < per), local, 0)
        picks.append(pick)
    loads[0].wait()
    for slot, (a, b) in enumerate(blocks):
        first = pl.multiple_of(lax.rem(mate["ctx"] + 2 * a, n_ctx) * chans, chans)
        state_send[slot] = state_in[picks[b], pl.ds(first, chans), :]
        send(state_send.at[slot], pair_recv.at[slot], done, pair_sems.at[slot], mate)

    for k in range(n_tp - 1, 0, -1):

        @pl.when(p >= k)
        def _():
            for place in whole_plane(-k):
                send(part_ref.at[place["dp"]], rows_recv.at[p, here_plane], done, line_sems.at[p], place)

    owns[2].wait()
    owns[3].wait()
    for o in across:
        send(xt_recv.at[d], xt_recv.at[d], done, xt_sem, device(o))
        send(bt_recv.at[d], bt_recv.at[d], done, bt_sem, device(o))
    for pair in pairs[2:]:
        fetch(*pair, weight_sem, loads)

    fold = (
        lax.broadcasted_iota(jnp.int32, (dim, chans), 0)
        == lax.rem(lax.broadcasted_iota(jnp.int32, (dim, chans), 1), dim)
    ).astype(F32)
    head_rows = lax.broadcasted_iota(jnp.int32, (heads, chans), 0) == lax.div(
        lax.broadcasted_iota(jnp.int32, (heads, chans), 1), dim
    )

    def flat(value):
        return jnp.sum(jnp.where(head_rows, f32_dot(value, fold), 0.0), axis=0, keepdims=True)

    def full_lanes(value):
        idle = jnp.zeros((value.shape[0], 128 - value.shape[1]), F32)
        return jnp.concatenate([value, idle], axis=1) if idle.size else value

    def spread(value, first):
        count = value.shape[1]
        chosen = (
            lax.broadcasted_iota(jnp.int32, (count, chans), 0)
            == first + lax.div(lax.broadcasted_iota(jnp.int32, (count, chans), 1), dim)
        ).astype(F32)
        return f32_dot(value, chosen)

    drain(seg_mate, mate_sem)
    shrink = []
    for b in range(n_dp):
        row = pl.ds(picks[b], 1)
        shrink.append(jnp.exp(-jnp.where(parity == 0, seg_mate[row, :], seg_own[row, :])))
    shrink = full_lanes(jnp.concatenate(shrink, axis=0))
    for slot, (a, b) in enumerate(blocks):
        drain(pair_recv.at[slot], pair_sems.at[slot])
        first = pl.multiple_of(lax.rem(c + 2 * a, n_ctx) * chans, chans)
        turned = pltpu.roll(shrink, 128 - lax.rem(c + 2 * a, n_ctx) * heads, 1)
        sums = pair_send.at[slot] if a + b else state_recv.at[d * half_ctx + lax.div(c, 2)]
        for h in range(heads):
            spot = pl.ds(h * dim, dim)
            factor = turned[b : b + 1, h : h + 1]
            here = state_in[picks[b], pl.ds(pl.multiple_of(first + h * dim, dim), dim), :].astype(F32)
            there = pair_recv[slot, spot, :].astype(F32)
            left = jnp.broadcast_to(jnp.where(parity == 0, factor, 1.0), here.shape)
            right = jnp.broadcast_to(jnp.where(parity == 0, 1.0, factor), here.shape)
            sums[spot, :] = (left * here + right * there).astype(BF16)
        target = state_recv.at[d * half_ctx + lax.div(c, 2)]
        if a + b:
            send(pair_send.at[slot], target, done, state_sem, device((2 * a, b, 0)))

    drain(rows_recv.at[p, pl.ds(0, plane - 1)], plane_sem)
    def rows_of(e, i):
        piece = rows_recv[e, i].astype(F32)
        for g in range(1, n_dp):
            piece += rows_recv[e, g * n_ctx + i].astype(F32)
        return piece

    for i in range(n_ctx):
        line_send[i] = rows_of(p, i).astype(BF16)

    @pl.when(p < n_tp - 1)
    def _():
        pl.semaphore_wait(ready, n_tp - 1 - p)

    for k in range(n_tp - 1, 0, -1):

        @pl.when(p + k < n_tp)
        def _():
            send(line_send, rows_recv.at[p, pl.ds(0, n_ctx)], done, line_sems.at[p], along(k))

    tallies = []

    def take(values, e):
        spots = [pl.ds(pl.multiple_of((i * n_tp + e) * feats, feats), feats) for i in range(n_ctx)]
        held = jnp.concatenate(values, axis=1)
        gains = jnp.concatenate([gain_ref[:, spot] for spot in spots], axis=1)
        low = (held * gains).astype(BF16)
        weights = jnp.concatenate([wbc[:, spot] for spot in spots], axis=1)
        for i, spot in enumerate(spots):
            normed_ref[:, spot] = low[:, i * feats : (i + 1) * feats]
        square = held * held
        while square.shape[1] % 256 == 0:
            width = square.shape[1] // 2
            square = square[:, :width] + square[:, width:]
        tallies.append((square, nt_dot(low, weights)))


    for load in smalls:
        load.wait()
    take([rows_of(p, i) for i in range(n_ctx)], p)
    tap_rows = [flat(cxw_ref[k]) for k in range(taps)]
    bias_row = flat(cxb_ref[...])
    gate_row = flat(gg_ref[...])
    idle = jnp.zeros((1, total_heads - heads), F32)
    dtb_row = jnp.concatenate([dtb_ref[...], idle], axis=1)
    rate_row = jnp.concatenate([-jnp.exp(alog_ref[...]), idle], axis=1)
    skip_row = jnp.concatenate([skip_ref[...], idle], axis=1)

    holders = [lax.div(dec_ref[d * per + j], per) for j in range(per)]
    places = [lax.rem(dec_ref[d * per + j], per) for j in range(per)]
    for one, ref in ((xt_sem, xt_recv), (bt_sem, bt_recv)):
        if across:
            drain(ref.at[pl.ds(0, n_dp - 1)], one)
    plane_rows = lax.broadcasted_iota(jnp.int32, (per, 1), 0)
    for k in range(taps - 1):
        for j in range(per):
            r = k * per + j
            xfull[r : r + 1, :] = flat(xt_recv[holders[j], places[j], k].astype(F32))
            tail = bt_recv[holders[j], k].astype(F32)
            bcfull[r : r + 1, :] = jnp.sum(
                jnp.where(plane_rows == places[j], tail, 0.0), axis=0, keepdims=True
            )

    drain(seg_recv.at[pl.ds(0, plane - 1)], seg_sem)
    weights = []
    for j in range(per):
        after = jnp.zeros((1, tp_heads), F32)
        ordered = []
        row = pl.ds(places[j], 1)
        for m in reversed(range(half_ctx)):
            ordered.append(jnp.exp(-after))
            for k in (2 * m + 1, 2 * m):
                after = after + seg_recv[holders[j] * n_ctx + k, row, :]
        weights.extend(reversed(ordered))
    weights = pltpu.roll(full_lanes(jnp.concatenate(weights, axis=0)), 128 - c * heads, 1)

    for e in reversed(far):
        there = peer((0, 0, e))[2]

        @pl.when(there > p)
        def _():
            drain(rows_recv.at[there], line_sems.at[there])

        @pl.when(there < p)
        def _():
            drain(rows_recv.at[there, pl.ds(0, n_ctx)], line_sems.at[there])

        take([rows_of(there, i) for i in range(n_ctx)], there)
    square, narrow = tallies[0]
    for more, columns in tallies[1:]:
        square, narrow = square + more, narrow + columns
    scale = lax.rsqrt(jnp.sum(square, axis=1, keepdims=True) / model + epsilon)
    padded = jnp.concatenate([narrow, jnp.zeros((rows, 128 - n_cols), F32)], axis=1)
    col_send[...] = pltpu.roll(padded, lax.rem(n_cols * mine, 128), 1) * scale
    for o in group:
        send(col_send, col_recv.at[mine], done, col_sem, device(o))
    col_recv[mine] = col_send[...]
    for load in loads[1:]:
        load.wait()
    x_rows = nt_dot(normed_ref[...], wzx[half : 2 * half, :]) * scale
    z_gate = silu(nt_dot(normed_ref[...], wzx[0:half, :]) * scale)

    lead = (taps - 1) * per
    xfull[lead : lead + rows, :] = x_rows
    conv = bias_row
    for k in range(taps):
        conv = conv + tap_rows[k] * xfull[k * per : k * per + rows, :]
    xc = silu(conv)

    drain(state_recv.at[pl.ds(0, n_dp * half_ctx - 1)], state_sem)
    for j in range(per):
        for h in range(heads):
            spot = pl.ds(h * dim, dim)
            begin = None
            for m in range(half_ctx):
                r = j * half_ctx + m
                term = state_recv[holders[j] * half_ctx + m, spot, :].astype(F32)
                term = jnp.broadcast_to(weights[r : r + 1, h : h + 1], term.shape) * term
                begin = term if begin is None else begin + term
            start_low[j, spot, :] = begin.astype(BF16)

    drain(col_recv.at[pl.ds(0, ring - 1)], col_sem)
    lanes = lax.broadcasted_iota(jnp.int32, (rows, 128), 1)
    blocks_of = []
    for v in range(-(-all_cols // 128)):
        block = jnp.zeros((rows, 128), F32)
        for i in range(ring):
            low = n_cols * i - 128 * v
            if low < 128 and low + n_cols > 0:
                block = jnp.where((lanes >= low) & (lanes < low + n_cols), col_recv[i], block)
        blocks_of.append(block)
    columns = jnp.concatenate(blocks_of, axis=1)
    bcfull[lead : lead + rows, :] = columns[:, :width]
    head_first = (p * n_ctx + c) * heads
    dt_raw = pltpu.roll(columns[:, width:all_cols], total_heads - head_first, 1)
    step_size = softplus(dt_raw + dtb_row)
    row_of = lax.broadcasted_iota(jnp.int32, (rows, 1), 0)

    def later(value, k):
        return pltpu.roll(value, k * per, 0) if k else value

    total = step_size * rate_row
    k = 1
    while k < steps:
        total = total + jnp.where(row_of >= k * per, later(total, k), 0.0)
        k *= 2
    conv = cbb_ref[...]
    for k in range(taps):
        conv = conv + cbw_ref[k : k + 1, :] * bcfull[k * per : k * per + rows, :]
    bcc = silu(conv)
    b_all, c_all = bcc[:, :state_n], bcc[:, state_n:]

    row_slot = lax.rem(row_of, per)
    from_start = jnp.zeros((rows, chans), F32)
    c_low = c_all.astype(BF16)
    for j in range(per):
        from_start += jnp.where(row_slot == j, nt_dot(c_low, start_low[j]), 0.0)

    def by_head(value):
        if 128 % dim or chans % 128:
            return spread(value, 0)
        packed = 128 // dim
        out = []
        for m in range(chans // 128):
            part = jnp.broadcast_to(value[:, m * packed : m * packed + 1], (rows, 128))
            for q in range(1, packed):
                one = value[:, m * packed + q : m * packed + q + 1]
                part = jnp.where(lanes >= q * dim, one, part)
            out.append(part)
        return jnp.concatenate(out, axis=1)

    def at(value, t):
        return value[t * per : (t + 1) * per]

    y = by_head(jnp.exp(total)) * from_start
    for k in range(steps):
        overlap = jnp.sum(later(b_all, k) * c_all, axis=1, keepdims=True)
        if k:
            valid = row_of >= k * per
            decay = jnp.exp(jnp.where(valid, total - later(total, k), 0.0))
            share = jnp.where(valid, decay * overlap * later(step_size, k), 0.0)
        else:
            share = step_size * overlap + skip_row
        y = y + by_head(share) * later(xc, k)
    gated = y * z_gate
    diagonal = lax.broadcasted_iota(jnp.int32, (rows, 128), 0) == lax.broadcasted_iota(
        jnp.int32, (rows, 128), 1
    )
    scaled = (gated * gate_row).astype(BF16)
    base = lax.div(c, 2) * 2
    pieces = []
    for e in far + [0]:
        chips = [[(2 * m, q, e) for q in range(2)] for m in reversed(range(half_ctx))]
        pieces.extend(chips if e == far[0] else [sum(chips, [])])
    for number, piece in enumerate(pieces):
        there = peer((0, 0, piece[0][2]))[2]
        goals = [lax.rem(base + m + q, n_ctx) for m, q, _ in piece]
        cuts = [wout[:, pl.ds(pl.multiple_of((a * n_tp + there) * feats, feats), feats)] for a in goals]
        partial = jnp.dot(scaled, jnp.concatenate(cuts, axis=1), preferred_element_type=F32)
        for i, a in enumerate(goals):
            out_send[there * n_ctx + a] = partial[:, i * feats : (i + 1) * feats].astype(BF16)
        for a, (m, _, e) in zip(goals, piece):
            place = {"ctx": a, "dp": d, "tp": there}
            spot = there * n_ctx + a
            if m + e:
                send(out_send.at[spot], out_recv.at[mine], done, out_sem, place)
        if number == half_ctx - 1:
            squares = jnp.sum(gated * gated, axis=1, keepdims=True)
            sq_send[...] = jnp.sum(jnp.where(diagonal, squares, 0.0), axis=0, keepdims=True)
            for o in group:
                send(sq_send, sq_recv.at[mine], done, sq_sem, device(o))
            sq_recv[mine] = sq_send[...]
    send(out_send.at[p * n_ctx + mate["ctx"]], out_recv.at[mine], done, out_sem, mate)
    out_recv[mine] = out_send[p * n_ctx + c]

    for j in range(per):
        for h in range(heads):
            spot = pl.ds(h * dim, dim)
            begin = None
            for m in range(half_ctx):
                r = j * half_ctx + m
                term = state_recv[holders[j] * half_ctx + m, spot, :].astype(F32)
                term = jnp.broadcast_to(weights[r : r + 1, h : h + 1], term.shape) * term
                begin = term if begin is None else begin + term
            start_state[j, spot, :] = begin

    last = jnp.concatenate([at(total, steps - 1)] * steps, axis=0)
    late = by_head(jnp.exp(last - total) * step_size) * xc
    flat_rows = jnp.concatenate([late, by_head(jnp.exp(last))], axis=0)
    tall = jnp.transpose(flat_rows)
    for j in range(per):
        b_own = jnp.where(row_slot == j, b_all, 0.0)
        final_ref[j] = (
            tall[:, rows + j : rows + j + 1] * start_state[j] + f32_dot(tall[:, :rows], b_own)
        )

    drain(rows_recv.at[p, pl.ds(0, plane - 1)], done)
    for k in range(1, n_tp):

        @pl.when(p >= k)
        def _():
            drain(rows_recv.at[p], done)

        @pl.when(p + k < n_tp)
        def _():
            drain(line_send, done)

    drain(seg_recv.at[pl.ds(0, plane - 1)], done)
    drain(seg_mate, done)
    drain(state_send, done)
    drain(pair_send.at[pl.ds(0, len(blocks) - 1)], done)
    if across:
        drain(xt_recv.at[pl.ds(0, n_dp - 1)], done)
        drain(bt_recv.at[pl.ds(0, n_dp - 1)], done)
    drain(col_recv.at[pl.ds(0, ring - 1)], done)
    drain(sq_recv.at[pl.ds(0, ring - 1)], done)
    drain(out_recv.at[pl.ds(0, ring - 1)], done)

    drain(sq_recv.at[pl.ds(0, ring - 1)], sq_sem)
    total_squares = sq_recv[0]
    for i in range(1, ring):
        total_squares = total_squares + sq_recv[i]
    total_squares = jnp.sum(jnp.where(diagonal, total_squares, 0.0), axis=1, keepdims=True)
    inverse = lax.rsqrt(total_squares / (total_heads * dim) + epsilon)
    drain(out_recv.at[pl.ds(0, ring - 1)], out_sem)
    mixed = out_recv[0].astype(F32)
    for i in range(1, ring):
        mixed = mixed + out_recv[i].astype(F32)
    mixed = mixed * inverse
    for t in range(steps):
        mixed_ref[t] = at(mixed, t).astype(BF16)


def tail_kernel(mixed_in, final_in, mixed_out, final_out, sems):
    copies = [
        pltpu.make_async_copy(final_in.at[j], final_out.at[j], sems.at[j])
        for j in range(final_in.shape[0])
    ]
    copies.append(pltpu.make_async_copy(mixed_in, mixed_out, sems.at[len(copies)]))
    for copy in copies:
        copy.start()
    for copy in copies:
        copy.wait()


def kernel_device(
    sizes,
    token_ids,
    decode_prompt,
    embedding,
    norm_gain,
    w_zx,
    w_bcdt,
    conv_x_weight,
    conv_x_bias,
    conv_bc_weight,
    conv_bc_bias,
    dt_bias,
    a_log,
    d_skip,
    gate_norm_gain,
    w_out,
    state_parts,
    seg_rate,
    x_tail,
    bc_tail,
):
    n_ctx, n_dp, n_tp, _ = sizes
    steps = token_ids.shape[0]
    slots = decode_prompt.shape[0]
    per = state_parts.shape[1]
    rows = steps * per
    vocab, feats = embedding.shape
    heads, dim, model = w_zx.shape[1:]
    chans = heads * dim
    tp_heads, state_n = state_parts.shape[2], state_parts.shape[4]
    ring, plane, blocks = n_ctx * n_tp, n_dp * n_ctx, n_dp * (n_ctx // 2)
    smem = pl.BlockSpec(memory_space=pltpu.SMEM)
    vmem = pl.BlockSpec(memory_space=pltpu.VMEM)
    anywhere = pl.BlockSpec(memory_space=pl.ANY)
    sem = pltpu.SemaphoreType.DMA
    rest = max(1, vocab % ROW_TILE)
    picked = pl.pallas_call(
        functools.partial(gather_kernel, steps, slots),
        out_shape=(
            pltpu.VMEM((steps * slots, ROW_TILE, feats), BF16),
            pltpu.VMEM((rest, feats), BF16),
            pltpu.VMEM((steps * slots, ROW_TILE, 128), F32),
            pltpu.VMEM((steps * slots, rest, 128), F32),
        ),
        in_specs=[smem, anywhere],
        out_specs=(vmem,) * 4,
        scratch_shapes=[sem, sem],
        name="gather_rows",
    )(token_ids, embedding)
    wide = 2 * state_n
    full_rows = -(-(conv_x_weight.shape[0] - 1 + steps) * per // 8) * 8
    smalls = (
        norm_gain[None],
        conv_x_weight,
        conv_x_bias,
        conv_bc_weight,
        conv_bc_bias[None],
        dt_bias[None],
        a_log[None],
        d_skip[None],
        gate_norm_gain,
    )
    bc_planes = jnp.swapaxes(bc_tail, 0, 1)
    mixed, final = pl.pallas_call(
        functools.partial(mixer_kernel, sizes, vocab),
        out_shape=(
            pltpu.VMEM((steps, per, feats), BF16),
            pltpu.VMEM((per, chans, state_n), F32),
        ),
        in_specs=[anywhere] + [vmem] * 4 + [anywhere] * 16,
        out_specs=(vmem, vmem),
        scratch_shapes=[
            pltpu.SMEM((slots,), jnp.int32),
            pltpu.VMEM((n_dp, rows, feats), BF16),
            *[pltpu.VMEM(small.shape, small.dtype) for small in smalls],
            pltpu.VMEM((blocks, chans, state_n), BF16),
            pltpu.VMEM((blocks, chans, state_n), BF16),
            pltpu.VMEM((2 * chans, model), BF16),
            pltpu.VMEM(w_bcdt.shape[::-1], BF16),
            pltpu.VMEM((chans, model), BF16),
            pltpu.VMEM((per, tp_heads * dim, state_n), BF16),
            pltpu.VMEM((blocks, chans, state_n), BF16),
            pltpu.VMEM((blocks, chans, state_n), BF16),
            pltpu.VMEM((n_tp, plane, rows, feats), BF16),
            pltpu.VMEM((n_ctx, rows, feats), BF16),
            pltpu.VMEM((plane, per, tp_heads), F32),
            pltpu.VMEM((per, tp_heads), F32),
            pltpu.VMEM((per, tp_heads), F32),
            pltpu.VMEM((n_dp,) + x_tail.shape, BF16),
            pltpu.VMEM((n_dp,) + bc_planes.shape, BF16),
            pltpu.VMEM((rows, 128), F32),
            pltpu.VMEM((ring, rows, 128), F32),
            pltpu.VMEM((1, 128), F32),
            pltpu.VMEM((ring, 1, 128), F32),
            pltpu.VMEM((ring, rows, feats), BF16),
            pltpu.VMEM((ring, rows, feats), BF16),
            pltpu.VMEM((per, chans, state_n), F32),
            pltpu.VMEM((per, chans, state_n), BF16),
            pltpu.VMEM((rows, model), BF16),
            pltpu.VMEM((full_rows, chans), F32),
            pltpu.VMEM((full_rows, wide), F32),
            sem,
            sem,
            sem,
            sem((2,)),
            sem((blocks,)),
            *[sem] * 3,
            sem((n_tp,)),
            *[sem] * 7,
            pltpu.SemaphoreType.REGULAR,
        ],
        compiler_params=pltpu.CompilerParams(
            collective_id=0, has_side_effects=True, vmem_limit_bytes=56 * 1024 * 1024
        ),
        name="mixer",
    )(
        decode_prompt,
        *[pltpu.with_memory_space_constraint(value, pltpu.VMEM) for value in picked],
        seg_rate,
        x_tail,
        bc_planes,
        *smalls,
        w_zx.reshape(2 * chans, model),
        w_bcdt.T,
        w_out.reshape(chans, model),
        state_parts.reshape(per, tp_heads * dim, state_n),
    )
    mixed, final = pl.pallas_call(
        tail_kernel,
        out_shape=(
            jax.ShapeDtypeStruct(mixed.shape, BF16),
            jax.ShapeDtypeStruct(final.shape, F32),
        ),
        in_specs=[anywhere] * 2,
        out_specs=(anywhere, anywhere),
        scratch_shapes=[sem((per + 1,))],
        name="tail",
    )(
        pltpu.with_memory_space_constraint(mixed, pltpu.VMEM),
        pltpu.with_memory_space_constraint(final, pltpu.VMEM),
    )
    return mixed, final.reshape(per, heads, dim, state_n)


def choose_device(sizes, *args):
    embedding, w_zx, w_bcdt = args[2], args[4], args[5]
    heads, dim = w_zx.shape[1:3]
    fits = (
        embedding.shape[1] % 128 == 0
        and sizes[0] % 2 == 0
        and (heads * dim) % 128 == 0
        and w_bcdt.shape[1] <= 128
        and embedding.shape[0] >= ROW_TILE
        and args[15].shape[2] <= 128
    )
    if fits:
        return kernel_device(sizes, *args)
    return per_device(*args)


def solution(mesh):
    sizes = (mesh.shape["ctx"], mesh.shape["dp"], mesh.shape["tp"], HEADS)
    return jax.shard_map(
        functools.partial(choose_device, sizes),
        mesh=mesh,
        in_specs=(
            P(),
            P(),
            P("dp", ("ctx", "tp")),
            P(),
            P(None, ("tp", "ctx"), None, None),
            P(None, ("ctx", "tp")),
            P(None, ("tp", "ctx"), None),
            P(("tp", "ctx"), None),
            P(),
            P(),
            P(("tp", "ctx")),
            P(("tp", "ctx")),
            P(("tp", "ctx")),
            P(("tp", "ctx"), None),
            P(("tp", "ctx"), None, None),
            P("ctx", "dp", "tp", None, None),
            P("ctx", "dp", "tp"),
            P("dp", None, ("tp", "ctx"), None),
            P("dp", None, None),
        ),
        out_specs=(P(None, "dp", ("ctx", "tp")), P("dp", ("tp", "ctx"), None, None)),
        check_vma=False,
    )
```
